512 devices in a mesh: gx: 16 (over y_lo, x, core), gy: 32 (over y_hi, z).
Axes of the slice: x: 4, y: 4 (y_hi: 2, y_lo: 2; y = y_hi * 2 + y_lo), z: 16, core: 2. Of those that a mesh axis runs over, the one named last changes fastest.
Arguments:
- phase_field: float32 [16, 2048, 2048], P(None, 'gy', 'gx'), may hold values from -1 to 1
- mobility: float32 [16, 2048, 2048], P(None, 'gy', 'gx'), may hold values from 0.25 to 2.5
- x_inverse: bfloat16 [2048, 2048], P('gx'), may hold values from -2 to 2
- y_inverse: bfloat16 [2048, 2048], P('gy'), may hold values from -2 to 2
Outputs:
- new_phase: float32 [16, 2048, 2048], P(None, 'gy', 'gx')
The draws below stay inside these ranges and needn't reach their ends.
All inputs are finite; a program needn't handle non-finite values.
Results may differ from the reference program's by a relative error of at most 0.0041.
Values may be sent and summed in bfloat16 or wider, within the bound.
No kernel may reach another device: no remote copies, remote signals or barrier semaphores. Data moves between devices by JAX's collectives and lax.ppermute only.
A program may use at most 64 MiB of HBM per device.

```python
import math
import jax
import jax.numpy as jnp
from jax import lax

NX = 2048
NY = 2048
PZ = 16
CX = 128
CY = 64


def line_inverse(key, order, reach):
    index = jnp.arange(order)
    distance = jnp.abs(index[:, None] - index[None, :]).astype(jnp.float32)
    envelope = jnp.exp(-distance / reach)
    noise = jnp.clip(jax.random.normal(jax.random.fold_in(key, 11), (order, order), jnp.float32), -4.0, 4.0)
    far_noise = jnp.clip(jax.random.normal(jax.random.fold_in(key, 13), (order, order), jnp.float32), -4.0, 4.0)
    diagonal = jax.random.uniform(jax.random.fold_in(key, 12), (order,), jnp.float32, 0.4, 0.8)
    matrix = jnp.diag(diagonal) + 0.5 * noise * envelope / jnp.sqrt(2.0 * reach)
    matrix = matrix + 0.6 * far_noise / jnp.sqrt(1.0 * order)
    return matrix.astype(jnp.bfloat16)


def draw_x_inverse(key, part):
    return line_inverse(jax.random.fold_in(key, 1), NX, 2.0 * CX)


def draw_y_inverse(key, part):
    return line_inverse(jax.random.fold_in(key, 2), NY, 2.0 * CY)


def block_levels(rng, extent, cuts, least, high):
    def one(position, blocks):
        steps = jax.random.uniform(jax.random.fold_in(jax.random.fold_in(rng, 6), position), (blocks,), jnp.float32, least / len(cuts), high / len(cuts))
        return jnp.repeat(jnp.exp(steps), extent[position] // blocks).reshape((-1,) + (1,) * (len(extent) - position - 1))

    factor_of = one(*cuts[0])
    for cut in cuts[1:]:
        factor_of = factor_of * one(*cut)
    return factor_of


def setup_inputs(seed: int = 0) -> dict:
    seeds = jax.random.split(jax.random.key(seed), 5)
    phase_field = jnp.clip(jax.random.uniform(seeds[0], (PZ, NY, NX), jnp.float32, -1.0, 1.0) * block_levels(seeds[0], (PZ, NY, NX), ((1, 32), (2, 16)), -0.4, 0.0), -1.0, 1.0)
    mobility = jnp.clip(jnp.exp(math.log(2.5) - 2.3025851 * jax.random.uniform(seeds[1], (PZ, NY, NX), jnp.float32) ** block_levels(seeds[1], (PZ, NY, NX), ((1, 32), (2, 16)), -0.2, 0.2)), 0.25, 2.5)
    x_inverse = draw_x_inverse(jax.random.fold_in(seeds[4], 71), 0)
    y_inverse = draw_y_inverse(jax.random.fold_in(seeds[4], 71), 0)
    return {"phase_field": phase_field, "mobility": mobility, "x_inverse": x_inverse, "y_inverse": y_inverse}


step_size = 0.15


def face_mob(center_mob, near_mob):
    return 2.0 * center_mob * near_mob / jnp.maximum(center_mob + near_mob, 0.25)


def laplace(values, mobile):
    values_z = jnp.pad(values, ((1, 1), (0, 0), (0, 0)))
    mobile_z = jnp.pad(mobile, ((1, 1), (0, 0), (0, 0)))
    center = values[:, 1:-1, 1:-1]
    center_mob = mobile[:, 1:-1, 1:-1]
    pairs = [
        (values_z[2:, 1:-1, 1:-1], mobile_z[2:, 1:-1, 1:-1]),
        (values_z[:-2, 1:-1, 1:-1], mobile_z[:-2, 1:-1, 1:-1]),
        (values[:, 2:, 1:-1], mobile[:, 2:, 1:-1]),
        (values[:, :-2, 1:-1], mobile[:, :-2, 1:-1]),
        (values[:, 1:-1, 2:], mobile[:, 1:-1, 2:]),
        (values[:, 1:-1, :-2], mobile[:, 1:-1, :-2]),
    ]
    result = jnp.zeros_like(center)
    for near_val, near_mob in pairs:
        result = result + face_mob(center_mob, near_mob) * (near_val - center)
    return result


def pad_yx(array):
    return jnp.pad(array, ((0, 0), (1, 1), (1, 1)))


def reference(phase_field, mobility, x_inverse, y_inverse):
    mob_pad = pad_yx(mobility)
    first = phase_field + step_size * laplace(pad_yx(phase_field), mob_pad)
    second = (first + step_size * laplace(pad_yx(first), mob_pad)).astype(jnp.bfloat16)

    def solve_x(plane):
        return jnp.dot(plane, x_inverse.T, preferred_element_type=jnp.float32)

    solved = lax.map(solve_x, second)
    chemical = solved * solved * solved - solved
    updated = (solved + step_size * laplace(pad_yx(chemical), mob_pad)).astype(jnp.bfloat16)

    def solve_y(plane):
        return jnp.dot(y_inverse, plane, preferred_element_type=jnp.float32)

    return lax.map(solve_y, updated)
```

```python
import jax
import jax.numpy as jnp
from jax import lax
from jax.sharding import Mesh
from jax.sharding import PartitionSpec as P

GX = ("yl", "x", "c")
GY = ("yh", "z")

step_size = 0.15


def extended(x, sides):
    for axis, dim, width in sides:
        size, length = (lax.axis_size(axis), x.shape[dim])
        up = [(i, (i + 1) % size) for i in range(size - 1)]
        down = [(j, i) for i, j in up]
        last = lax.slice_in_dim(x, length - width, length, axis=dim)
        leading = lax.slice_in_dim(x, 0, width, axis=dim)
        before = lax.ppermute(last, axis, up)
        after = lax.ppermute(leading, axis, down)
        x = jnp.concatenate([before, x, after], axis=dim)
    return x


def face_mob(center_mob, near_mob):
    return 2.0 * center_mob * near_mob / jnp.maximum(center_mob + near_mob, 0.25)


def laplace(values, mobile):
    values_z = jnp.pad(values, ((1, 1), (0, 0), (0, 0)))
    mobile_z = jnp.pad(mobile, ((1, 1), (0, 0), (0, 0)))
    center = values[:, 1:-1, 1:-1]
    center_mob = mobile[:, 1:-1, 1:-1]
    pairs = [
        (values_z[2:, 1:-1, 1:-1], mobile_z[2:, 1:-1, 1:-1]),
        (values_z[:-2, 1:-1, 1:-1], mobile_z[:-2, 1:-1, 1:-1]),
        (values[:, 2:, 1:-1], mobile[:, 2:, 1:-1]),
        (values[:, :-2, 1:-1], mobile[:, :-2, 1:-1]),
        (values[:, 1:-1, 2:], mobile[:, 1:-1, 2:]),
        (values[:, 1:-1, :-2], mobile[:, 1:-1, :-2]),
    ]
    result = jnp.zeros_like(center)
    for near_val, near_mob in pairs:
        result = result + face_mob(center_mob, near_mob) * (near_val - center)
    return result


def local(phase_field, mobility, x_inverse, y_inverse):
    planes, cy, cx = phase_field.shape
    order = y_inverse.shape[1]
    half = order // 2
    core, high = lax.axis_index("c"), lax.axis_index("yh")

    part = lax.dynamic_slice_in_dim(y_inverse, core * half, half, axis=1)
    y_mine = lax.all_gather(part, "z", axis=0, tiled=True)
    y_other = lax.ppermute(y_mine, "c", [(0, 1), (1, 0)])

    stacked = jnp.stack((phase_field, mobility))
    padded = extended(stacked, ((GX, 3, 2), (GY, 2, 3)))
    rows = extended(x_inverse, ((GX, 0, 1),))
    x_rows = lax.all_to_all(jnp.broadcast_to(rows[None], (4, *rows.shape)), ("yl", "c"), 0, 0, tiled=True)

    phase_pad, mob = padded[0], padded[1]
    first_pad = phase_pad[:, 1:-1, 1:-1] + step_size * laplace(phase_pad, mob)
    mob_near = mob[:, 1:-1, 1:-1]
    first = first_pad[:, 1:-1, 1:-1]
    second = (first + step_size * laplace(first_pad, mob_near)).astype(jnp.bfloat16)

    quarter = planes // 4
    lines = quarter * (cy + 2)
    send = second.reshape(2, 1, 2, lines, cx)
    send = jnp.broadcast_to(send, (2, 4, 2, lines, cx)).reshape(16, lines, cx)
    got = lax.all_to_all(send, GX, 0, 0, tiled=True)
    wide = x_rows.reshape(4, cx + 2, 16, cx)
    solved = jnp.einsum("slk,bnsk->bln", got, wide, preferred_element_type=jnp.float32)
    edges = solved.reshape(4, quarter, cy + 2, cx + 2)[:, :, 1:-1]
    edges = jnp.stack((edges[..., 0], edges[..., -1]), axis=1).reshape(4, 2 * quarter * cy // cx, cx)
    edge_rows = edges.shape[1]
    back = jnp.concatenate([solved[:, :, 1:-1], jnp.pad(edges, ((0, 0), (0, 8 - edge_rows), (0, 0)))], axis=1)
    back = lax.all_to_all(back, ("yl", "c"), 0, 0, tiled=True)
    solved = back[:, :lines].reshape(planes, cy + 2, cx)
    edges = back[:, lines : lines + edge_rows].reshape(4, 2, quarter, cy)
    edges = edges.transpose(1, 0, 2, 3).reshape(2, planes, cy)
    edges = jnp.pad(edges, ((0, 0), (0, 0), (1, 1)))
    solved_pad = jnp.concatenate([edges[0][..., None], solved, edges[1][..., None]], axis=2)
    chemical = solved_pad * solved_pad * solved_pad - solved_pad
    mob_last = mob[:, 2:-2, 1:-1]
    updated = (solved[:, 1:-1] + step_size * laplace(chemical, mob_last)).astype(jnp.bfloat16)

    mine = lax.all_to_all(updated, "z", 0, 0, tiled=True).reshape(half, cx)
    theirs = lax.ppermute(mine, "yh", [(0, 1), (1, 0)])
    same = core == high
    near = jnp.where(same, mine, theirs)
    far = jnp.where(same, theirs, mine)
    dot = lambda a, b: jnp.dot(a, b, preferred_element_type=jnp.float32)
    out = (dot(y_mine, near) + dot(y_other, far)).astype(jnp.bfloat16)
    out = lax.all_to_all(out.reshape(16, cy, cx), "z", 0, 0, tiled=True)
    return out.astype(jnp.float32)


def solution(mesh):
    shape = (2, mesh.shape["gx"] // 4, 2, 2, mesh.shape["gy"] // 2)
    torus = Mesh(mesh.devices.reshape(shape), ("yl", "x", "c", "yh", "z"))
    in_specs = (P(None, GY, GX), P(None, GY, GX), P(GX, None), P(GY, None))
    return jax.shard_map(local, mesh=torus, in_specs=in_specs, out_specs=P(None, GY, GX), check_vma=False)
```

```python
import jax
import jax.numpy as jnp
from jax import lax
from jax.experimental import pallas as pl
from jax.experimental.pallas import tpu as pltpu
from jax.sharding import Mesh
from jax.sharding import PartitionSpec as P

GX = ("yl", "x", "c")
GY = ("yh", "z")

step_size = 0.15


def extended(x, sides):
    for axis, dim, width in sides:
        size, length = (lax.axis_size(axis), x.shape[dim])
        up = [(i, (i + 1) % size) for i in range(size - 1)]
        down = [(j, i) for i, j in up]
        last = lax.slice_in_dim(x, length - width, length, axis=dim)
        leading = lax.slice_in_dim(x, 0, width, axis=dim)
        before = lax.ppermute(last, axis, up)
        after = lax.ppermute(leading, axis, down)
        x = jnp.concatenate([before, x, after], axis=dim)
    return x


def face_mob(center_mob, near_mob):
    return 2.0 * center_mob * near_mob / jnp.maximum(center_mob + near_mob, 0.25)


def laplace(values, mobile):
    values_z = jnp.pad(values, ((1, 1), (0, 0), (0, 0)))
    mobile_z = jnp.pad(mobile, ((1, 1), (0, 0), (0, 0)))
    center = values[:, 1:-1, 1:-1]
    center_mob = mobile[:, 1:-1, 1:-1]
    pairs = [
        (values_z[2:, 1:-1, 1:-1], mobile_z[2:, 1:-1, 1:-1]),
        (values_z[:-2, 1:-1, 1:-1], mobile_z[:-2, 1:-1, 1:-1]),
        (values[:, 2:, 1:-1], mobile[:, 2:, 1:-1]),
        (values[:, :-2, 1:-1], mobile[:, :-2, 1:-1]),
        (values[:, 1:-1, 2:], mobile[:, 1:-1, 2:]),
        (values[:, 1:-1, :-2], mobile[:, 1:-1, :-2]),
    ]
    result = jnp.zeros_like(center)
    for near_val, near_mob in pairs:
        result = result + face_mob(center_mob, near_mob) * (near_val - center)
    return result


NT = (((1,), (1,)), ((), ()))
VMEM = pl.BlockSpec(memory_space=pltpu.VMEM)


def solve_x_kernel(block_ref, got_ref, x0_ref, x1_ref, x2_ref, x3_ref, out_ref):
    own = block_ref[0]
    parts, lines, cx = got_ref.shape
    main = lines - 16
    a = jnp.concatenate([got_ref[s] for s in range(parts)], axis=1)
    for turn, x_ref in enumerate((x0_ref, x1_ref, x2_ref, x3_ref)):
        block = own ^ turn
        m = lax.dot_general(a, x_ref[:cx], NT, preferred_element_type=jnp.float32)
        out_ref[block, : main + 8] = m[: main + 8]
        e = lax.dot_general(x_ref[cx:], a[:main], NT, preferred_element_type=jnp.float32)
        out_ref[block, main + 8 : main + 10] = e[:2, :cx]
        out_ref[block, main + 10 : main + 12] = e[:2, cx:]
        out_ref[block, main + 12 :] = jnp.zeros((4, cx), jnp.float32)


def solve_x(block, got, x_blocks):
    parts, lines, cx = got.shape
    return pl.pallas_call(
        solve_x_kernel,
        out_shape=jax.ShapeDtypeStruct((4, lines, cx), jnp.float32),
        in_specs=[pl.BlockSpec(memory_space=pltpu.SMEM)] + [VMEM] * 5,
        out_specs=VMEM,
        name="solve_x",
    )(block, got, *x_blocks)


def local(phase_field, mobility, x_inverse, y_inverse):
    planes, cy, cx = phase_field.shape
    order = y_inverse.shape[1]
    half = order // 2
    core, high = lax.axis_index("c"), lax.axis_index("yh")

    part = lax.dynamic_slice_in_dim(y_inverse, core * half, half, axis=1)
    y_mine = lax.all_gather(part, "z", axis=0, tiled=True)
    y_other = lax.ppermute(y_mine, "c", [(0, 1), (1, 0)])

    stacked = jnp.stack((phase_field, mobility))
    padded = extended(stacked, ((GX, 3, 2), (GY, 2, 3)))
    rows = extended(x_inverse, ((GX, 0, 1),))
    rows = jnp.concatenate([rows[1:-1], rows[:1], rows[-1:], jnp.zeros((14, order), rows.dtype)], axis=0)
    swap = [(0, 1), (1, 0)]
    rows_yl = lax.ppermute(rows, "yl", swap)
    x_blocks = (rows, lax.ppermute(rows, "c", swap), rows_yl, lax.ppermute(rows_yl, "c", swap))

    phase_pad, mob = padded[0], padded[1]
    first_pad = phase_pad[:, 1:-1, 1:-1] + step_size * laplace(phase_pad, mob)
    mob_near = mob[:, 1:-1, 1:-1]
    first = first_pad[:, 1:-1, 1:-1]
    second = (first + step_size * laplace(first_pad, mob_near)).astype(jnp.bfloat16)

    quarter = planes // 4
    main = quarter * cy
    body = second[:, 1:-1].reshape(4, main, cx)
    rims = jnp.stack((second[:, 0], second[:, -1]), axis=1).reshape(4, 2 * quarter, cx)
    send = jnp.concatenate([body, rims, jnp.zeros((4, 16 - 2 * quarter, cx), body.dtype)], axis=1)
    lines = send.shape[1]
    send = send.reshape(2, 1, 2, lines, cx)
    send = jnp.broadcast_to(send, (2, 4, 2, lines, cx)).reshape(16, lines, cx)
    got = lax.all_to_all(send, GX, 0, 0, tiled=True)
    block = (lax.axis_index("yl") * 2 + core).reshape(1).astype(jnp.int32)
    back = solve_x(block, got, x_blocks)
    back = lax.all_to_all(back, ("yl", "c"), 0, 0, tiled=True)
    body = back[:, :main].reshape(planes, cy, cx)
    rims = back[:, main : main + 2 * quarter].reshape(planes, 2, cx)
    solved = jnp.concatenate([rims[:, :1], body, rims[:, 1:]], axis=1)
    edges = back[:, main + 8 : main + 12].reshape(4, 2, 2, 2, cy).transpose(0, 2, 1, 3, 4).reshape(4, 2, quarter, cy)
    edges = edges.transpose(1, 0, 2, 3).reshape(2, planes, cy)
    edges = jnp.pad(edges, ((0, 0), (0, 0), (1, 1)))
    solved_pad = jnp.concatenate([edges[0][..., None], solved, edges[1][..., None]], axis=2)
    chemical = solved_pad * solved_pad * solved_pad - solved_pad
    mob_last = mob[:, 2:-2, 1:-1]
    updated = (solved[:, 1:-1] + step_size * laplace(chemical, mob_last)).astype(jnp.bfloat16)

    mine = lax.all_to_all(updated, "z", 0, 0, tiled=True).reshape(half, cx)
    theirs = lax.ppermute(mine, "yh", [(0, 1), (1, 0)])
    same = core == high
    near = jnp.where(same, mine, theirs)
    far = jnp.where(same, theirs, mine)
    dot = lambda a, b: jnp.dot(a, b, preferred_element_type=jnp.float32)
    out = (dot(y_mine, near) + dot(y_other, far)).astype(jnp.bfloat16)
    out = lax.all_to_all(out.reshape(16, cy, cx), "z", 0, 0, tiled=True)
    return out.astype(jnp.float32)


def solution(mesh):
    shape = (2, mesh.shape["gx"] // 4, 2, 2, mesh.shape["gy"] // 2)
    torus = Mesh(mesh.devices.reshape(shape), ("yl", "x", "c", "yh", "z"))
    in_specs = (P(None, GY, GX), P(None, GY, GX), P(GX, None), P(GY, None))
    return jax.shard_map(local, mesh=torus, in_specs=in_specs, out_specs=P(None, GY, GX), check_vma=False)
```

```python
import jax
import jax.numpy as jnp
from jax import lax
from jax.experimental import pallas as pl
from jax.experimental.pallas import tpu as pltpu
from jax.sharding import Mesh
from jax.sharding import PartitionSpec as P

GX = ("yl", "x", "c")
GY = ("yh", "z")


step_size = 0.15


def extended(x, sides):
    for axis, dim, width in sides:
        size, length = (lax.axis_size(axis), x.shape[dim])
        up = [(i, (i + 1) % size) for i in range(size - 1)]
        down = [(j, i) for i, j in up]
        last = lax.slice_in_dim(x, length - width, length, axis=dim)
        leading = lax.slice_in_dim(x, 0, width, axis=dim)
        before = lax.ppermute(last, axis, up)
        after = lax.ppermute(leading, axis, down)
        x = jnp.concatenate([before, x, after], axis=dim)
    return x


def face_mob(center_mob, near_mob):
    return 2.0 * center_mob * near_mob / jnp.maximum(center_mob + near_mob, 0.25)


def laplace(values, mobile):
    values_z = jnp.pad(values, ((1, 1), (0, 0), (0, 0)))
    mobile_z = jnp.pad(mobile, ((1, 1), (0, 0), (0, 0)))
    center = values[:, 1:-1, 1:-1]
    center_mob = mobile[:, 1:-1, 1:-1]
    pairs = [
        (values_z[2:, 1:-1, 1:-1], mobile_z[2:, 1:-1, 1:-1]),
        (values_z[:-2, 1:-1, 1:-1], mobile_z[:-2, 1:-1, 1:-1]),
        (values[:, 2:, 1:-1], mobile[:, 2:, 1:-1]),
        (values[:, :-2, 1:-1], mobile[:, :-2, 1:-1]),
        (values[:, 1:-1, 2:], mobile[:, 1:-1, 2:]),
        (values[:, 1:-1, :-2], mobile[:, 1:-1, :-2]),
    ]
    result = jnp.zeros_like(center)
    for near_val, near_mob in pairs:
        result = result + face_mob(center_mob, near_mob) * (near_val - center)
    return result


NT = (((1,), (1,)), ((), ()))
VMEM = pl.BlockSpec(memory_space=pltpu.VMEM)


def solve_x_kernel(block_ref, got_ref, x0_ref, x1_ref, x2_ref, x3_ref, out_ref):
    own = block_ref[0]
    parts, lines, cx = got_ref.shape
    main = lines - 16
    a = jnp.concatenate([got_ref[s] for s in range(parts)], axis=1)
    for turn, x_ref in enumerate((x0_ref, x1_ref, x2_ref, x3_ref)):
        block = own ^ turn
        m = lax.dot_general(a, x_ref[:cx], NT, preferred_element_type=jnp.float32)
        out_ref[block, : main + 8] = m[: main + 8]
        e = lax.dot_general(x_ref[cx:], a[:main], NT, preferred_element_type=jnp.float32)
        out_ref[block, main + 8 : main + 10] = e[:2, :cx]
        out_ref[block, main + 10 : main + 12] = e[:2, cx:]
        out_ref[block, main + 12 :] = jnp.zeros((4, cx), jnp.float32)


def solve_x(block, got, x_blocks):
    parts, lines, cx = got.shape
    return pl.pallas_call(
        solve_x_kernel,
        out_shape=pltpu.VMEM((4, lines, cx), jnp.float32),
        in_specs=[pl.BlockSpec(memory_space=pltpu.SMEM)] + [VMEM] * 5,
        out_specs=VMEM,
        compiler_params=pltpu.CompilerParams(vmem_limit_bytes=16 << 20),
        name="solve_x",
    )(block, *[pltpu.with_memory_space_constraint(v, pltpu.VMEM) for v in (got, *x_blocks)])


def solve_y_kernel(side_ref, y0_ref, y1_ref, y2_ref, y3_ref, u0_ref, u1_ref, out_ref, u_ref):
    low, core, high = side_ref[0], side_ref[1], side_ref[2]
    rows, cx = u0_ref.shape
    fourth = rows // 2
    u_ref[high] = u0_ref[...]
    u_ref[1 - high] = u1_ref[...]

    def part(y, h, q):
        u = u_ref[h, pl.ds(pl.multiple_of(q * fourth, fourth), fourth)]
        return jnp.dot(y, u, preferred_element_type=jnp.float32)

    total = part(y0_ref[...], core, low) + part(y1_ref[...], core, 1 - low)
    total = total + part(y2_ref[...], 1 - core, low) + part(y3_ref[...], 1 - core, 1 - low)
    out_ref[...] = total.astype(out_ref.dtype)


def solve_y(sides, *parts):
    rows, cx = parts[-1].shape
    return pl.pallas_call(
        solve_y_kernel,
        out_shape=pltpu.VMEM((rows, cx), jnp.bfloat16),
        in_specs=[pl.BlockSpec(memory_space=pltpu.SMEM)] + [VMEM] * 6,
        out_specs=VMEM,
        scratch_shapes=[pltpu.VMEM((2, rows, cx), jnp.bfloat16)],
        compiler_params=pltpu.CompilerParams(vmem_limit_bytes=16 << 20),
        name="solve_y",
    )(sides, *[pltpu.with_memory_space_constraint(v, pltpu.VMEM) for v in parts])


def local(phase_field, mobility, x_inverse, y_inverse):
    planes, cy, cx = phase_field.shape
    order = y_inverse.shape[1]
    half = order // 2
    core, high = lax.axis_index("c"), lax.axis_index("yh")

    swap = [(0, 1), (1, 0)]
    fourth = order // 4
    low = lax.axis_index("yl")
    part = lax.dynamic_slice_in_dim(y_inverse, (core * 2 + low) * fourth, fourth, axis=1)
    part, phase_field, mobility = lax.optimization_barrier((part, phase_field, mobility))
    y_quarter = lax.all_gather(part, "z", axis=0, tiled=True)

    stacked = jnp.stack((phase_field, mobility))
    padded = extended(stacked, ((GX, 3, 2), (GY, 2, 3)))
    rows = extended(x_inverse, ((GX, 0, 1),))
    rows = jnp.concatenate([rows[1:-1], rows[:1], rows[-1:], jnp.zeros((14, order), rows.dtype)], axis=0)
    rows_yl = lax.ppermute(rows, "yl", swap)
    x_blocks = (rows, lax.ppermute(rows, "c", swap), rows_yl, lax.ppermute(rows_yl, "c", swap))

    phase_pad, mob = padded[0], padded[1]
    first_pad = phase_pad[:, 1:-1, 1:-1] + step_size * laplace(phase_pad, mob)
    mob_near = mob[:, 1:-1, 1:-1]
    first = first_pad[:, 1:-1, 1:-1]
    second = (first + step_size * laplace(first_pad, mob_near)).astype(jnp.bfloat16)

    quarter = planes // 4
    main = quarter * cy
    body = second[:, 1:-1].reshape(4, main, cx)
    rims = jnp.stack((second[:, 0], second[:, -1]), axis=1).reshape(4, 2 * quarter, cx)
    send = jnp.concatenate([body, rims, jnp.zeros((4, 16 - 2 * quarter, cx), body.dtype)], axis=1)
    lines = send.shape[1]
    send = send.reshape(2, 1, 2, lines, cx)
    send = jnp.broadcast_to(send, (2, 4, 2, lines, cx)).reshape(16, lines, cx)
    got = lax.all_to_all(send, GX, 0, 0, tiled=True)
    block = (low * 2 + core).reshape(1).astype(jnp.int32)
    back = solve_x(block, got, x_blocks)
    back = lax.all_to_all(back, ("yl", "c"), 0, 0, tiled=True)
    body = back[:, :main].reshape(planes, cy, cx)
    rims = back[:, main : main + 2 * quarter].reshape(planes, 2, cx)
    solved = jnp.concatenate([rims[:, :1], body, rims[:, 1:]], axis=1)
    edges = back[:, main + 8 : main + 12].reshape(4, 2, 2, 2, cy).transpose(0, 2, 1, 3, 4).reshape(4, 2, quarter, cy)
    edges = edges.transpose(1, 0, 2, 3).reshape(2, planes, cy)
    edges = jnp.pad(edges, ((0, 0), (0, 0), (1, 1)))
    solved_pad = jnp.concatenate([edges[0][..., None], solved, edges[1][..., None]], axis=2)
    chemical = solved_pad * solved_pad * solved_pad - solved_pad
    mob_last = mob[:, 2:-2, 1:-1]
    updated = (solved[:, 1:-1] + step_size * laplace(chemical, mob_last)).astype(jnp.bfloat16)

    y_quarter, updated = lax.optimization_barrier((y_quarter, updated))
    y_beside = lax.ppermute(y_quarter, "yl", swap)
    y_across = lax.ppermute(y_quarter, "c", swap)
    mine = lax.all_to_all(updated, "z", 0, 0, tiled=True).reshape(half, cx)
    theirs = lax.ppermute(mine, "yh", swap)
    y_beside, mine = lax.optimization_barrier((y_beside, mine))
    y_far = lax.ppermute(y_beside, "c", swap)
    sides = jnp.stack((low, core, high)).astype(jnp.int32)
    out = solve_y(sides, y_quarter, y_beside, y_across, y_far, mine, theirs)
    out = lax.all_to_all(out.reshape(16, cy, cx), "z", 0, 0, tiled=True)
    return out.astype(jnp.float32)


def solution(mesh):
    shape = (2, mesh.shape["gx"] // 4, 2, 2, mesh.shape["gy"] // 2)
    torus = Mesh(mesh.devices.reshape(shape), ("yl", "x", "c", "yh", "z"))
    in_specs = (P(None, GY, GX), P(None, GY, GX), P(GX, None), P(GY, None))
    return jax.shard_map(local, mesh=torus, in_specs=in_specs, out_specs=P(None, GY, GX), check_vma=False)
```

```python
import jax
import jax.numpy as jnp
from jax import lax
from jax.experimental import pallas as pl
from jax.experimental.pallas import tpu as pltpu
from jax.sharding import Mesh
from jax.sharding import PartitionSpec as P

GX = ("yl", "x", "c")
GY = ("yh", "z")


step_size = 0.15


def extended(x, sides):
    for axis, dim, width in sides:
        size, length = (lax.axis_size(axis), x.shape[dim])
        up = [(i, (i + 1) % size) for i in range(size - 1)]
        down = [(j, i) for i, j in up]
        last = lax.slice_in_dim(x, length - width, length, axis=dim)
        leading = lax.slice_in_dim(x, 0, width, axis=dim)
        before = lax.ppermute(last, axis, up)
        after = lax.ppermute(leading, axis, down)
        x = jnp.concatenate([before, x, after], axis=dim)
    return x


def face_mob(center_mob, near_mob):
    return 2.0 * center_mob * near_mob / jnp.maximum(center_mob + near_mob, 0.25)


def laplace(values, mobile):
    values_z = jnp.pad(values, ((1, 1), (0, 0), (0, 0)))
    mobile_z = jnp.pad(mobile, ((1, 1), (0, 0), (0, 0)))
    center = values[:, 1:-1, 1:-1]
    center_mob = mobile[:, 1:-1, 1:-1]
    pairs = [
        (values_z[2:, 1:-1, 1:-1], mobile_z[2:, 1:-1, 1:-1]),
        (values_z[:-2, 1:-1, 1:-1], mobile_z[:-2, 1:-1, 1:-1]),
        (values[:, 2:, 1:-1], mobile[:, 2:, 1:-1]),
        (values[:, :-2, 1:-1], mobile[:, :-2, 1:-1]),
        (values[:, 1:-1, 2:], mobile[:, 1:-1, 2:]),
        (values[:, 1:-1, :-2], mobile[:, 1:-1, :-2]),
    ]
    result = jnp.zeros_like(center)
    for near_val, near_mob in pairs:
        result = result + face_mob(center_mob, near_mob) * (near_val - center)
    return result


NT = (((1,), (1,)), ((), ()))
VMEM = pl.BlockSpec(memory_space=pltpu.VMEM)


def solve_x_kernel(block_ref, got_ref, x0_ref, x1_ref, x2_ref, x3_ref, out_ref):
    own = block_ref[0]
    parts, lines, cx = got_ref.shape
    main = lines - 16
    a = jnp.concatenate([got_ref[s] for s in range(parts)], axis=1)
    for turn, x_ref in enumerate((x0_ref, x1_ref, x2_ref, x3_ref)):
        block = own ^ turn
        m = lax.dot_general(a, x_ref[:cx], NT, preferred_element_type=jnp.float32)
        out_ref[block, : main + 8] = m[: main + 8]
        e = lax.dot_general(x_ref[cx:], a[:main], NT, preferred_element_type=jnp.float32)
        out_ref[block, main + 8 : main + 10] = e[:2, :cx]
        out_ref[block, main + 10 : main + 12] = e[:2, cx:]
        out_ref[block, main + 12 :] = jnp.zeros((4, cx), jnp.float32)


def solve_x(block, got, x_blocks):
    parts, lines, cx = got.shape
    return pl.pallas_call(
        solve_x_kernel,
        out_shape=pltpu.VMEM((4, lines, cx), jnp.float32),
        in_specs=[pl.BlockSpec(memory_space=pltpu.SMEM)] + [VMEM] * 5,
        out_specs=VMEM,
        compiler_params=pltpu.CompilerParams(vmem_limit_bytes=16 << 20),
        name="solve_x",
    )(block, *[pltpu.with_memory_space_constraint(v, pltpu.VMEM) for v in (got, *x_blocks)])


def solve_y_kernel(side_ref, y_ref, u0_ref, u1_ref, out_ref):
    high = side_ref[0]
    half, cx = u0_ref.shape
    y0 = y_ref[:, pl.ds(pl.multiple_of(high * half, half), half)]
    y1 = y_ref[:, pl.ds(pl.multiple_of((1 - high) * half, half), half)]
    total = jnp.dot(y0, u0_ref[...], preferred_element_type=jnp.float32)
    total = total + jnp.dot(y1, u1_ref[...], preferred_element_type=jnp.float32)
    out_ref[...] = total.astype(out_ref.dtype)


def solve_y(side, *parts):
    rows, cx = parts[-1].shape
    return pl.pallas_call(
        solve_y_kernel,
        out_shape=pltpu.VMEM((rows, cx), jnp.bfloat16),
        in_specs=[pl.BlockSpec(memory_space=pltpu.SMEM)] + [VMEM] * 3,
        out_specs=VMEM,
        compiler_params=pltpu.CompilerParams(vmem_limit_bytes=16 << 20),
        name="solve_y",
    )(side, *[pltpu.with_memory_space_constraint(v, pltpu.VMEM) for v in parts])


def local(phase_field, mobility, x_inverse, y_inverse):
    planes, cy, cx = phase_field.shape
    order = y_inverse.shape[1]
    half = order // 2
    core, high = lax.axis_index("c"), lax.axis_index("yh")

    swap = [(0, 1), (1, 0)]
    low = lax.axis_index("yl")
    y_rows = lax.all_gather(y_inverse, "z", axis=0, tiled=True)

    stacked = jnp.stack((phase_field, mobility))
    padded = extended(stacked, ((GX, 3, 2), (GY, 2, 3)))
    rows = extended(x_inverse, ((GX, 0, 1),))
    rows = jnp.concatenate([rows[1:-1], rows[:1], rows[-1:], jnp.zeros((14, order), rows.dtype)], axis=0)
    rows_yl = lax.ppermute(rows, "yl", swap)
    x_blocks = (rows, lax.ppermute(rows, "c", swap), rows_yl, lax.ppermute(rows_yl, "c", swap))

    phase_pad, mob = padded[0], padded[1]
    first_pad = phase_pad[:, 1:-1, 1:-1] + step_size * laplace(phase_pad, mob)
    mob_near = mob[:, 1:-1, 1:-1]
    first = first_pad[:, 1:-1, 1:-1]
    second = (first + step_size * laplace(first_pad, mob_near)).astype(jnp.bfloat16)

    quarter = planes // 4
    main = quarter * cy
    body = second[:, 1:-1].reshape(4, main, cx)
    rims = jnp.stack((second[:, 0], second[:, -1]), axis=1).reshape(4, 2 * quarter, cx)
    send = jnp.concatenate([body, rims, jnp.zeros((4, 16 - 2 * quarter, cx), body.dtype)], axis=1)
    lines = send.shape[1]
    send = send.reshape(2, 1, 2, lines, cx)
    send = jnp.broadcast_to(send, (2, 4, 2, lines, cx)).reshape(16, lines, cx)
    got = lax.all_to_all(send, GX, 0, 0, tiled=True)
    block = (low * 2 + core).reshape(1).astype(jnp.int32)
    back = solve_x(block, got, x_blocks)
    back = lax.all_to_all(back, ("yl", "c"), 0, 0, tiled=True)
    body = back[:, :main].reshape(planes, cy, cx)
    rims = back[:, main : main + 2 * quarter].reshape(planes, 2, cx)
    solved = jnp.concatenate([rims[:, :1], body, rims[:, 1:]], axis=1)
    edges = back[:, main + 8 : main + 12].reshape(4, 2, 2, 2, cy).transpose(0, 2, 1, 3, 4).reshape(4, 2, quarter, cy)
    edges = edges.transpose(1, 0, 2, 3).reshape(2, planes, cy)
    edges = jnp.pad(edges, ((0, 0), (0, 0), (1, 1)))
    solved_pad = jnp.concatenate([edges[0][..., None], solved, edges[1][..., None]], axis=2)
    chemical = solved_pad * solved_pad * solved_pad - solved_pad
    mob_last = mob[:, 2:-2, 1:-1]
    updated = (solved[:, 1:-1] + step_size * laplace(chemical, mob_last)).astype(jnp.bfloat16)

    mine = lax.all_to_all(updated, "z", 0, 0, tiled=True).reshape(half, cx)
    theirs = lax.ppermute(mine, "yh", swap)
    out = solve_y(high.reshape(1).astype(jnp.int32), y_rows, mine, theirs)
    out = lax.all_to_all(out.reshape(16, cy, cx), "z", 0, 0, tiled=True)
    return out.astype(jnp.float32)


def solution(mesh):
    shape = (2, mesh.shape["gx"] // 4, 2, 2, mesh.shape["gy"] // 2)
    torus = Mesh(mesh.devices.reshape(shape), ("yl", "x", "c", "yh", "z"))
    in_specs = (P(None, GY, GX), P(None, GY, GX), P(GX, None), P(GY, None))
    return jax.shard_map(local, mesh=torus, in_specs=in_specs, out_specs=P(None, GY, GX), check_vma=False)
```

```python
import jax
import jax.numpy as jnp
from jax import lax
from jax.experimental import pallas as pl
from jax.experimental.pallas import tpu as pltpu
from jax.sharding import Mesh
from jax.sharding import PartitionSpec as P

GX = ("yl", "x", "c")
GY = ("yh", "z")

step_size = 0.15
F32 = jnp.float32
BF16 = jnp.bfloat16
NT = (((1,), (1,)), ((), ()))
VMEM = pl.BlockSpec(memory_space=pltpu.VMEM)
OFF = 8


def near(v):
    return pltpu.with_memory_space_constraint(v, pltpu.VMEM)


def kept(shape, dtype):
    return pltpu.VMEM(shape, dtype)


def call(kernel, name, out_shape, args, scalar=None, scratch=()):
    scalars = [] if scalar is None else [scalar]
    many = isinstance(out_shape, tuple)
    return pl.pallas_call(
        kernel,
        out_shape=out_shape,
        in_specs=[pl.BlockSpec(memory_space=pltpu.SMEM)] * len(scalars) + [VMEM] * len(args),
        out_specs=(VMEM,) * len(out_shape) if many else VMEM,
        scratch_shapes=list(scratch),
        compiler_params=pltpu.CompilerParams(vmem_limit_bytes=16 << 20),
        name=name,
    )(*scalars, *[near(v) for v in args])


def face_mob(p, q):
    return 2.0 * p * q / jnp.maximum(p + q, 0.25)


def turn(x, shift, axis):
    return pltpu.roll(x, shift % x.shape[axis], axis)


def places(shape, axis):
    return lax.broadcasted_iota(jnp.int32, shape, axis)


def pack_x_kernel(p_ref, m_ref, first_ref, last_ref, left_ref, right_ref):
    planes, cy, cx = p_ref.shape
    pairs = planes // 2
    for a, ref in enumerate((p_ref, m_ref)):
        for i in range(pairs):
            t = jnp.concatenate([ref[i], ref[i + pairs]], axis=0).T
            for j in range(2):
                k = (2 * a + j) * pairs + i
                left_ref[k : k + 1, :] = t[j : j + 1]
                right_ref[k : k + 1, :] = t[cx - 2 + j : cx - 1 + j]
    base = 4 * pairs
    first = first_ref[0:1, :].astype(F32)
    last = last_ref[15:16, :].astype(F32)
    for s in range(16):
        left_ref[base + s : base + s + 1, :] = first[:, s * cx : (s + 1) * cx]
        right_ref[base + s : base + s + 1, :] = last[:, s * cx : (s + 1) * cx]


def strip(x, cy):
    both = jnp.concatenate([turn(x, OFF, 1), turn(x, OFF - cy, 1)], axis=0)
    lane = places(both.shape, 1)
    return jnp.where((lane >= OFF) & (lane < OFF + cy), both, 0.0)


def received(left_ref, right_ref, a, pairs, cy):
    refs = ((left_ref, 2 * a), (left_ref, 2 * a + 1), (right_ref, 2 * a), (right_ref, 2 * a + 1))
    return [strip(ref[k * pairs : (k + 1) * pairs, :], cy) for ref, k in refs]


def pack_y_kernel(p_ref, m_ref, left_ref, right_ref, up_ref, down_ref):
    planes, cy, cx = p_ref.shape
    for a, ref in enumerate((p_ref, m_ref)):
        for r in range(3):
            up_ref[3 * a + r] = ref[:, cy - 3 + r, :]
            down_ref[3 * a + r] = ref[:, r, :]
    lane = places((planes, cx), 1)
    up = jnp.zeros((planes, cx), F32)
    down = up
    for a in range(2):
        for j, s in enumerate(received(left_ref, right_ref, a, planes // 2, cy)):
            at = 3 * (4 * a + j)
            here = (lane >= at) & (lane < at + 3)
            up = jnp.where(here, turn(s, at - (OFF + cy - 3), 1), up)
            down = jnp.where(here, turn(s, at - OFF, 1), down)
    up_ref[6] = up
    down_ref[6] = down


def explicit_kernel(
    p_ref, m_ref, own_l_ref, own_r_ref, left_ref, right_ref, up_ref, down_ref,
    send_ref, fz_ref, fy_ref, fx_ref, edge_ref,
    v_ref, c_ref, f_ref, side_ref, rim_ref,
):
    planes, cy, cx = p_ref.shape
    pairs = planes // 2
    tall = cy + 2 * OFF
    lane = places((planes, cx), 1)
    plane = places((planes, cx), 0)

    def strips(a):
        out = []
        for j, s in enumerate(received(left_ref, right_ref, a, pairs, cy)):
            at = 3 * (4 * a + j)
            s = jnp.where((lane >= OFF - 3) & (lane < OFF), turn(up_ref[6], OFF - 3 - at, 1), s)
            s = jnp.where((lane >= OFF + cy) & (lane < OFF + cy + 3), turn(down_ref[6], OFF + cy - at, 1), s)
            out.append(s)
        own = []
        for ref, j, at in ((own_l_ref, 0, 0), (own_l_ref, 1, 1), (own_r_ref, 0, cx - 2), (own_r_ref, 1, cx - 1)):
            k = 2 * a + j
            s = strip(ref[k * pairs : (k + 1) * pairs, :], cy)
            for r in (1, 2):
                s = jnp.where(lane == OFF - 3 + r, turn(up_ref[3 * a + r], OFF - 3 + r - at, 1), s)
            for r in (0, 1):
                s = jnp.where(lane == OFF + cy + r, turn(down_ref[3 * a + r], OFF + cy + r - at, 1), s)
            own.append(s)
        return out[:2] + own[:2], own[2:] + out[2:]

    def strip_first(v, m, vl, ml, vr, mr):
        above = jnp.where(plane == planes - 1, 0.0, turn(m, -1, 0))
        fz = face_mob(m, above)
        gz = fz * (turn(v, -1, 0) - v)
        fy = face_mob(m, turn(m, -1, 1))
        gy = fy * (turn(v, -1, 1) - v)
        lap = gz - jnp.where(plane == 0, 0.0, turn(gz, 1, 0)) + gy - turn(gy, 1, 1)
        lap = lap + face_mob(m, mr) * (vr - v) + face_mob(m, ml) * (vl - v)
        return v + step_size * lap

    columns = []
    for side, (v, m) in enumerate(zip(strips(0), strips(1), strict=True)):
        f = face_mob(m[1], m[2])
        a = strip_first(v[1], m[1], v[0], m[0], v[2], m[2])
        b = strip_first(v[2], m[2], v[1], m[1], v[3], m[3])
        columns += [f * (v[2] - v[1]), f * (b - a)]
        side_ref[...] = f
        even = turn(side_ref[pl.ds(0, pairs, stride=2), :], -OFF, 1)
        odd = turn(side_ref[pl.ds(1, pairs, stride=2), :], cy - OFF, 1)
        edge_ref[side * pairs : (side + 1) * pairs, :] = jnp.where(lane[:pairs] < cy, even, odd)
    stacked = jnp.concatenate(columns + [jnp.zeros((cx - 4 * planes, cx), F32)], axis=0)
    across = stacked.T[:tall]

    def column(k, z):
        at = k * planes + z
        return jnp.broadcast_to(across[:, at : at + 1], (tall, cx))

    blank = jnp.zeros((OFF, cx), F32)
    for ref in (v_ref, c_ref, f_ref):
        for z in (0, planes + 1):
            ref[z * tall : (z + 1) * tall, :] = jnp.zeros((tall, cx), F32)
    for ref, a, field in ((v_ref, 0, p_ref), (c_ref, 1, m_ref)):
        for z in range(planes):
            base = (z + 1) * tall
            ref[base : base + OFF, :] = blank
            ref[base + OFF : base + OFF + cy, :] = field[z]
            ref[base + OFF + cy : base + tall, :] = blank
        for r in range(3):
            ref[pl.ds(tall + OFF - 3 + r, planes, stride=tall), :] = up_ref[3 * a + r]
            ref[pl.ds(tall + OFF + cy + r, planes, stride=tall), :] = down_ref[3 * a + r]

    wide = places((tall, cx), 1)

    def step(v, above, fz, fy, fx, gz_before, gl, gr):
        gz = fz * (above - v)
        gy = fy * (turn(v, -1, 0) - v)
        gx = jnp.where(wide == 0, gl, fx * (v - turn(v, 1, 1)))
        lap = gz - gz_before + gy - turn(gy, 1, 0)
        lap = lap + jnp.where(wide == cx - 1, gr, turn(gx, -1, 1)) - gx
        return v + step_size * lap, gz

    fz_ref[:tall, :] = jnp.zeros((tall, cx), F32)
    before = jnp.zeros((tall, cx), F32)
    for z in range(planes):
        here, above = pl.ds((z + 1) * tall, tall), pl.ds((z + 2) * tall, tall)
        flat = pl.ds(z * tall, tall)
        m = c_ref[here, :]
        fz = face_mob(m, c_ref[above, :])
        fy = face_mob(m, turn(m, -1, 0))
        fx = face_mob(m, turn(m, 1, 1))
        fz_ref[here, :] = fz
        fy_ref[flat, :] = fy
        fx_ref[flat, :] = fx
        out, before = step(v_ref[here, :], v_ref[above, :], fz, fy, fx, before, column(0, z), column(2, z))
        f_ref[here, :] = out

    rim_ref[...] = jnp.zeros(rim_ref.shape, F32)
    before = jnp.zeros((tall, cx), F32)
    quarter = planes // 4
    for z in range(planes):
        here, above = pl.ds((z + 1) * tall, tall), pl.ds((z + 2) * tall, tall)
        flat = pl.ds(z * tall, tall)
        out, before = step(
            f_ref[here, :], f_ref[above, :], fz_ref[here, :], fy_ref[flat, :], fx_ref[flat, :],
            before, column(1, z), column(3, z),
        )
        q, at = z // quarter, z % quarter
        body = out[OFF : OFF + cy].astype(BF16)
        for x in range(4):
            send_ref[(q // 2) * 8 + x * 2 + q % 2, at * cy : (at + 1) * cy, :] = body
        rim_ref[q, 2 * at : 2 * at + 1, :] = out[OFF - 1 : OFF]
        rim_ref[q, 2 * at + 1 : 2 * at + 2, :] = out[OFF + cy : OFF + cy + 1]
    for q in range(4):
        rims = rim_ref[q].astype(BF16)
        for x in range(4):
            send_ref[(q // 2) * 8 + x * 2 + q % 2, quarter * cy :, :] = rims


def solve_x_kernel(block_ref, got_ref, x0_ref, x1_ref, x2_ref, x3_ref, out_ref):
    own = block_ref[0]
    parts, lines, cx = got_ref.shape
    main = lines - 16
    a = jnp.concatenate([got_ref[s] for s in range(parts)], axis=1)
    for other, x_ref in enumerate((x0_ref, x1_ref, x2_ref, x3_ref)):
        block = own ^ other
        m = lax.dot_general(a, x_ref[:cx], NT, preferred_element_type=F32)
        out_ref[block, : main + 8] = m[: main + 8]
        e = lax.dot_general(x_ref[cx:], a[:main], NT, preferred_element_type=F32)
        out_ref[block, main + 8 : main + 12] = e[:4, :cx]
        out_ref[block, main + 12 :] = e[:4, cx:]


def implicit_kernel(back_ref, fz_ref, fy_ref, fx_ref, edge_ref, out_ref, c_ref, e_ref):
    planes, cy, cx = out_ref.shape
    tall = cy + 2 * OFF
    quarter, pairs = planes // 4, planes // 2
    main = quarter * cy

    def chemical(s):
        return s * s * s - s

    for z in (0, planes + 1):
        c_ref[z * tall : (z + 1) * tall, :] = jnp.zeros((tall, cx), F32)
    for q in range(4):
        e_ref[q * 8 : (q + 1) * 8, :] = chemical(back_ref[q, main + 8 : main + 16])
        rims = chemical(back_ref[q, main : main + 8])
        for at in range(quarter):
            base = (q * quarter + at + 1) * tall
            c_ref[base + OFF : base + OFF + cy, :] = chemical(back_ref[q, at * cy : (at + 1) * cy])
            c_ref[base + OFF - 1 : base + OFF, :] = rims[2 * at : 2 * at + 1]
            c_ref[base + OFF + cy : base + OFF + cy + 1, :] = rims[2 * at + 1 : 2 * at + 2]
    ends = [e_ref[pl.ds(j, pairs, stride=4), :] for j in range(4)]
    left = edge_ref[:pairs, :] * (ends[1] - ends[0])
    right = edge_ref[pairs:, :] * (ends[3] - ends[2])
    across = jnp.concatenate([left, right, jnp.zeros((cx - planes, cx), F32)], axis=0).T
    lane = places((cy, cx), 1)
    before = jnp.zeros((cy, cx), F32)
    for z in range(planes):
        base = (z + 1) * tall + OFF
        flat = z * tall + OFF
        c = c_ref[base : base + cy, :]
        gz = fz_ref[base : base + cy, :] * (c_ref[base + tall : base + tall + cy, :] - c)
        gy = fy_ref[flat : flat + cy, :] * (c_ref[base + 1 : base + 1 + cy, :] - c)
        gu = fy_ref[flat - 1 : flat - 1 + cy, :] * (c - c_ref[base - 1 : base - 1 + cy, :])
        rows = slice((z % 2) * cy, (z % 2 + 1) * cy)
        gl = jnp.broadcast_to(across[rows, z // 2 : z // 2 + 1], (cy, cx))
        gr = jnp.broadcast_to(across[rows, pairs + z // 2 : pairs + z // 2 + 1], (cy, cx))
        gx = jnp.where(lane == 0, gl, fx_ref[flat : flat + cy, :] * (c - turn(c, 1, 1)))
        lap = gz - before + gy - gu + jnp.where(lane == cx - 1, gr, turn(gx, -1, 1)) - gx
        s = back_ref[z // quarter, (z % quarter) * cy : (z % quarter + 1) * cy]
        out_ref[z] = (s + step_size * lap).astype(BF16)
        before = gz


def solve_y_kernel(side_ref, y_ref, u0_ref, u1_ref, out_ref):
    high = side_ref[0]
    half, cx = u0_ref.shape
    y0 = y_ref[:, pl.ds(pl.multiple_of(high * half, half), half)]
    y1 = y_ref[:, pl.ds(pl.multiple_of((1 - high) * half, half), half)]
    total = jnp.dot(y0, u0_ref[...], preferred_element_type=F32)
    total = total + jnp.dot(y1, u1_ref[...], preferred_element_type=F32)
    out_ref[...] = total.astype(BF16)


def pack_x(p, m, x_inverse):
    _, _, cx = p.shape
    shape = (2 * p.shape[0] + 16, cx)
    return call(pack_x_kernel, "pack_x", (kept(shape, F32),) * 2, (p, m, x_inverse[:16], x_inverse[-16:]))


def pack_y(p, m, left, right):
    shape = (7, p.shape[0], p.shape[2])
    return call(pack_y_kernel, "pack_y", (kept(shape, F32),) * 2, (p, m, left, right))


def explicit(*args):
    planes, cy, cx = args[0].shape
    tall = cy + 2 * OFF
    lines = planes // 4 * cy + 16
    field = pltpu.VMEM(((planes + 2) * tall, cx), F32)
    out = (
        kept((16, lines, cx), BF16),
        kept(((planes + 1) * tall, cx), F32),
        kept((planes * tall, cx), F32),
        kept((planes * tall, cx), F32),
        kept((planes, cx), F32),
    )
    scratch = (field, field, field, pltpu.VMEM((planes, cx), F32), pltpu.VMEM((4, 16, cx), F32))
    return call(explicit_kernel, "explicit", out, args, scratch=scratch)


def solve_x(block, got, x_blocks):
    _, lines, cx = got.shape
    return call(solve_x_kernel, "solve_x", kept((4, lines, cx), F32), (got, *x_blocks), scalar=block)


def implicit(back, faces, planes, cy):
    cx = back.shape[2]
    scratch = (pltpu.VMEM(((planes + 2) * (cy + 2 * OFF), cx), F32), pltpu.VMEM((32, cx), F32))
    return call(implicit_kernel, "implicit", kept((planes, cy, cx), BF16), (back, *faces), scratch=scratch)


def solve_y(side, *parts):
    return call(solve_y_kernel, "solve_y", kept(parts[-1].shape, BF16), parts, scalar=side)


def both_ways(to_before, to_after, axis):
    size = lax.axis_size(axis)
    up = [(i, i + 1) for i in range(size - 1)]
    return lax.ppermute(to_after, axis, up), lax.ppermute(to_before, axis, [(j, i) for i, j in up])


def local(phase_field, mobility, x_inverse, y_inverse):
    planes, cy, cx = phase_field.shape
    order = y_inverse.shape[1]
    half = order // 2
    core, low, high = lax.axis_index("c"), lax.axis_index("yl"), lax.axis_index("yh")
    swap = [(0, 1), (1, 0)]

    y_rows = lax.all_gather(y_inverse, "z", axis=0, tiled=True)

    own_l, own_r = pack_x(phase_field, mobility, x_inverse)
    left, right = both_ways(own_l, own_r, GX)
    to_up, to_down = pack_y(phase_field, mobility, left, right)
    up, down = both_ways(to_down, to_up, GY)

    row_before = left[-16:].reshape(1, order).astype(BF16)
    row_after = right[-16:].reshape(1, order).astype(BF16)
    ends = [x_inverse, row_before, x_inverse[:1], x_inverse[-1:], row_after, jnp.zeros((12, order), BF16)]
    rows = jnp.concatenate(ends, axis=0)
    rows_yl = lax.ppermute(rows, "yl", swap)
    x_blocks = (rows, lax.ppermute(rows, "c", swap), rows_yl, lax.ppermute(rows_yl, "c", swap))

    send, *faces = explicit(phase_field, mobility, own_l, own_r, left, right, up, down)
    got = lax.all_to_all(send, GX, 0, 0, tiled=True)
    back = solve_x((low * 2 + core).reshape(1).astype(jnp.int32), got, x_blocks)
    back = lax.all_to_all(back, ("yl", "c"), 0, 0, tiled=True)
    updated = implicit(back, faces, planes, cy)

    mine = lax.all_to_all(updated, "z", 0, 0, tiled=True).reshape(half, cx)
    y_rows, mine = lax.optimization_barrier((y_rows, mine))
    theirs = lax.ppermute(mine, "yh", swap)
    out = solve_y(high.reshape(1).astype(jnp.int32), y_rows, mine, theirs)
    out = lax.all_to_all(out.reshape(16, cy, cx), "z", 0, 0, tiled=True)
    return out.astype(F32)


def solution(mesh):
    shape = (2, mesh.shape["gx"] // 4, 2, 2, mesh.shape["gy"] // 2)
    torus = Mesh(mesh.devices.reshape(shape), ("yl", "x", "c", "yh", "z"))
    in_specs = (P(None, GY, GX), P(None, GY, GX), P(GX, None), P(GY, None))
    return jax.shard_map(local, mesh=torus, in_specs=in_specs, out_specs=P(None, GY, GX), check_vma=False)
```

```python
import jax
import jax.numpy as jnp
from jax import lax
from jax.experimental import pallas as pl
from jax.experimental.pallas import tpu as pltpu
from jax.sharding import Mesh
from jax.sharding import PartitionSpec as P

GX = ("yl", "x", "c")
GY = ("yh", "z")

step_size = 0.15
F32 = jnp.float32
BF16 = jnp.bfloat16
NT = (((1,), (1,)), ((), ()))
VMEM = pl.BlockSpec(memory_space=pltpu.VMEM)
OFF = 8


def near(v):
    return pltpu.with_memory_space_constraint(v, pltpu.VMEM)


def away(v):
    return pltpu.with_memory_space_constraint(v, pltpu.HBM)


def kept(shape, dtype):
    return pltpu.VMEM(shape, dtype)


FAR = pl.BlockSpec(memory_space=pltpu.HBM)


def call(kernel, out_shape, args, scalar=None, scratch=(), far=(), far_out=()):
    scalars = [] if scalar is None else [scalar]
    many = isinstance(out_shape, tuple)
    return pl.pallas_call(
        kernel,
        out_shape=out_shape,
        in_specs=[pl.BlockSpec(memory_space=pltpu.SMEM)] * len(scalars) + [FAR if i in far else VMEM for i in range(len(args))],
        out_specs=tuple(FAR if i in far_out else VMEM for i in range(len(out_shape))) if many else VMEM,
        scratch_shapes=list(scratch),
        compiler_params=pltpu.CompilerParams(vmem_limit_bytes=16 << 20),
    )(*scalars, *[away(v) if i in far else near(v) for i, v in enumerate(args)])


def face_mob(p, q):
    return 2.0 * p * q / jnp.maximum(p + q, 0.25)


def turn(x, shift, axis):
    return pltpu.roll(x, shift % x.shape[axis], axis)


def places(shape, axis):
    return lax.broadcasted_iota(jnp.int32, shape, axis)


def pack_x_kernel(core_ref, p_hbm, m_hbm, x_hbm, y_hbm, left_ref, right_ref, p_ref, m_ref, part_hbm, first_ref, last_ref, sems):
    planes, _, cx = p_ref.shape
    pairs = planes // 2
    rows = part_hbm.shape[0]
    copies = (
        (y_hbm.at[pl.ds(pl.multiple_of(core_ref[0] * rows, rows), rows)], part_hbm),
        (p_hbm, p_ref),
        (m_hbm, m_ref),
        (x_hbm.at[pl.ds(0, 16)], first_ref),
        (x_hbm.at[pl.ds(x_hbm.shape[0] - 16, 16)], last_ref),
    )
    copies = [pltpu.make_async_copy(src, dst, sems.at[i]) for i, (src, dst) in enumerate(copies)]
    for copy in copies:
        copy.start()
    for a, ref in enumerate((p_ref, m_ref)):
        copies[1 + a].wait()
        for i in range(pairs):
            t = jnp.concatenate([ref[i], ref[i + pairs]], axis=0).T
            for j in range(2):
                k = (2 * a + j) * pairs + i
                left_ref[k : k + 1, :] = t[j : j + 1]
                right_ref[k : k + 1, :] = t[cx - 2 + j : cx - 1 + j]
    base = 4 * pairs
    copies[3].wait()
    copies[4].wait()
    first = first_ref[0:1, :].astype(F32)
    last = last_ref[15:16, :].astype(F32)
    for s in range(16):
        left_ref[base + s : base + s + 1, :] = first[:, s * cx : (s + 1) * cx]
        right_ref[base + s : base + s + 1, :] = last[:, s * cx : (s + 1) * cx]
    copies[0].wait()


def strip(x, cy):
    both = jnp.concatenate([turn(x, OFF, 1), turn(x, OFF - cy, 1)], axis=0)
    lane = places(both.shape, 1)
    return jnp.where((lane >= OFF) & (lane < OFF + cy), both, 0.0)


def received(left_ref, right_ref, a, pairs, cy):
    refs = ((left_ref, 2 * a), (left_ref, 2 * a + 1), (right_ref, 2 * a), (right_ref, 2 * a + 1))
    return [strip(ref[k * pairs : (k + 1) * pairs, :], cy) for ref, k in refs]


def pack_y_kernel(p_ref, m_ref, left_ref, right_ref, up_ref, down_ref):
    planes, cy, cx = p_ref.shape
    for a, ref in enumerate((p_ref, m_ref)):
        for r in range(3):
            up_ref[3 * a + r] = ref[:, cy - 3 + r, :]
            down_ref[3 * a + r] = ref[:, r, :]
    lane = places((planes, cx), 1)
    up = jnp.zeros((planes, cx), F32)
    down = up
    for a in range(2):
        for j, s in enumerate(received(left_ref, right_ref, a, planes // 2, cy)):
            at = 3 * (4 * a + j)
            here = (lane >= at) & (lane < at + 3)
            up = jnp.where(here, turn(s, at - (OFF + cy - 3), 1), up)
            down = jnp.where(here, turn(s, at - OFF, 1), down)
    up_ref[6] = up
    down_ref[6] = down


def explicit_kernel(
    p_ref, m_ref, own_l_ref, own_r_ref, left_ref, right_ref, up_ref, down_ref,
    send_ref, fz_ref, fy_ref, fx_ref, edge_ref,
    v_ref, c_ref, f_ref, side_ref, rim_ref,
):
    planes, cy, cx = p_ref.shape
    pairs = planes // 2
    tall = cy + 2 * OFF
    lane = places((planes, cx), 1)
    plane = places((planes, cx), 0)

    def strips(a):
        out = []
        for j, s in enumerate(received(left_ref, right_ref, a, pairs, cy)):
            at = 3 * (4 * a + j)
            s = jnp.where((lane >= OFF - 3) & (lane < OFF), turn(up_ref[6], OFF - 3 - at, 1), s)
            s = jnp.where((lane >= OFF + cy) & (lane < OFF + cy + 3), turn(down_ref[6], OFF + cy - at, 1), s)
            out.append(s)
        own = []
        for ref, j, at in ((own_l_ref, 0, 0), (own_l_ref, 1, 1), (own_r_ref, 0, cx - 2), (own_r_ref, 1, cx - 1)):
            k = 2 * a + j
            s = strip(ref[k * pairs : (k + 1) * pairs, :], cy)
            for r in (1, 2):
                s = jnp.where(lane == OFF - 3 + r, turn(up_ref[3 * a + r], OFF - 3 + r - at, 1), s)
            for r in (0, 1):
                s = jnp.where(lane == OFF + cy + r, turn(down_ref[3 * a + r], OFF + cy + r - at, 1), s)
            own.append(s)
        return out[:2] + own[:2], own[2:] + out[2:]

    def strip_first(v, m, vl, ml, vr, mr):
        above = jnp.where(plane == planes - 1, 0.0, turn(m, -1, 0))
        fz = face_mob(m, above)
        gz = fz * (turn(v, -1, 0) - v)
        fy = face_mob(m, turn(m, -1, 1))
        gy = fy * (turn(v, -1, 1) - v)
        lap = gz - jnp.where(plane == 0, 0.0, turn(gz, 1, 0)) + gy - turn(gy, 1, 1)
        lap = lap + face_mob(m, mr) * (vr - v) + face_mob(m, ml) * (vl - v)
        return v + step_size * lap

    columns = []
    for side, (v, m) in enumerate(zip(strips(0), strips(1), strict=True)):
        f = face_mob(m[1], m[2])
        a = strip_first(v[1], m[1], v[0], m[0], v[2], m[2])
        b = strip_first(v[2], m[2], v[1], m[1], v[3], m[3])
        columns += [f * (v[2] - v[1]), f * (b - a)]
        side_ref[...] = f
        even = turn(side_ref[pl.ds(0, pairs, stride=2), :], -OFF, 1)
        odd = turn(side_ref[pl.ds(1, pairs, stride=2), :], cy - OFF, 1)
        edge_ref[side * pairs : (side + 1) * pairs, :] = jnp.where(lane[:pairs] < cy, even, odd)
    stacked = jnp.concatenate(columns + [jnp.zeros((cx - 4 * planes, cx), F32)], axis=0)
    across = stacked.T[:tall]

    def column(k, z):
        at = k * planes + z
        return jnp.broadcast_to(across[:, at : at + 1], (tall, cx))

    blank = jnp.zeros((OFF, cx), F32)
    for ref in (v_ref, c_ref, f_ref):
        for z in (0, planes + 1):
            ref[z * tall : (z + 1) * tall, :] = jnp.zeros((tall, cx), F32)
    for ref, a, field in ((v_ref, 0, p_ref), (c_ref, 1, m_ref)):
        for z in range(planes):
            base = (z + 1) * tall
            ref[base : base + OFF, :] = blank
            ref[base + OFF : base + OFF + cy, :] = field[z]
            ref[base + OFF + cy : base + tall, :] = blank
        for r in range(3):
            ref[pl.ds(tall + OFF - 3 + r, planes, stride=tall), :] = up_ref[3 * a + r]
            ref[pl.ds(tall + OFF + cy + r, planes, stride=tall), :] = down_ref[3 * a + r]

    wide = places((tall, cx), 1)

    def step(v, above, fz, fy, fx, gz_before, gl, gr):
        gz = fz * (above - v)
        gy = fy * (turn(v, -1, 0) - v)
        gx = jnp.where(wide == 0, gl, fx * (v - turn(v, 1, 1)))
        lap = gz - gz_before + gy - turn(gy, 1, 0)
        lap = lap + jnp.where(wide == cx - 1, gr, turn(gx, -1, 1)) - gx
        return v + step_size * lap, gz

    fz_ref[:tall, :] = jnp.zeros((tall, cx), F32)
    before = jnp.zeros((tall, cx), F32)
    for z in range(planes):
        here, above = pl.ds((z + 1) * tall, tall), pl.ds((z + 2) * tall, tall)
        flat = pl.ds(z * tall, tall)
        m = c_ref[here, :]
        fz = face_mob(m, c_ref[above, :])
        fy = face_mob(m, turn(m, -1, 0))
        fx = face_mob(m, turn(m, 1, 1))
        fz_ref[here, :] = fz
        fy_ref[flat, :] = fy
        fx_ref[flat, :] = fx
        out, before = step(v_ref[here, :], v_ref[above, :], fz, fy, fx, before, column(0, z), column(2, z))
        f_ref[here, :] = out

    rim_ref[...] = jnp.zeros(rim_ref.shape, F32)
    before = jnp.zeros((tall, cx), F32)
    quarter = planes // 4
    for z in range(planes):
        here, above = pl.ds((z + 1) * tall, tall), pl.ds((z + 2) * tall, tall)
        flat = pl.ds(z * tall, tall)
        out, before = step(
            f_ref[here, :], f_ref[above, :], fz_ref[here, :], fy_ref[flat, :], fx_ref[flat, :],
            before, column(1, z), column(3, z),
        )
        q, at = z // quarter, z % quarter
        body = out[OFF : OFF + cy].astype(BF16)
        for x in range(4):
            send_ref[(q // 2) * 8 + x * 2 + q % 2, at * cy : (at + 1) * cy, :] = body
        rim_ref[q, 2 * at : 2 * at + 1, :] = out[OFF - 1 : OFF]
        rim_ref[q, 2 * at + 1 : 2 * at + 2, :] = out[OFF + cy : OFF + cy + 1]
    for q in range(4):
        rims = rim_ref[q].astype(BF16)
        for x in range(4):
            send_ref[(q // 2) * 8 + x * 2 + q % 2, quarter * cy :, :] = rims


def solve_x_kernel(block_ref, got_ref, x0_ref, x1_ref, x2_ref, x3_ref, out_ref):
    own = block_ref[0]
    parts, lines, cx = got_ref.shape
    main = lines - 16
    a = jnp.concatenate([got_ref[s] for s in range(parts)], axis=1)
    for other, x_ref in enumerate((x0_ref, x1_ref, x2_ref, x3_ref)):
        block = own ^ other
        m = lax.dot_general(a, x_ref[:cx], NT, preferred_element_type=F32)
        out_ref[block, : main + 8] = m[: main + 8]
        e = lax.dot_general(x_ref[cx:], a[:main], NT, preferred_element_type=F32)
        out_ref[block, main + 8 : main + 12] = e[:4, :cx]
        out_ref[block, main + 12 :] = e[:4, cx:]


def implicit_kernel(back_ref, fz_ref, fy_ref, fx_ref, edge_ref, out_ref, c_ref, e_ref):
    planes, cy, cx = out_ref.shape
    tall = cy + 2 * OFF
    quarter, pairs = planes // 4, planes // 2
    main = quarter * cy

    def chemical(s):
        return s * s * s - s

    for z in (0, planes + 1):
        c_ref[z * tall : (z + 1) * tall, :] = jnp.zeros((tall, cx), F32)
    for q in range(4):
        e_ref[q * 8 : (q + 1) * 8, :] = chemical(back_ref[q, main + 8 : main + 16])
        rims = chemical(back_ref[q, main : main + 8])
        for at in range(quarter):
            base = (q * quarter + at + 1) * tall
            c_ref[base + OFF : base + OFF + cy, :] = chemical(back_ref[q, at * cy : (at + 1) * cy])
            c_ref[base + OFF - 1 : base + OFF, :] = rims[2 * at : 2 * at + 1]
            c_ref[base + OFF + cy : base + OFF + cy + 1, :] = rims[2 * at + 1 : 2 * at + 2]
    ends = [e_ref[pl.ds(j, pairs, stride=4), :] for j in range(4)]
    left = edge_ref[:pairs, :] * (ends[1] - ends[0])
    right = edge_ref[pairs:, :] * (ends[3] - ends[2])
    across = jnp.concatenate([left, right, jnp.zeros((cx - planes, cx), F32)], axis=0).T
    lane = places((cy, cx), 1)
    before = jnp.zeros((cy, cx), F32)
    for z in range(planes):
        base = (z + 1) * tall + OFF
        flat = z * tall + OFF
        c = c_ref[base : base + cy, :]
        gz = fz_ref[base : base + cy, :] * (c_ref[base + tall : base + tall + cy, :] - c)
        gy = fy_ref[flat : flat + cy, :] * (c_ref[base + 1 : base + 1 + cy, :] - c)
        gu = fy_ref[flat - 1 : flat - 1 + cy, :] * (c - c_ref[base - 1 : base - 1 + cy, :])
        rows = slice((z % 2) * cy, (z % 2 + 1) * cy)
        gl = jnp.broadcast_to(across[rows, z // 2 : z // 2 + 1], (cy, cx))
        gr = jnp.broadcast_to(across[rows, pairs + z // 2 : pairs + z // 2 + 1], (cy, cx))
        gx = jnp.where(lane == 0, gl, fx_ref[flat : flat + cy, :] * (c - turn(c, 1, 1)))
        lap = gz - before + gy - gu + jnp.where(lane == cx - 1, gr, turn(gx, -1, 1)) - gx
        s = back_ref[z // quarter, (z % quarter) * cy : (z % quarter + 1) * cy]
        out_ref[z] = (s + step_size * lap).astype(BF16)
        before = gz


def solve_y_near_kernel(side_ref, y_hbm, u_ref, sum_ref, y_ref, sem):
    high = side_ref[0]
    half, _ = u_ref.shape
    copy = pltpu.make_async_copy(y_hbm, y_ref, sem)
    copy.start()
    copy.wait()
    y0 = y_ref[:, pl.ds(pl.multiple_of(high * half, half), half)]
    sum_ref[...] = jnp.dot(y0, u_ref[...], preferred_element_type=F32)


def solve_y_far_kernel(side_ref, sum_ref, y_ref, o_ref, u0_ref, u1_ref, out_ref):
    high, core = side_ref[0], side_ref[1]
    half, cx = u0_ref.shape
    k0 = pl.ds(pl.multiple_of(high * half, half), half)
    k1 = pl.ds(pl.multiple_of((1 - high) * half, half), half)
    mine = sum_ref[...] + jnp.dot(y_ref[:, k1], u1_ref[...], preferred_element_type=F32)
    other = jnp.dot(o_ref[:, k0], u0_ref[...], preferred_element_type=F32)
    other = other + jnp.dot(o_ref[:, k1], u1_ref[...], preferred_element_type=F32)
    parts, cy, _ = out_ref.shape
    rows = cy // 2
    out_ref[:, pl.ds(pl.multiple_of(core * rows, rows), rows), :] = mine.astype(BF16).reshape(parts, rows, cx)
    out_ref[:, pl.ds(pl.multiple_of((1 - core) * rows, rows), rows), :] = other.astype(BF16).reshape(parts, rows, cx)


def pack_x(core, p, m, x_inverse, y_inverse):
    cx = p.shape[2]
    shape = (2 * p.shape[0] + 16, cx)
    cy, order = y_inverse.shape
    out = (kept(shape, F32),) * 2 + (kept(p.shape, F32),) * 2 + (jax.ShapeDtypeStruct((cy // 2, order), BF16),)
    rows = pltpu.VMEM((16, order), BF16)
    scratch = (rows, rows, pltpu.SemaphoreType.DMA((5,)))
    return call(pack_x_kernel, out, (p, m, x_inverse, y_inverse), core, scratch, range(4), (4,))


def pack_y(p, m, left, right):
    shape = (7, p.shape[0], p.shape[2])
    return call(pack_y_kernel, (kept(shape, F32),) * 2, (p, m, left, right))


def explicit(*args):
    planes, cy, cx = args[0].shape
    tall = cy + 2 * OFF
    lines = planes // 4 * cy + 16
    field = pltpu.VMEM(((planes + 2) * tall, cx), F32)
    out = (
        kept((16, lines, cx), BF16),
        kept(((planes + 1) * tall, cx), F32),
        kept((planes * tall, cx), F32),
        kept((planes * tall, cx), F32),
        kept((planes, cx), F32),
    )
    scratch = (field, field, field, pltpu.VMEM((planes, cx), F32), pltpu.VMEM((4, 16, cx), F32))
    return call(explicit_kernel, out, args, scratch=scratch)


def solve_x(block, got, x_blocks):
    _, lines, cx = got.shape
    return call(solve_x_kernel, kept((4, lines, cx), F32), (got, *x_blocks), scalar=block)


def implicit(back, faces, planes, cy):
    cx = back.shape[2]
    scratch = (pltpu.VMEM(((planes + 2) * (cy + 2 * OFF), cx), F32), pltpu.VMEM((32, cx), F32))
    return call(implicit_kernel, kept((planes, cy, cx), BF16), (back, *faces), scratch=scratch)


def solve_y_near(side, y, u):
    out = (kept((y.shape[0], u.shape[1]), F32), kept(y.shape, BF16))
    return call(solve_y_near_kernel, out, (y, u), side, (pltpu.SemaphoreType.DMA(()),), (0,))


def solve_y_far(side, *parts):
    half, cx = parts[-1].shape
    return call(solve_y_far_kernel, kept((16, half // 16, cx), BF16), parts, side)


def both_ways(to_before, to_after, axis):
    size = lax.axis_size(axis)
    up = [(i, i + 1) for i in range(size - 1)]
    return lax.ppermute(to_after, axis, up), lax.ppermute(to_before, axis, [(j, i) for i, j in up])


def local(phase_field, mobility, x_inverse, y_inverse):
    planes, cy, cx = phase_field.shape
    order = y_inverse.shape[1]
    half = order // 2
    core, low, high = lax.axis_index("c"), lax.axis_index("yl"), lax.axis_index("yh")
    swap = [(0, 1), (1, 0)]

    one = lambda v: v.reshape(1).astype(jnp.int32)

    own_l, own_r, phase_field, mobility, y_part = pack_x(one(core), phase_field, mobility, x_inverse, y_inverse)
    y_mine = lax.all_gather(y_part, "z", axis=0, tiled=True)
    left, right = both_ways(own_l, own_r, GX)
    to_up, to_down = pack_y(phase_field, mobility, left, right)

    row_before = left[-16:].reshape(1, order).astype(BF16)
    row_after = right[-16:].reshape(1, order).astype(BF16)
    row_before, row_after, to_up = lax.optimization_barrier((row_before, row_after, to_up))
    ends = [x_inverse, row_before, x_inverse[:1], x_inverse[-1:], row_after, jnp.zeros((12, order), BF16)]
    up, down = both_ways(to_down, to_up, GY)
    rows = jnp.concatenate(ends, axis=0)
    rows_yl = lax.ppermute(rows, "yl", swap)
    x_blocks = (rows, lax.ppermute(rows, "c", swap), rows_yl, lax.ppermute(rows_yl, "c", swap))

    send, *faces = explicit(phase_field, mobility, own_l, own_r, left, right, up, down)
    got = lax.all_to_all(send, GX, 0, 0, tiled=True)
    back = solve_x(one(low * 2 + core), got, x_blocks)
    back = lax.all_to_all(back, ("yl", "c"), 0, 0, tiled=True)
    updated = implicit(back, faces, planes, cy)

    mine = lax.all_to_all(updated, "z", 0, 0, tiled=True).reshape(half, cx)
    y_mine, mine = lax.optimization_barrier((y_mine, mine))
    theirs = lax.ppermute(mine, "yh", swap)
    side = jnp.concatenate([one(high), one(core)])
    part, y_mine = solve_y_near(side, y_mine, mine)
    y_other = lax.ppermute(y_mine, "c", swap)
    out = solve_y_far(side, part, y_mine, y_other, mine, theirs)
    out = lax.all_to_all(out, "z", 0, 0, tiled=True)
    return out.astype(F32)


def solution(mesh):
    shape = (2, mesh.shape["gx"] // 4, 2, 2, mesh.shape["gy"] // 2)
    torus = Mesh(mesh.devices.reshape(shape), ("yl", "x", "c", "yh", "z"))
    in_specs = (P(None, GY, GX), P(None, GY, GX), P(GX, None), P(GY, None))
    return jax.shard_map(local, mesh=torus, in_specs=in_specs, out_specs=P(None, GY, GX), check_vma=False)
```

```python
import jax
import jax.numpy as jnp
from jax import lax
from jax.experimental import pallas as pl
from jax.experimental.pallas import tpu as pltpu
from jax.sharding import Mesh
from jax.sharding import PartitionSpec as P

GX = ("yl", "x", "c")
GY = ("yh", "z")

step_size = 0.15
F32 = jnp.float32
BF16 = jnp.bfloat16
NT = (((1,), (1,)), ((), ()))
VMEM = pl.BlockSpec(memory_space=pltpu.VMEM)
OFF = 8


def near(v):
    return pltpu.with_memory_space_constraint(v, pltpu.VMEM)


def away(v):
    return pltpu.with_memory_space_constraint(v, pltpu.HBM)


def kept(shape, dtype):
    return pltpu.VMEM(shape, dtype)


FAR = pl.BlockSpec(memory_space=pltpu.HBM)


def call(kernel, out_shape, args, scalar=None, scratch=(), far=(), far_out=()):
    scalars = [] if scalar is None else [scalar]
    many = isinstance(out_shape, tuple)
    return pl.pallas_call(
        kernel,
        out_shape=out_shape,
        in_specs=[pl.BlockSpec(memory_space=pltpu.SMEM)] * len(scalars) + [FAR if i in far else VMEM for i in range(len(args))],
        out_specs=tuple(FAR if i in far_out else VMEM for i in range(len(out_shape))) if many else VMEM,
        scratch_shapes=list(scratch),
        compiler_params=pltpu.CompilerParams(vmem_limit_bytes=16 << 20),
    )(*scalars, *[away(v) if i in far else near(v) for i, v in enumerate(args)])


def face_mob(p, q):
    return 2.0 * p * q / jnp.maximum(p + q, 0.25)


def turn(x, shift, axis):
    return pltpu.roll(x, shift % x.shape[axis], axis)


def places(shape, axis):
    return lax.broadcasted_iota(jnp.int32, shape, axis)


def pack_x_kernel(part_ref, p_hbm, m_hbm, x_hbm, y_hbm, left_ref, right_ref, p_ref, m_ref, y_ref, first_ref, last_ref, sems):
    planes, _, cx = p_ref.shape
    pairs = planes // 2
    copies = (
        (y_hbm.at[:, pl.ds(pl.multiple_of(part_ref[0] * cx, cx), cx)], y_ref),
        (p_hbm, p_ref),
        (m_hbm, m_ref),
        (x_hbm.at[pl.ds(0, 16)], first_ref),
        (x_hbm.at[pl.ds(x_hbm.shape[0] - 16, 16)], last_ref),
    )
    copies = [pltpu.make_async_copy(src, dst, sems.at[i]) for i, (src, dst) in enumerate(copies)]
    for copy in copies:
        copy.start()
    for a, ref in enumerate((p_ref, m_ref)):
        copies[1 + a].wait()
        for i in range(pairs):
            t = jnp.concatenate([ref[i], ref[i + pairs]], axis=0).T
            for j in range(2):
                k = (2 * a + j) * pairs + i
                left_ref[k : k + 1, :] = t[j : j + 1]
                right_ref[k : k + 1, :] = t[cx - 2 + j : cx - 1 + j]
    base = 4 * pairs
    copies[3].wait()
    copies[4].wait()
    first = first_ref[0:1, :].astype(F32)
    last = last_ref[15:16, :].astype(F32)
    for s in range(16):
        left_ref[base + s : base + s + 1, :] = first[:, s * cx : (s + 1) * cx]
        right_ref[base + s : base + s + 1, :] = last[:, s * cx : (s + 1) * cx]
    copies[0].wait()


def strip(x, cy):
    both = jnp.concatenate([turn(x, OFF, 1), turn(x, OFF - cy, 1)], axis=0)
    lane = places(both.shape, 1)
    return jnp.where((lane >= OFF) & (lane < OFF + cy), both, 0.0)


def received(left_ref, right_ref, a, pairs, cy):
    refs = ((left_ref, 2 * a), (left_ref, 2 * a + 1), (right_ref, 2 * a), (right_ref, 2 * a + 1))
    return [strip(ref[k * pairs : (k + 1) * pairs, :], cy) for ref, k in refs]


def pack_y_kernel(p_ref, m_ref, left_ref, right_ref, up_ref, down_ref):
    planes, cy, cx = p_ref.shape
    for a, ref in enumerate((p_ref, m_ref)):
        for r in range(3):
            up_ref[3 * a + r] = ref[:, cy - 3 + r, :]
            down_ref[3 * a + r] = ref[:, r, :]
    lane = places((planes, cx), 1)
    up = jnp.zeros((planes, cx), F32)
    down = up
    for a in range(2):
        for j, s in enumerate(received(left_ref, right_ref, a, planes // 2, cy)):
            at = 3 * (4 * a + j)
            here = (lane >= at) & (lane < at + 3)
            up = jnp.where(here, turn(s, at - (OFF + cy - 3), 1), up)
            down = jnp.where(here, turn(s, at - OFF, 1), down)
    up_ref[6] = up
    down_ref[6] = down


def explicit_kernel(
    p_ref, m_ref, own_l_ref, own_r_ref, left_ref, right_ref, up_ref, down_ref,
    send_ref, fz_ref, fy_ref, fx_ref, edge_ref,
    v_ref, c_ref, f_ref, side_ref, rim_ref,
):
    planes, cy, cx = p_ref.shape
    pairs = planes // 2
    tall = cy + 2 * OFF
    lane = places((planes, cx), 1)
    plane = places((planes, cx), 0)

    def strips(a):
        out = []
        for j, s in enumerate(received(left_ref, right_ref, a, pairs, cy)):
            at = 3 * (4 * a + j)
            s = jnp.where((lane >= OFF - 3) & (lane < OFF), turn(up_ref[6], OFF - 3 - at, 1), s)
            s = jnp.where((lane >= OFF + cy) & (lane < OFF + cy + 3), turn(down_ref[6], OFF + cy - at, 1), s)
            out.append(s)
        own = []
        for ref, j, at in ((own_l_ref, 0, 0), (own_l_ref, 1, 1), (own_r_ref, 0, cx - 2), (own_r_ref, 1, cx - 1)):
            k = 2 * a + j
            s = strip(ref[k * pairs : (k + 1) * pairs, :], cy)
            for r in (1, 2):
                s = jnp.where(lane == OFF - 3 + r, turn(up_ref[3 * a + r], OFF - 3 + r - at, 1), s)
            for r in (0, 1):
                s = jnp.where(lane == OFF + cy + r, turn(down_ref[3 * a + r], OFF + cy + r - at, 1), s)
            own.append(s)
        return out[:2] + own[:2], own[2:] + out[2:]

    def strip_first(v, m, vl, ml, vr, mr):
        above = jnp.where(plane == planes - 1, 0.0, turn(m, -1, 0))
        fz = face_mob(m, above)
        gz = fz * (turn(v, -1, 0) - v)
        fy = face_mob(m, turn(m, -1, 1))
        gy = fy * (turn(v, -1, 1) - v)
        lap = gz - jnp.where(plane == 0, 0.0, turn(gz, 1, 0)) + gy - turn(gy, 1, 1)
        lap = lap + face_mob(m, mr) * (vr - v) + face_mob(m, ml) * (vl - v)
        return v + step_size * lap

    columns = []
    for side, (v, m) in enumerate(zip(strips(0), strips(1), strict=True)):
        f = face_mob(m[1], m[2])
        a = strip_first(v[1], m[1], v[0], m[0], v[2], m[2])
        b = strip_first(v[2], m[2], v[1], m[1], v[3], m[3])
        columns += [f * (v[2] - v[1]), f * (b - a)]
        side_ref[...] = f
        even = turn(side_ref[pl.ds(0, pairs, stride=2), :], -OFF, 1)
        odd = turn(side_ref[pl.ds(1, pairs, stride=2), :], cy - OFF, 1)
        edge_ref[side * pairs : (side + 1) * pairs, :] = jnp.where(lane[:pairs] < cy, even, odd)
    stacked = jnp.concatenate(columns + [jnp.zeros((cx - 4 * planes, cx), F32)], axis=0)
    across = stacked.T[:tall]

    def column(k, z):
        at = k * planes + z
        return jnp.broadcast_to(across[:, at : at + 1], (tall, cx))

    blank = jnp.zeros((OFF, cx), F32)
    for ref in (v_ref, c_ref, f_ref):
        for z in (0, planes + 1):
            ref[z * tall : (z + 1) * tall, :] = jnp.zeros((tall, cx), F32)
    for ref, a, field in ((v_ref, 0, p_ref), (c_ref, 1, m_ref)):
        for z in range(planes):
            base = (z + 1) * tall
            ref[base : base + OFF, :] = blank
            ref[base + OFF : base + OFF + cy, :] = field[z]
            ref[base + OFF + cy : base + tall, :] = blank
        for r in range(3):
            ref[pl.ds(tall + OFF - 3 + r, planes, stride=tall), :] = up_ref[3 * a + r]
            ref[pl.ds(tall + OFF + cy + r, planes, stride=tall), :] = down_ref[3 * a + r]

    wide = places((tall, cx), 1)

    def step(v, above, fz, fy, fx, gz_before, gl, gr):
        gz = fz * (above - v)
        gy = fy * (turn(v, -1, 0) - v)
        gx = jnp.where(wide == 0, gl, fx * (v - turn(v, 1, 1)))
        lap = gz - gz_before + gy - turn(gy, 1, 0)
        lap = lap + jnp.where(wide == cx - 1, gr, turn(gx, -1, 1)) - gx
        return v + step_size * lap, gz

    fz_ref[:tall, :] = jnp.zeros((tall, cx), F32)
    before = jnp.zeros((tall, cx), F32)
    for z in range(planes):
        here, above = pl.ds((z + 1) * tall, tall), pl.ds((z + 2) * tall, tall)
        flat = pl.ds(z * tall, tall)
        m = c_ref[here, :]
        fz = face_mob(m, c_ref[above, :])
        fy = face_mob(m, turn(m, -1, 0))
        fx = face_mob(m, turn(m, 1, 1))
        fz_ref[here, :] = fz
        fy_ref[flat, :] = fy
        fx_ref[flat, :] = fx
        out, before = step(v_ref[here, :], v_ref[above, :], fz, fy, fx, before, column(0, z), column(2, z))
        f_ref[here, :] = out

    rim_ref[...] = jnp.zeros(rim_ref.shape, F32)
    before = jnp.zeros((tall, cx), F32)
    quarter = planes // 4
    for z in range(planes):
        here, above = pl.ds((z + 1) * tall, tall), pl.ds((z + 2) * tall, tall)
        flat = pl.ds(z * tall, tall)
        out, before = step(
            f_ref[here, :], f_ref[above, :], fz_ref[here, :], fy_ref[flat, :], fx_ref[flat, :],
            before, column(1, z), column(3, z),
        )
        q, at = z // quarter, z % quarter
        body = out[OFF : OFF + cy].astype(BF16)
        for x in range(4):
            send_ref[(q // 2) * 8 + x * 2 + q % 2, at * cy : (at + 1) * cy, :] = body
        rim_ref[q, 2 * at : 2 * at + 1, :] = out[OFF - 1 : OFF]
        rim_ref[q, 2 * at + 1 : 2 * at + 2, :] = out[OFF + cy : OFF + cy + 1]
    for q in range(4):
        rims = rim_ref[q].astype(BF16)
        for x in range(4):
            send_ref[(q // 2) * 8 + x * 2 + q % 2, quarter * cy :, :] = rims


def solve_x_kernel(block_ref, got_ref, x0_ref, x1_ref, x2_ref, x3_ref, out_ref):
    own = block_ref[0]
    parts, lines, cx = got_ref.shape
    main = lines - 16
    a = jnp.concatenate([got_ref[s] for s in range(parts)], axis=1)
    for other, x_ref in enumerate((x0_ref, x1_ref, x2_ref, x3_ref)):
        block = own ^ other
        m = lax.dot_general(a, x_ref[:cx], NT, preferred_element_type=F32)
        out_ref[block, : main + 8] = m[: main + 8]
        e = lax.dot_general(x_ref[cx:], a[:main], NT, preferred_element_type=F32)
        out_ref[block, main + 8 : main + 12] = e[:4, :cx]
        out_ref[block, main + 12 :] = e[:4, cx:]


def implicit_kernel(back_ref, fz_ref, fy_ref, fx_ref, edge_ref, out_ref, c_ref, e_ref):
    planes, cy, cx = out_ref.shape
    tall = cy + 2 * OFF
    quarter, pairs = planes // 4, planes // 2
    main = quarter * cy

    def chemical(s):
        return s * s * s - s

    for z in (0, planes + 1):
        c_ref[z * tall : (z + 1) * tall, :] = jnp.zeros((tall, cx), F32)
    for q in range(4):
        e_ref[q * 8 : (q + 1) * 8, :] = chemical(back_ref[q, main + 8 : main + 16])
        rims = chemical(back_ref[q, main : main + 8])
        for at in range(quarter):
            base = (q * quarter + at + 1) * tall
            c_ref[base + OFF : base + OFF + cy, :] = chemical(back_ref[q, at * cy : (at + 1) * cy])
            c_ref[base + OFF - 1 : base + OFF, :] = rims[2 * at : 2 * at + 1]
            c_ref[base + OFF + cy : base + OFF + cy + 1, :] = rims[2 * at + 1 : 2 * at + 2]
    ends = [e_ref[pl.ds(j, pairs, stride=4), :] for j in range(4)]
    left = edge_ref[:pairs, :] * (ends[1] - ends[0])
    right = edge_ref[pairs:, :] * (ends[3] - ends[2])
    across = jnp.concatenate([left, right, jnp.zeros((cx - planes, cx), F32)], axis=0).T
    lane = places((cy, cx), 1)
    before = jnp.zeros((cy, cx), F32)
    for z in range(planes):
        base = (z + 1) * tall + OFF
        flat = z * tall + OFF
        c = c_ref[base : base + cy, :]
        gz = fz_ref[base : base + cy, :] * (c_ref[base + tall : base + tall + cy, :] - c)
        gy = fy_ref[flat : flat + cy, :] * (c_ref[base + 1 : base + 1 + cy, :] - c)
        gu = fy_ref[flat - 1 : flat - 1 + cy, :] * (c - c_ref[base - 1 : base - 1 + cy, :])
        rows = slice((z % 2) * cy, (z % 2 + 1) * cy)
        gl = jnp.broadcast_to(across[rows, z // 2 : z // 2 + 1], (cy, cx))
        gr = jnp.broadcast_to(across[rows, pairs + z // 2 : pairs + z // 2 + 1], (cy, cx))
        gx = jnp.where(lane == 0, gl, fx_ref[flat : flat + cy, :] * (c - turn(c, 1, 1)))
        lap = gz - before + gy - gu + jnp.where(lane == cx - 1, gr, turn(gx, -1, 1)) - gx
        s = back_ref[z // quarter, (z % quarter) * cy : (z % quarter + 1) * cy]
        out_ref[z] = (s + step_size * lap).astype(BF16)
        before = gz


def solve_y_kernel(place_ref, d_ref, l_ref, r_ref, s0_ref, s1_ref, near_ref, far_ref, mine_ref, theirs_ref, out_ref, u_ref):
    high, low, x, core, z = (place_ref[i] for i in range(5))
    parts, cy, cx = out_ref.shape
    u_ref[high] = mine_ref[...]
    u_ref[1 - high] = theirs_ref[...]

    def product(turned, at, mine, other):
        half = low ^ turned
        base = (x + at) % 4 * 2
        ua = u_ref[half, pl.ds(pl.multiple_of((base + core) * cx, cx), cx)]
        ub = u_ref[half, pl.ds(pl.multiple_of((base + 1 - core) * cx, cx), cx)]
        y = jnp.concatenate([mine, other], axis=1)
        return jnp.dot(y, jnp.concatenate([ua, ub], axis=0), preferred_element_type=F32)

    total = product(0, 2, s0_ref[...], far_ref[0]) + product(1, 2, s1_ref[...], far_ref[1])
    for i, (ref, at) in enumerate(((d_ref, 0), (l_ref, 3), (r_ref, 1))):
        for turned in range(2):
            total = total + product(turned, at, ref[turned], near_ref[2 * i + turned])
    for i in range(parts):
        back = 8 * (i & 1) + 4 * (i >> 1 & 1) + 2 * (i >> 2 & 1) + (i >> 3 & 1)
        out_ref[(z + parts - back) % parts] = total[i * cy : (i + 1) * cy].astype(BF16)


def pack_x(part, p, m, x_inverse, y_inverse):
    cx = p.shape[2]
    shape = (2 * p.shape[0] + 16, cx)
    cy, order = y_inverse.shape
    out = (kept(shape, F32),) * 2 + (kept(p.shape, F32),) * 2 + (kept((cy, cx), BF16),)
    rows = pltpu.VMEM((16, order), BF16)
    scratch = (rows, rows, pltpu.SemaphoreType.DMA((5,)))
    return call(pack_x_kernel, out, (p, m, x_inverse, y_inverse), part, scratch, range(4))


def pack_y(p, m, left, right):
    shape = (7, p.shape[0], p.shape[2])
    return call(pack_y_kernel, (kept(shape, F32),) * 2, (p, m, left, right))


def explicit(*args):
    planes, cy, cx = args[0].shape
    tall = cy + 2 * OFF
    lines = planes // 4 * cy + 16
    field = pltpu.VMEM(((planes + 2) * tall, cx), F32)
    out = (
        kept((16, lines, cx), BF16),
        kept(((planes + 1) * tall, cx), F32),
        kept((planes * tall, cx), F32),
        kept((planes * tall, cx), F32),
        kept((planes, cx), F32),
    )
    scratch = (field, field, field, pltpu.VMEM((planes, cx), F32), pltpu.VMEM((4, 16, cx), F32))
    return call(explicit_kernel, out, args, scratch=scratch)


def solve_x(block, got, x_blocks):
    _, lines, cx = got.shape
    return call(solve_x_kernel, kept((4, lines, cx), F32), (got, *x_blocks), scalar=block)


def implicit(back, faces, planes, cy):
    cx = back.shape[2]
    scratch = (pltpu.VMEM(((planes + 2) * (cy + 2 * OFF), cx), F32), pltpu.VMEM((32, cx), F32))
    return call(implicit_kernel, kept((planes, cy, cx), BF16), (back, *faces), scratch=scratch)


def solve_y(place, *parts):
    half, cx = parts[-1].shape
    scratch = (pltpu.VMEM((2, half, cx), BF16),)
    return call(solve_y_kernel, kept((16, half // 16, cx), BF16), parts, place, scratch)


def both_ways(to_before, to_after, axis):
    size = lax.axis_size(axis)
    up = [(i, i + 1) for i in range(size - 1)]
    return lax.ppermute(to_after, axis, up), lax.ppermute(to_before, axis, [(j, i) for i, j in up])


def moved(v, axis, distance):
    size = lax.axis_size(axis)
    return lax.ppermute(v, axis, [(i, (i + distance) % size) for i in range(size)])


def exchanged(v, axes):
    return lax.all_to_all(v, axes, 0, 0, tiled=True)


def local(phase_field, mobility, x_inverse, y_inverse):
    planes, cy, cx = phase_field.shape
    order = y_inverse.shape[1]
    half = order // 2
    high, low, x, core, z = (lax.axis_index(a) for a in ("yh", "yl", "x", "c", "z"))
    place = jnp.stack((high, low, x, core, z)).astype(jnp.int32)
    one = lambda v: v.reshape(1).astype(jnp.int32)

    own_l, own_r, phase_field, mobility, part = pack_x(
        one(low * 8 + x * 2 + core), phase_field, mobility, x_inverse, y_inverse
    )
    left, right = both_ways(own_l, own_r, GX)
    to_up, to_down = pack_y(phase_field, mobility, left, right)
    row_before = left[-16:].reshape(1, order).astype(BF16)
    row_after = right[-16:].reshape(1, order).astype(BF16)
    row_before, row_after, to_up = lax.optimization_barrier((row_before, row_after, to_up))
    up, down = both_ways(to_down, to_up, GY)

    ends = [x_inverse, row_before, x_inverse[:1], x_inverse[-1:], row_after, jnp.zeros((12, order), BF16)]
    rows = jnp.concatenate(ends, axis=0)
    rows_yl = moved(rows, "yl", 1)
    x_blocks = (rows, moved(rows, "c", 1), rows_yl, moved(rows_yl, "c", 1))

    ys = part[None]
    for d in (8, 4, 2, 1):
        ys = jnp.concatenate([ys, moved(ys, "z", d)], axis=0)
    ys = ys.reshape(1, half, cx)
    ys = jnp.concatenate([ys, moved(ys, "yl", 1)], axis=0)
    y_left = moved(ys, "x", 1)
    y_right = moved(ys, "x", -1)
    y_near = moved(jnp.concatenate([ys, y_left, y_right], axis=0), "c", 1)
    y_s0 = moved(y_left[0], "x", 1)
    y_s1 = moved(y_right[1], "x", -1)
    y_far = moved(jnp.stack((y_s0, y_s1)), "c", 1)

    send, *faces = explicit(phase_field, mobility, own_l, own_r, left, right, up, down)
    got = exchanged(send, GX)
    back = solve_x(one(low * 2 + core), got, x_blocks)
    back = exchanged(back, ("yl", "c"))
    updated = implicit(back, faces, planes, cy)
    mine = exchanged(updated, "z").reshape(half, cx)
    theirs = moved(mine, "yh", 1)
    out = solve_y(place, ys, y_left, y_right, y_s0, y_s1, y_near, y_far, mine, theirs)
    return exchanged(out, "z").astype(F32)


def solution(mesh):
    shape = (2, mesh.shape["gx"] // 4, 2, 2, mesh.shape["gy"] // 2)
    torus = Mesh(mesh.devices.reshape(shape), ("yl", "x", "c", "yh", "z"))
    in_specs = (P(None, GY, GX), P(None, GY, GX), P(GX, None), P(GY, None))
    return jax.shard_map(local, mesh=torus, in_specs=in_specs, out_specs=P(None, GY, GX), check_vma=False)
```

```python
import jax
import jax.numpy as jnp
from jax import lax
from jax.experimental import pallas as pl
from jax.experimental.pallas import tpu as pltpu
from jax.sharding import Mesh
from jax.sharding import PartitionSpec as P

GX = ("yl", "x", "c")
GY = ("yh", "z")

step_size = 0.15
F32 = jnp.float32
BF16 = jnp.bfloat16
NT = (((1,), (1,)), ((), ()))
VMEM = pl.BlockSpec(memory_space=pltpu.VMEM)
OFF = 8


def near(v):
    return pltpu.with_memory_space_constraint(v, pltpu.VMEM)


def away(v):
    return pltpu.with_memory_space_constraint(v, pltpu.HBM)


def kept(shape, dtype):
    return pltpu.VMEM(shape, dtype)


FAR = pl.BlockSpec(memory_space=pltpu.HBM)


def call(kernel, out_shape, args, scalar=None, scratch=(), far=(), far_out=()):
    scalars = [] if scalar is None else [scalar]
    many = isinstance(out_shape, tuple)
    return pl.pallas_call(
        kernel,
        out_shape=out_shape,
        in_specs=[pl.BlockSpec(memory_space=pltpu.SMEM)] * len(scalars) + [FAR if i in far else VMEM for i in range(len(args))],
        out_specs=tuple(FAR if i in far_out else VMEM for i in range(len(out_shape))) if many else VMEM,
        scratch_shapes=list(scratch),
        compiler_params=pltpu.CompilerParams(vmem_limit_bytes=16 << 20),
    )(*scalars, *[away(v) if i in far else near(v) for i, v in enumerate(args)])


def face_mob(p, q):
    return 2.0 * p * q / jnp.maximum(p + q, 0.25)


def turn(x, shift, axis):
    return pltpu.roll(x, shift % x.shape[axis], axis)


def places(shape, axis):
    return lax.broadcasted_iota(jnp.int32, shape, axis)


def pack_x_kernel(core_ref, p_hbm, m_hbm, x_hbm, y_hbm, left_ref, right_ref, p_ref, m_ref, part_hbm, first_ref, last_ref, part_ref, sems):
    planes, _, cx = p_ref.shape
    pairs = planes // 2
    rows = part_hbm.shape[0]
    copies = (
        (y_hbm.at[pl.ds(pl.multiple_of(core_ref[0] * rows, rows), rows)], part_ref),
        (p_hbm, p_ref),
        (m_hbm, m_ref),
        (x_hbm.at[pl.ds(0, 16)], first_ref),
        (x_hbm.at[pl.ds(x_hbm.shape[0] - 16, 16)], last_ref),
    )
    copies = [pltpu.make_async_copy(src, dst, sems.at[i]) for i, (src, dst) in enumerate(copies)]
    for copy in copies:
        copy.start()
    copies[0].wait()
    out = pltpu.make_async_copy(part_ref, part_hbm, sems.at[0])
    out.start()
    for a, ref in enumerate((p_ref, m_ref)):
        copies[1 + a].wait()
        for i in range(pairs):
            t = jnp.concatenate([ref[i], ref[i + pairs]], axis=0).T
            for j in range(2):
                k = (2 * a + j) * pairs + i
                left_ref[k : k + 1, :] = t[j : j + 1]
                right_ref[k : k + 1, :] = t[cx - 2 + j : cx - 1 + j]
    base = 4 * pairs
    copies[3].wait()
    copies[4].wait()
    first = first_ref[0:1, :].astype(F32)
    last = last_ref[15:16, :].astype(F32)
    for s in range(16):
        left_ref[base + s : base + s + 1, :] = first[:, s * cx : (s + 1) * cx]
        right_ref[base + s : base + s + 1, :] = last[:, s * cx : (s + 1) * cx]
    out.wait()


def strip(x, cy):
    both = jnp.concatenate([turn(x, OFF, 1), turn(x, OFF - cy, 1)], axis=0)
    lane = places(both.shape, 1)
    return jnp.where((lane >= OFF) & (lane < OFF + cy), both, 0.0)


def received(left_ref, right_ref, a, pairs, cy):
    refs = ((left_ref, 2 * a), (left_ref, 2 * a + 1), (right_ref, 2 * a), (right_ref, 2 * a + 1))
    return [strip(ref[k * pairs : (k + 1) * pairs, :], cy) for ref, k in refs]


def pack_y_kernel(p_ref, m_ref, left_ref, right_ref, up_ref, down_ref):
    planes, cy, cx = p_ref.shape
    for a, ref in enumerate((p_ref, m_ref)):
        for r in range(3):
            up_ref[3 * a + r] = ref[:, cy - 3 + r, :]
            down_ref[3 * a + r] = ref[:, r, :]
    lane = places((planes, cx), 1)
    up = jnp.zeros((planes, cx), F32)
    down = up
    for a in range(2):
        for j, s in enumerate(received(left_ref, right_ref, a, planes // 2, cy)):
            at = 3 * (4 * a + j)
            here = (lane >= at) & (lane < at + 3)
            up = jnp.where(here, turn(s, at - (OFF + cy - 3), 1), up)
            down = jnp.where(here, turn(s, at - OFF, 1), down)
    up_ref[6] = up
    down_ref[6] = down


def explicit_kernel(
    p_ref, m_ref, own_l_ref, own_r_ref, left_ref, right_ref, up_ref, down_ref,
    send_ref, fz_ref, fy_ref, fx_ref, edge_ref,
    v_ref, c_ref, f_ref, side_ref, rim_ref,
):
    planes, cy, cx = p_ref.shape
    pairs = planes // 2
    tall = cy + 2 * OFF
    lane = places((planes, cx), 1)
    plane = places((planes, cx), 0)

    def strips(a):
        out = []
        for j, s in enumerate(received(left_ref, right_ref, a, pairs, cy)):
            at = 3 * (4 * a + j)
            s = jnp.where((lane >= OFF - 3) & (lane < OFF), turn(up_ref[6], OFF - 3 - at, 1), s)
            s = jnp.where((lane >= OFF + cy) & (lane < OFF + cy + 3), turn(down_ref[6], OFF + cy - at, 1), s)
            out.append(s)
        own = []
        for ref, j, at in ((own_l_ref, 0, 0), (own_l_ref, 1, 1), (own_r_ref, 0, cx - 2), (own_r_ref, 1, cx - 1)):
            k = 2 * a + j
            s = strip(ref[k * pairs : (k + 1) * pairs, :], cy)
            for r in (1, 2):
                s = jnp.where(lane == OFF - 3 + r, turn(up_ref[3 * a + r], OFF - 3 + r - at, 1), s)
            for r in (0, 1):
                s = jnp.where(lane == OFF + cy + r, turn(down_ref[3 * a + r], OFF + cy + r - at, 1), s)
            own.append(s)
        return out[:2] + own[:2], own[2:] + out[2:]

    def strip_first(v, m, vl, ml, vr, mr):
        above = jnp.where(plane == planes - 1, 0.0, turn(m, -1, 0))
        fz = face_mob(m, above)
        gz = fz * (turn(v, -1, 0) - v)
        fy = face_mob(m, turn(m, -1, 1))
        gy = fy * (turn(v, -1, 1) - v)
        lap = gz - jnp.where(plane == 0, 0.0, turn(gz, 1, 0)) + gy - turn(gy, 1, 1)
        lap = lap + face_mob(m, mr) * (vr - v) + face_mob(m, ml) * (vl - v)
        return v + step_size * lap

    columns = []
    for side, (v, m) in enumerate(zip(strips(0), strips(1), strict=True)):
        f = face_mob(m[1], m[2])
        a = strip_first(v[1], m[1], v[0], m[0], v[2], m[2])
        b = strip_first(v[2], m[2], v[1], m[1], v[3], m[3])
        columns += [f * (v[2] - v[1]), f * (b - a)]
        side_ref[...] = f
        even = turn(side_ref[pl.ds(0, pairs, stride=2), :], -OFF, 1)
        odd = turn(side_ref[pl.ds(1, pairs, stride=2), :], cy - OFF, 1)
        edge_ref[side * pairs : (side + 1) * pairs, :] = jnp.where(lane[:pairs] < cy, even, odd)
    stacked = jnp.concatenate(columns + [jnp.zeros((cx - 4 * planes, cx), F32)], axis=0)
    across = stacked.T[:tall]

    def column(k, z):
        at = k * planes + z
        return jnp.broadcast_to(across[:, at : at + 1], (tall, cx))

    blank = jnp.zeros((OFF, cx), F32)
    for ref in (v_ref, c_ref, f_ref):
        for z in (0, planes + 1):
            ref[z * tall : (z + 1) * tall, :] = jnp.zeros((tall, cx), F32)
    for ref, a, field in ((v_ref, 0, p_ref), (c_ref, 1, m_ref)):
        for z in range(planes):
            base = (z + 1) * tall
            ref[base : base + OFF, :] = blank
            ref[base + OFF : base + OFF + cy, :] = field[z]
            ref[base + OFF + cy : base + tall, :] = blank
        for r in range(3):
            ref[pl.ds(tall + OFF - 3 + r, planes, stride=tall), :] = up_ref[3 * a + r]
            ref[pl.ds(tall + OFF + cy + r, planes, stride=tall), :] = down_ref[3 * a + r]

    wide = places((tall, cx), 1)

    def step(v, above, fz, fy, fx, gz_before, gl, gr):
        gz = fz * (above - v)
        gy = fy * (turn(v, -1, 0) - v)
        gx = jnp.where(wide == 0, gl, fx * (v - turn(v, 1, 1)))
        lap = gz - gz_before + gy - turn(gy, 1, 0)
        lap = lap + jnp.where(wide == cx - 1, gr, turn(gx, -1, 1)) - gx
        return v + step_size * lap, gz

    fz_ref[:tall, :] = jnp.zeros((tall, cx), F32)
    before = jnp.zeros((tall, cx), F32)
    for z in range(planes):
        here, above = pl.ds((z + 1) * tall, tall), pl.ds((z + 2) * tall, tall)
        flat = pl.ds(z * tall, tall)
        m = c_ref[here, :]
        fz = face_mob(m, c_ref[above, :])
        fy = face_mob(m, turn(m, -1, 0))
        fx = face_mob(m, turn(m, 1, 1))
        fz_ref[here, :] = fz
        fy_ref[flat, :] = fy
        fx_ref[flat, :] = fx
        out, before = step(v_ref[here, :], v_ref[above, :], fz, fy, fx, before, column(0, z), column(2, z))
        f_ref[here, :] = out

    rim_ref[...] = jnp.zeros(rim_ref.shape, F32)
    before = jnp.zeros((tall, cx), F32)
    quarter = planes // 4
    for z in range(planes):
        here, above = pl.ds((z + 1) * tall, tall), pl.ds((z + 2) * tall, tall)
        flat = pl.ds(z * tall, tall)
        out, before = step(
            f_ref[here, :], f_ref[above, :], fz_ref[here, :], fy_ref[flat, :], fx_ref[flat, :],
            before, column(1, z), column(3, z),
        )
        q, at = z // quarter, z % quarter
        body = out[OFF : OFF + cy].astype(BF16)
        for x in range(4):
            send_ref[(q // 2) * 8 + x * 2 + q % 2, at * cy : (at + 1) * cy, :] = body
        rim_ref[q, 2 * at : 2 * at + 1, :] = out[OFF - 1 : OFF]
        rim_ref[q, 2 * at + 1 : 2 * at + 2, :] = out[OFF + cy : OFF + cy + 1]
    for q in range(4):
        rims = rim_ref[q].astype(BF16)
        for x in range(4):
            send_ref[(q // 2) * 8 + x * 2 + q % 2, quarter * cy :, :] = rims


def solve_x_kernel(block_ref, got_ref, x0_ref, x1_ref, x2_ref, x3_ref, out_ref):
    own = block_ref[0]
    parts, lines, cx = got_ref.shape
    main = lines - 16
    a = jnp.concatenate([got_ref[s] for s in range(parts)], axis=1)
    for other, x_ref in enumerate((x0_ref, x1_ref, x2_ref, x3_ref)):
        block = own ^ other
        m = lax.dot_general(a, x_ref[:cx], NT, preferred_element_type=F32)
        out_ref[block, : main + 8] = m[: main + 8]
        e = lax.dot_general(x_ref[cx:], a[:main], NT, preferred_element_type=F32)
        out_ref[block, main + 8 : main + 12] = e[:4, :cx]
        out_ref[block, main + 12 :] = e[:4, cx:]


def implicit_kernel(back_ref, fz_ref, fy_ref, fx_ref, edge_ref, out_ref, c_ref, e_ref):
    planes, cy, cx = out_ref.shape
    tall = cy + 2 * OFF
    quarter, pairs = planes // 4, planes // 2
    main = quarter * cy

    def chemical(s):
        return s * s * s - s

    for z in (0, planes + 1):
        c_ref[z * tall : (z + 1) * tall, :] = jnp.zeros((tall, cx), F32)
    for q in range(4):
        e_ref[q * 8 : (q + 1) * 8, :] = chemical(back_ref[q, main + 8 : main + 16])
        rims = chemical(back_ref[q, main : main + 8])
        for at in range(quarter):
            base = (q * quarter + at + 1) * tall
            c_ref[base + OFF : base + OFF + cy, :] = chemical(back_ref[q, at * cy : (at + 1) * cy])
            c_ref[base + OFF - 1 : base + OFF, :] = rims[2 * at : 2 * at + 1]
            c_ref[base + OFF + cy : base + OFF + cy + 1, :] = rims[2 * at + 1 : 2 * at + 2]
    ends = [e_ref[pl.ds(j, pairs, stride=4), :] for j in range(4)]
    left = edge_ref[:pairs, :] * (ends[1] - ends[0])
    right = edge_ref[pairs:, :] * (ends[3] - ends[2])
    across = jnp.concatenate([left, right, jnp.zeros((cx - planes, cx), F32)], axis=0).T
    lane = places((cy, cx), 1)
    before = jnp.zeros((cy, cx), F32)
    for z in range(planes):
        base = (z + 1) * tall + OFF
        flat = z * tall + OFF
        c = c_ref[base : base + cy, :]
        gz = fz_ref[base : base + cy, :] * (c_ref[base + tall : base + tall + cy, :] - c)
        gy = fy_ref[flat : flat + cy, :] * (c_ref[base + 1 : base + 1 + cy, :] - c)
        gu = fy_ref[flat - 1 : flat - 1 + cy, :] * (c - c_ref[base - 1 : base - 1 + cy, :])
        rows = slice((z % 2) * cy, (z % 2 + 1) * cy)
        gl = jnp.broadcast_to(across[rows, z // 2 : z // 2 + 1], (cy, cx))
        gr = jnp.broadcast_to(across[rows, pairs + z // 2 : pairs + z // 2 + 1], (cy, cx))
        gx = jnp.where(lane == 0, gl, fx_ref[flat : flat + cy, :] * (c - turn(c, 1, 1)))
        lap = gz - before + gy - gu + jnp.where(lane == cx - 1, gr, turn(gx, -1, 1)) - gx
        s = back_ref[z // quarter, (z % quarter) * cy : (z % quarter + 1) * cy]
        out_ref[z] = (s + step_size * lap).astype(BF16)
        before = gz


def solve_y_near_kernel(side_ref, y_hbm, u_ref, sum_ref, y_ref, near_ref, sems):
    high = side_ref[0]
    half, _ = u_ref.shape
    halves = (high, 1 - high)
    columns = [y_hbm.at[:, pl.ds(pl.multiple_of(h * half, half), half)] for h in halves]
    copies = [pltpu.make_async_copy(c, ref, sems.at[i]) for i, (c, ref) in enumerate(zip(columns, (near_ref, y_ref), strict=True))]
    for copy in copies:
        copy.start()
    copies[0].wait()
    sum_ref[...] = jnp.dot(near_ref[...], u_ref[...], preferred_element_type=F32)
    copies[1].wait()


def solve_y_far_kernel(sum_ref, y_ref, u_ref, out_ref):
    total = sum_ref[...] + jnp.dot(y_ref[...], u_ref[...], preferred_element_type=F32)
    out_ref[...] = total.astype(BF16)


def pack_x(core, p, m, x_inverse, y_inverse):
    cx = p.shape[2]
    shape = (2 * p.shape[0] + 16, cx)
    cy, order = y_inverse.shape
    out = (kept(shape, F32),) * 2 + (kept(p.shape, F32),) * 2 + (jax.ShapeDtypeStruct((cy // 2, order), BF16),)
    rows = pltpu.VMEM((16, order), BF16)
    scratch = (rows, rows, pltpu.VMEM((cy // 2, order), BF16), pltpu.SemaphoreType.DMA((5,)))
    return call(pack_x_kernel, out, (p, m, x_inverse, y_inverse), core, scratch, range(4), (4,))


def pack_y(p, m, left, right):
    shape = (7, p.shape[0], p.shape[2])
    return call(pack_y_kernel, (kept(shape, F32),) * 2, (p, m, left, right))


def explicit(*args):
    planes, cy, cx = args[0].shape
    tall = cy + 2 * OFF
    lines = planes // 4 * cy + 16
    field = pltpu.VMEM(((planes + 2) * tall, cx), F32)
    out = (
        kept((16, lines, cx), BF16),
        kept(((planes + 1) * tall, cx), F32),
        kept((planes * tall, cx), F32),
        kept((planes * tall, cx), F32),
        kept((planes, cx), F32),
    )
    scratch = (field, field, field, pltpu.VMEM((planes, cx), F32), pltpu.VMEM((4, 16, cx), F32))
    return call(explicit_kernel, out, args, scratch=scratch)


def solve_x(block, got, x_blocks):
    _, lines, cx = got.shape
    return call(solve_x_kernel, kept((4, lines, cx), F32), (got, *x_blocks), scalar=block)


def implicit(back, faces, planes, cy):
    cx = back.shape[2]
    scratch = (pltpu.VMEM(((planes + 2) * (cy + 2 * OFF), cx), F32), pltpu.VMEM((32, cx), F32))
    return call(implicit_kernel, kept((planes, cy, cx), BF16), (back, *faces), scratch=scratch)


def solve_y_near(side, y, u):
    half, cx = u.shape
    out = (kept((half, cx), F32), kept((half, half), BF16))
    scratch = (pltpu.VMEM((half, half), BF16), pltpu.SemaphoreType.DMA((2,)))
    return call(solve_y_near_kernel, out, (y, u), side, scratch, (0,))


def solve_y_far(*parts):
    return call(solve_y_far_kernel, kept(parts[-1].shape, BF16), parts)


def both_ways(to_before, to_after, axis):
    size = lax.axis_size(axis)
    up = [(i, i + 1) for i in range(size - 1)]
    return lax.ppermute(to_after, axis, up), lax.ppermute(to_before, axis, [(j, i) for i, j in up])


def local(phase_field, mobility, x_inverse, y_inverse):
    planes, cy, cx = phase_field.shape
    order = y_inverse.shape[1]
    half = order // 2
    core, low, high = lax.axis_index("c"), lax.axis_index("yl"), lax.axis_index("yh")
    swap = [(0, 1), (1, 0)]

    one = lambda v: v.reshape(1).astype(jnp.int32)

    own_l, own_r, phase_field, mobility, y_part = pack_x(one(core), phase_field, mobility, x_inverse, y_inverse)
    y_rows = lax.all_gather(y_part, ("z", "c"), axis=0, tiled=True)
    left, right = both_ways(own_l, own_r, GX)
    to_up, to_down = pack_y(phase_field, mobility, left, right)

    row_before = left[-16:].reshape(1, order).astype(BF16)
    row_after = right[-16:].reshape(1, order).astype(BF16)
    row_before, row_after, to_up = lax.optimization_barrier((row_before, row_after, to_up))
    ends = [x_inverse, row_before, x_inverse[:1], x_inverse[-1:], row_after, jnp.zeros((12, order), BF16)]
    up, down = both_ways(to_down, to_up, GY)
    rows = jnp.concatenate(ends, axis=0)
    rows_yl = lax.ppermute(rows, "yl", swap)
    x_blocks = (rows, lax.ppermute(rows, "c", swap), rows_yl, lax.ppermute(rows_yl, "c", swap))

    send, *faces = explicit(phase_field, mobility, own_l, own_r, left, right, up, down)
    got = lax.all_to_all(send, GX, 0, 0, tiled=True)
    back = solve_x(one(low * 2 + core), got, x_blocks)
    back = lax.all_to_all(back, ("yl", "c"), 0, 0, tiled=True)
    updated = implicit(back, faces, planes, cy)

    mine = lax.all_to_all(updated, "z", 0, 0, tiled=True).reshape(half, cx)
    y_rows, mine = lax.optimization_barrier((y_rows, mine))
    theirs = lax.ppermute(mine, "yh", swap)
    part, y_far = solve_y_near(one(high), y_rows, mine)
    out = solve_y_far(part, y_far, theirs).reshape(16, cy, cx)
    out = lax.all_to_all(out, "z", 0, 0, tiled=True)
    return out.astype(F32)


def solution(mesh):
    shape = (2, mesh.shape["gx"] // 4, 2, 2, mesh.shape["gy"] // 2)
    torus = Mesh(mesh.devices.reshape(shape), ("yl", "x", "c", "yh", "z"))
    in_specs = (P(None, GY, GX), P(None, GY, GX), P(GX, None), P(GY, None))
    return jax.shard_map(local, mesh=torus, in_specs=in_specs, out_specs=P(None, GY, GX), check_vma=False)
```

```python
import jax
import jax.numpy as jnp
from jax import lax
from jax.experimental import pallas as pl
from jax.experimental.pallas import tpu as pltpu
from jax.sharding import Mesh
from jax.sharding import PartitionSpec as P

GX = ("yl", "x", "c")
GY = ("yh", "z")

step_size = 0.15
F32 = jnp.float32
BF16 = jnp.bfloat16
NT = (((1,), (1,)), ((), ()))
VMEM = pl.BlockSpec(memory_space=pltpu.VMEM)
OFF = 8


def near(v):
    return pltpu.with_memory_space_constraint(v, pltpu.VMEM)


def away(v):
    return pltpu.with_memory_space_constraint(v, pltpu.HBM)


def kept(shape, dtype):
    return pltpu.VMEM(shape, dtype)


FAR = pl.BlockSpec(memory_space=pltpu.HBM)


def call(kernel, out_shape, args, scalar=None, scratch=(), far=(), far_out=()):
    scalars = [] if scalar is None else [scalar]
    many = isinstance(out_shape, tuple)
    return pl.pallas_call(
        kernel,
        out_shape=out_shape,
        in_specs=[pl.BlockSpec(memory_space=pltpu.SMEM)] * len(scalars) + [FAR if i in far else VMEM for i in range(len(args))],
        out_specs=tuple(FAR if i in far_out else VMEM for i in range(len(out_shape))) if many else VMEM,
        scratch_shapes=list(scratch),
        compiler_params=pltpu.CompilerParams(vmem_limit_bytes=16 << 20),
    )(*scalars, *[away(v) if i in far else near(v) for i, v in enumerate(args)])


def face_mob(p, q):
    return 2.0 * p * q / jnp.maximum(p + q, 0.25)


def turn(x, shift, axis):
    return pltpu.roll(x, shift % x.shape[axis], axis)


def places(shape, axis):
    return lax.broadcasted_iota(jnp.int32, shape, axis)


def pack_x_kernel(core_ref, p_hbm, m_hbm, x_hbm, y_hbm, left_ref, right_ref, p_ref, m_ref, x_ref, part_hbm, part_ref, sems):
    planes, _, cx = p_ref.shape
    pairs = planes // 2
    rows = part_hbm.shape[0]
    copies = (
        (y_hbm.at[pl.ds(pl.multiple_of(core_ref[0] * rows, rows), rows)], part_ref),
        (p_hbm, p_ref),
        (m_hbm, m_ref),
        (x_hbm, x_ref),
    )
    copies = [pltpu.make_async_copy(src, dst, sems.at[i]) for i, (src, dst) in enumerate(copies)]
    for copy in copies:
        copy.start()
    copies[0].wait()
    out = pltpu.make_async_copy(part_ref, part_hbm, sems.at[0])
    out.start()
    for a, ref in enumerate((p_ref, m_ref)):
        copies[1 + a].wait()
        for i in range(pairs):
            t = jnp.concatenate([ref[i], ref[i + pairs]], axis=0).T
            for j in range(2):
                k = (2 * a + j) * pairs + i
                left_ref[k : k + 1, :] = t[j : j + 1]
                right_ref[k : k + 1, :] = t[cx - 2 + j : cx - 1 + j]
    base = 4 * pairs
    copies[3].wait()
    first = x_ref[0:16, :][0:1].astype(F32)
    last = x_ref[cx - 16 : cx, :][15:16].astype(F32)
    for s in range(16):
        left_ref[base + s : base + s + 1, :] = first[:, s * cx : (s + 1) * cx]
        right_ref[base + s : base + s + 1, :] = last[:, s * cx : (s + 1) * cx]
    out.wait()


def strip(x, cy):
    both = jnp.concatenate([turn(x, OFF, 1), turn(x, OFF - cy, 1)], axis=0)
    lane = places(both.shape, 1)
    return jnp.where((lane >= OFF) & (lane < OFF + cy), both, 0.0)


def received(left_ref, right_ref, a, pairs, cy):
    refs = ((left_ref, 2 * a), (left_ref, 2 * a + 1), (right_ref, 2 * a), (right_ref, 2 * a + 1))
    return [strip(ref[k * pairs : (k + 1) * pairs, :], cy) for ref, k in refs]


def pack_y_kernel(p_ref, m_ref, x_ref, left_ref, right_ref, up_ref, down_ref, rows_ref, row_ref):
    planes, cy, cx = p_ref.shape
    for a, ref in enumerate((p_ref, m_ref)):
        for r in range(3):
            up_ref[3 * a + r] = ref[:, cy - 3 + r, :]
            down_ref[3 * a + r] = ref[:, r, :]
    lane = places((planes, cx), 1)
    up = jnp.zeros((planes, cx), F32)
    down = up
    for a in range(2):
        for j, s in enumerate(received(left_ref, right_ref, a, planes // 2, cy)):
            at = 3 * (4 * a + j)
            here = (lane >= at) & (lane < at + 3)
            up = jnp.where(here, turn(s, at - (OFF + cy - 3), 1), up)
            down = jnp.where(here, turn(s, at - OFF, 1), down)
    up_ref[6] = up
    down_ref[6] = down
    rows_ref[:cx] = x_ref[...]
    row_ref[...] = jnp.zeros(row_ref.shape, F32)
    base = left_ref.shape[0] - 16
    for s in range(16):
        row_ref[0:1, s * cx : (s + 1) * cx] = left_ref[base + s : base + s + 1, :]
        row_ref[3:4, s * cx : (s + 1) * cx] = right_ref[base + s : base + s + 1, :]
    row_ref[1:2, :] = x_ref[0:16, :][0:1].astype(F32)
    row_ref[2:3, :] = x_ref[cx - 16 : cx, :][15:16].astype(F32)
    rows_ref[cx:] = row_ref[...].astype(BF16)


def explicit_kernel(
    p_ref, m_ref, own_l_ref, own_r_ref, left_ref, right_ref, up_ref, down_ref,
    send_ref, fz_ref, fy_ref, fx_hbm, edge_ref,
    v_ref, c_ref, f_ref, fx_ref, side_ref, rim_ref, sem,
):
    planes, cy, cx = p_ref.shape
    pairs = planes // 2
    tall = cy + 2 * OFF
    lane = places((planes, cx), 1)
    plane = places((planes, cx), 0)

    def strips(a):
        out = []
        for j, s in enumerate(received(left_ref, right_ref, a, pairs, cy)):
            at = 3 * (4 * a + j)
            s = jnp.where((lane >= OFF - 3) & (lane < OFF), turn(up_ref[6], OFF - 3 - at, 1), s)
            s = jnp.where((lane >= OFF + cy) & (lane < OFF + cy + 3), turn(down_ref[6], OFF + cy - at, 1), s)
            out.append(s)
        own = []
        for ref, j, at in ((own_l_ref, 0, 0), (own_l_ref, 1, 1), (own_r_ref, 0, cx - 2), (own_r_ref, 1, cx - 1)):
            k = 2 * a + j
            s = strip(ref[k * pairs : (k + 1) * pairs, :], cy)
            for r in (1, 2):
                s = jnp.where(lane == OFF - 3 + r, turn(up_ref[3 * a + r], OFF - 3 + r - at, 1), s)
            for r in (0, 1):
                s = jnp.where(lane == OFF + cy + r, turn(down_ref[3 * a + r], OFF + cy + r - at, 1), s)
            own.append(s)
        return out[:2] + own[:2], own[2:] + out[2:]

    def strip_first(v, m, vl, ml, vr, mr):
        above = jnp.where(plane == planes - 1, 0.0, turn(m, -1, 0))
        fz = face_mob(m, above)
        gz = fz * (turn(v, -1, 0) - v)
        fy = face_mob(m, turn(m, -1, 1))
        gy = fy * (turn(v, -1, 1) - v)
        lap = gz - jnp.where(plane == 0, 0.0, turn(gz, 1, 0)) + gy - turn(gy, 1, 1)
        lap = lap + face_mob(m, mr) * (vr - v) + face_mob(m, ml) * (vl - v)
        return v + step_size * lap

    columns = []
    for side, (v, m) in enumerate(zip(strips(0), strips(1), strict=True)):
        f = face_mob(m[1], m[2])
        a = strip_first(v[1], m[1], v[0], m[0], v[2], m[2])
        b = strip_first(v[2], m[2], v[1], m[1], v[3], m[3])
        columns += [f * (v[2] - v[1]), f * (b - a)]
        side_ref[...] = f
        even = turn(side_ref[pl.ds(0, pairs, stride=2), :], -OFF, 1)
        odd = turn(side_ref[pl.ds(1, pairs, stride=2), :], cy - OFF, 1)
        edge_ref[side * pairs : (side + 1) * pairs, :] = jnp.where(lane[:pairs] < cy, even, odd)
    stacked = jnp.concatenate(columns + [jnp.zeros((cx - 4 * planes, cx), F32)], axis=0)
    across = stacked.T[:tall]

    part = tall // 2

    def column(k, z, h):
        at = k * planes + z
        return jnp.broadcast_to(across[h * part : (h + 1) * part, at : at + 1], (part, cx))

    blank = jnp.zeros((OFF, cx), F32)
    for ref in (v_ref, c_ref, f_ref):
        for z in (0, planes + 1):
            ref[z * tall : (z + 1) * tall, :] = jnp.zeros((tall, cx), F32)
    for ref, a, field in ((v_ref, 0, p_ref), (c_ref, 1, m_ref)):
        for z in range(planes):
            base = (z + 1) * tall
            ref[base : base + OFF, :] = blank
            ref[base + OFF : base + OFF + cy, :] = field[z]
            ref[base + OFF + cy : base + tall, :] = blank
        for r in range(3):
            ref[pl.ds(tall + OFF - 3 + r, planes, stride=tall), :] = up_ref[3 * a + r]
            ref[pl.ds(tall + OFF + cy + r, planes, stride=tall), :] = down_ref[3 * a + r]

    wide = places((part, cx), 1)

    def step(ref, z, h, fz, fy, fx, gz_before, gl, gr):
        at = (z + 1) * tall + h * part
        v = ref[at : at + part, :]
        gz = fz * (ref[at + tall : at + tall + part, :] - v)
        gy = fy * (ref[at + 1 : at + 1 + part, :] - v)
        flat = OFF + z * tall + h * part - 1
        gu = fy_ref[flat : flat + part, :] * (v - ref[at - 1 : at - 1 + part, :])
        gx = jnp.where(wide == 0, gl, fx * (v - turn(v, 1, 1)))
        lap = gz - gz_before + gy - gu + jnp.where(wide == cx - 1, gr, turn(gx, -1, 1)) - gx
        return v + step_size * lap, gz

    fz_ref[:tall, :] = jnp.zeros((tall, cx), F32)
    fy_ref[:OFF, :] = jnp.zeros((OFF, cx), F32)
    for h in range(2):
        before = jnp.zeros((part, cx), F32)
        for z in range(planes):
            at = (z + 1) * tall + h * part
            flat = z * tall + h * part
            m = c_ref[at : at + part, :]
            fz = face_mob(m, c_ref[at + tall : at + tall + part, :])
            fy = face_mob(m, c_ref[at + 1 : at + 1 + part, :])
            fx = face_mob(m, turn(m, 1, 1))
            fz_ref[at : at + part, :] = fz
            fy_ref[OFF + flat : OFF + flat + part, :] = fy
            fx_ref[flat : flat + part, :] = fx
            out, before = step(v_ref, z, h, fz, fy, fx, before, column(0, z, h), column(2, z, h))
            f_ref[at : at + part, :] = out
    leave = pltpu.make_async_copy(fx_ref, fx_hbm, sem)
    leave.start()

    rim_ref[...] = jnp.zeros(rim_ref.shape, F32)
    quarter = planes // 4
    for h in range(2):
        before = jnp.zeros((part, cx), F32)
        for z in range(planes):
            at = (z + 1) * tall + h * part
            flat = z * tall + h * part
            out, before = step(
                f_ref, z, h, fz_ref[at : at + part, :], fy_ref[OFF + flat : OFF + flat + part, :],
                fx_ref[flat : flat + part, :], before, column(1, z, h), column(3, z, h),
            )
            v_ref[at : at + part, :] = out
    for z in range(planes):
        out = v_ref[(z + 1) * tall : (z + 2) * tall, :]
        q, at = z // quarter, z % quarter
        body = out[OFF : OFF + cy].astype(BF16)
        for x in range(4):
            send_ref[(q // 2) * 8 + x * 2 + q % 2, at * cy : (at + 1) * cy, :] = body
        rim_ref[q, 2 * at : 2 * at + 1, :] = out[OFF - 1 : OFF]
        rim_ref[q, 2 * at + 1 : 2 * at + 2, :] = out[OFF + cy : OFF + cy + 1]
    for q in range(4):
        rims = rim_ref[q].astype(BF16)
        for x in range(4):
            send_ref[(q // 2) * 8 + x * 2 + q % 2, quarter * cy :, :] = rims
    leave.wait()


def solve_x_kernel(block_ref, got_ref, x0_ref, x1_hbm, x2_hbm, x3_hbm, out_ref, x1_ref, x2_ref, x3_ref, sems):
    own = block_ref[0]
    parts, lines, cx = got_ref.shape
    main = lines - 16
    moves = ((x1_hbm, x1_ref), (x2_hbm, x2_ref), (x3_hbm, x3_ref))
    copies = [pltpu.make_async_copy(src, dst, sems.at[i]) for i, (src, dst) in enumerate(moves)]
    for copy in copies:
        copy.start()
    a = jnp.concatenate([got_ref[s] for s in range(parts)], axis=1)
    for other, x_ref in enumerate((x0_ref, x1_ref, x2_ref, x3_ref)):
        if other:
            copies[other - 1].wait()
        block = own ^ other
        m = lax.dot_general(a, x_ref[:cx], NT, preferred_element_type=F32)
        out_ref[block, : main + 8] = m[: main + 8]
        e = lax.dot_general(x_ref[cx:], a[:main], NT, preferred_element_type=F32)
        out_ref[block, main + 8 : main + 12] = e[:4, :cx]
        out_ref[block, main + 12 :] = e[:4, cx:]


def implicit_kernel(back_ref, fz_ref, fy_ref, fx_hbm, edge_ref, out_ref, c_ref, e_ref, fx_ref, sem):
    planes, cy, cx = out_ref.shape
    tall = cy + 2 * OFF
    quarter, pairs = planes // 4, planes // 2
    main = quarter * cy

    come = pltpu.make_async_copy(fx_hbm, fx_ref, sem)
    come.start()

    def chemical(s):
        return s * s * s - s

    for z in (0, planes + 1):
        c_ref[z * tall : (z + 1) * tall, :] = jnp.zeros((tall, cx), F32)
    for q in range(4):
        e_ref[q * 8 : (q + 1) * 8, :] = chemical(back_ref[q, main + 8 : main + 16])
        rims = chemical(back_ref[q, main : main + 8])
        for at in range(quarter):
            base = (q * quarter + at + 1) * tall
            c_ref[base + OFF : base + OFF + cy, :] = chemical(back_ref[q, at * cy : (at + 1) * cy])
            c_ref[base + OFF - 1 : base + OFF, :] = rims[2 * at : 2 * at + 1]
            c_ref[base + OFF + cy : base + OFF + cy + 1, :] = rims[2 * at + 1 : 2 * at + 2]
    ends = [e_ref[pl.ds(j, pairs, stride=4), :] for j in range(4)]
    left = edge_ref[:pairs, :] * (ends[1] - ends[0])
    right = edge_ref[pairs:, :] * (ends[3] - ends[2])
    across = jnp.concatenate([left, right, jnp.zeros((cx - planes, cx), F32)], axis=0).T
    lane = places((cy, cx), 1)
    before = jnp.zeros((cy, cx), F32)
    come.wait()
    for z in range(planes):
        base = (z + 1) * tall + OFF
        flat = z * tall + OFF
        c = c_ref[base : base + cy, :]
        gz = fz_ref[base : base + cy, :] * (c_ref[base + tall : base + tall + cy, :] - c)
        gy = fy_ref[flat + OFF : flat + OFF + cy, :] * (c_ref[base + 1 : base + 1 + cy, :] - c)
        gu = fy_ref[flat + OFF - 1 : flat + OFF - 1 + cy, :] * (c - c_ref[base - 1 : base - 1 + cy, :])
        rows = slice((z % 2) * cy, (z % 2 + 1) * cy)
        gl = jnp.broadcast_to(across[rows, z // 2 : z // 2 + 1], (cy, cx))
        gr = jnp.broadcast_to(across[rows, pairs + z // 2 : pairs + z // 2 + 1], (cy, cx))
        gx = jnp.where(lane == 0, gl, fx_ref[flat : flat + cy, :] * (c - turn(c, 1, 1)))
        lap = gz - before + gy - gu + jnp.where(lane == cx - 1, gr, turn(gx, -1, 1)) - gx
        s = back_ref[z // quarter, (z % quarter) * cy : (z % quarter + 1) * cy]
        out_ref[z] = (s + step_size * lap).astype(BF16)
        before = gz


def solve_y_near_kernel(side_ref, y_hbm, u_ref, sum_ref, y_ref, near_ref, sems):
    high = side_ref[0]
    half, _ = u_ref.shape
    halves = (high, 1 - high)
    columns = [y_hbm.at[:, pl.ds(pl.multiple_of(h * half, half), half)] for h in halves]
    copies = [pltpu.make_async_copy(c, ref, sems.at[i]) for i, (c, ref) in enumerate(zip(columns, (near_ref, y_ref), strict=True))]
    for copy in copies:
        copy.start()
    copies[0].wait()
    sum_ref[...] = jnp.dot(near_ref[...], u_ref[...], preferred_element_type=F32)
    copies[1].wait()


def solve_y_far_kernel(sum_ref, y_ref, u_ref, out_ref):
    total = sum_ref[...] + jnp.dot(y_ref[...], u_ref[...], preferred_element_type=F32)
    out_ref[...] = total.astype(BF16)


def pack_x(core, p, m, x_inverse, y_inverse):
    cx = p.shape[2]
    shape = (2 * p.shape[0] + 16, cx)
    cy, order = y_inverse.shape
    out = (kept(shape, F32),) * 2 + (kept(p.shape, F32),) * 2 + (kept(x_inverse.shape, BF16),)
    out += (jax.ShapeDtypeStruct((cy // 2, order), BF16),)
    scratch = (pltpu.VMEM((cy // 2, order), BF16), pltpu.SemaphoreType.DMA((4,)))
    return call(pack_x_kernel, out, (p, m, x_inverse, y_inverse), core, scratch, range(4), (5,))


def pack_y(p, m, x_inverse, left, right):
    cx, order = x_inverse.shape
    out = (kept((7, p.shape[0], cx), F32),) * 2 + (kept((cx + 16, order), BF16),)
    return call(pack_y_kernel, out, (p, m, x_inverse, left, right), scratch=(pltpu.VMEM((16, order), F32),))


def explicit(*args):
    planes, cy, cx = args[0].shape
    tall = cy + 2 * OFF
    lines = planes // 4 * cy + 16
    field = pltpu.VMEM(((planes + 2) * tall, cx), F32)
    out = (
        kept((16, lines, cx), BF16),
        kept(((planes + 1) * tall, cx), F32),
        kept((planes * tall + OFF, cx), F32),
        jax.ShapeDtypeStruct((planes * tall, cx), F32),
        kept((planes, cx), F32),
    )
    scratch = (field, field, field, pltpu.VMEM((planes * tall, cx), F32), pltpu.VMEM((planes, cx), F32))
    scratch += (pltpu.VMEM((4, 16, cx), F32), pltpu.SemaphoreType.DMA(()))
    return call(explicit_kernel, out, args, scratch=scratch, far_out=(3,))


def solve_x(block, got, x_blocks):
    _, lines, cx = got.shape
    blocks = pltpu.VMEM(x_blocks[0].shape, BF16)
    scratch = (blocks, blocks, blocks, pltpu.SemaphoreType.DMA((3,)))
    return call(solve_x_kernel, kept((4, lines, cx), F32), (got, *x_blocks), block, scratch, (2, 3, 4))


def implicit(back, faces, planes, cy):
    cx = back.shape[2]
    tall = cy + 2 * OFF
    scratch = (pltpu.VMEM(((planes + 2) * tall, cx), F32), pltpu.VMEM((32, cx), F32))
    scratch += (pltpu.VMEM((planes * tall, cx), F32), pltpu.SemaphoreType.DMA(()))
    return call(implicit_kernel, kept((planes, cy, cx), BF16), (back, *faces), None, scratch, (3,))


def solve_y_near(side, y, u):
    half, cx = u.shape
    out = (kept((half, cx), F32), kept((half, half), BF16))
    scratch = (pltpu.VMEM((half, half), BF16), pltpu.SemaphoreType.DMA((2,)))
    return call(solve_y_near_kernel, out, (y, u), side, scratch, (0,))


def solve_y_far(*parts):
    return call(solve_y_far_kernel, kept(parts[-1].shape, BF16), parts)


def both_ways(to_before, to_after, axis):
    size = lax.axis_size(axis)
    up = [(i, i + 1) for i in range(size - 1)]
    return lax.ppermute(to_after, axis, up), lax.ppermute(to_before, axis, [(j, i) for i, j in up])


def local(phase_field, mobility, x_inverse, y_inverse):
    planes, cy, cx = phase_field.shape
    order = y_inverse.shape[1]
    half = order // 2
    core, low, high = lax.axis_index("c"), lax.axis_index("yl"), lax.axis_index("yh")
    swap = [(0, 1), (1, 0)]

    one = lambda v: v.reshape(1).astype(jnp.int32)

    own_l, own_r, phase_field, mobility, x_own, y_part = pack_x(one(core), phase_field, mobility, x_inverse, y_inverse)
    y_rows = lax.all_gather(y_part, ("z", "c"), axis=0, tiled=True)
    left, right = both_ways(own_l, own_r, GX)
    to_up, to_down, rows = pack_y(phase_field, mobility, x_own, left, right)
    up, down = both_ways(to_down, to_up, GY)
    rows_yl = lax.ppermute(rows, "yl", swap)
    x_blocks = (rows, lax.ppermute(rows, "c", swap), rows_yl, lax.ppermute(rows_yl, "c", swap))

    send, *faces = explicit(phase_field, mobility, own_l, own_r, left, right, up, down)
    got = lax.all_to_all(send, GX, 0, 0, tiled=True)
    back = solve_x(one(low * 2 + core), got, x_blocks)
    back = lax.all_to_all(back, ("yl", "c"), 0, 0, tiled=True)
    updated = implicit(back, faces, planes, cy)

    mine = lax.all_to_all(updated, "z", 0, 0, tiled=True).reshape(half, cx)
    y_rows, mine = lax.optimization_barrier((y_rows, mine))
    theirs = lax.ppermute(mine, "yh", swap)
    part, y_far = solve_y_near(one(high), y_rows, mine)
    out = solve_y_far(part, y_far, theirs).reshape(16, cy, cx)
    out = lax.all_to_all(out, "z", 0, 0, tiled=True)
    return out.astype(F32)


def solution(mesh):
    shape = (2, mesh.shape["gx"] // 4, 2, 2, mesh.shape["gy"] // 2)
    torus = Mesh(mesh.devices.reshape(shape), ("yl", "x", "c", "yh", "z"))
    in_specs = (P(None, GY, GX), P(None, GY, GX), P(GX, None), P(GY, None))
    return jax.shard_map(local, mesh=torus, in_specs=in_specs, out_specs=P(None, GY, GX), check_vma=False)
```

```python
import jax
import jax.numpy as jnp
from jax import lax
from jax.experimental import pallas as pl
from jax.experimental.pallas import tpu as pltpu
from jax.sharding import Mesh
from jax.sharding import PartitionSpec as P

GX = ("yl", "x", "c")
GY = ("yh", "z")

step_size = 0.15
F32 = jnp.float32
BF16 = jnp.bfloat16
NT = (((1,), (1,)), ((), ()))
VMEM = pl.BlockSpec(memory_space=pltpu.VMEM)
OFF = 8


def near(v):
    return pltpu.with_memory_space_constraint(v, pltpu.VMEM)


def away(v):
    return pltpu.with_memory_space_constraint(v, pltpu.HBM)


def kept(shape, dtype):
    return pltpu.VMEM(shape, dtype)


FAR = pl.BlockSpec(memory_space=pltpu.HBM)


def away_kept(shape, dtype):
    return pltpu.HBM(shape, dtype)


def call(kernel, out_shape, args, scalar=None, scratch=(), far=(), far_out=()):
    scalars = [] if scalar is None else [scalar]
    many = isinstance(out_shape, tuple)
    return pl.pallas_call(
        kernel,
        out_shape=out_shape,
        in_specs=[pl.BlockSpec(memory_space=pltpu.SMEM)] * len(scalars) + [FAR if i in far else VMEM for i in range(len(args))],
        out_specs=tuple(FAR if i in far_out else VMEM for i in range(len(out_shape))) if many else VMEM,
        scratch_shapes=list(scratch),
        compiler_params=pltpu.CompilerParams(vmem_limit_bytes=16 << 20),
    )(*scalars, *[away(v) if i in far else near(v) for i, v in enumerate(args)])


def face_mob(p, q):
    return 2.0 * p * q / jnp.maximum(p + q, 0.25)


def turn(x, shift, axis):
    return pltpu.roll(x, shift % x.shape[axis], axis)


def places(shape, axis):
    return lax.broadcasted_iota(jnp.int32, shape, axis)


def pack_x_kernel(core_ref, p_hbm, m_hbm, x_hbm, y_hbm, left_ref, right_ref, p_ref, m_ref, x_ref, part_hbm, part_ref, sems):
    planes, _, cx = p_ref.shape
    pairs = planes // 2
    rows = part_hbm.shape[0]
    copies = (
        (y_hbm.at[pl.ds(pl.multiple_of(core_ref[0] * rows, rows), rows)], part_ref),
        (p_hbm, p_ref),
        (m_hbm, m_ref),
        (x_hbm, x_ref),
    )
    copies = [pltpu.make_async_copy(src, dst, sems.at[i]) for i, (src, dst) in enumerate(copies)]
    for copy in copies:
        copy.start()
    copies[0].wait()
    out = pltpu.make_async_copy(part_ref, part_hbm, sems.at[0])
    out.start()
    for a, ref in enumerate((p_ref, m_ref)):
        copies[1 + a].wait()
        for i in range(pairs):
            t = jnp.concatenate([ref[i], ref[i + pairs]], axis=0).T
            for j in range(2):
                k = (2 * a + j) * pairs + i
                left_ref[k : k + 1, :] = t[j : j + 1]
                right_ref[k : k + 1, :] = t[cx - 2 + j : cx - 1 + j]
    base = 4 * pairs
    copies[3].wait()
    first = x_ref[0:16, :][0:1].astype(F32)
    last = x_ref[cx - 16 : cx, :][15:16].astype(F32)
    for s in range(16):
        left_ref[base + s : base + s + 1, :] = first[:, s * cx : (s + 1) * cx]
        right_ref[base + s : base + s + 1, :] = last[:, s * cx : (s + 1) * cx]
    out.wait()


def strip(x, cy):
    both = jnp.concatenate([turn(x, OFF, 1), turn(x, OFF - cy, 1)], axis=0)
    lane = places(both.shape, 1)
    return jnp.where((lane >= OFF) & (lane < OFF + cy), both, 0.0)


def received(left_ref, right_ref, a, pairs, cy):
    refs = ((left_ref, 2 * a), (left_ref, 2 * a + 1), (right_ref, 2 * a), (right_ref, 2 * a + 1))
    return [strip(ref[k * pairs : (k + 1) * pairs, :], cy) for ref, k in refs]


def pack_y_kernel(p_ref, m_ref, x_ref, left_ref, right_ref, up_ref, down_ref, rows_ref, row_ref):
    planes, cy, cx = p_ref.shape
    for a, ref in enumerate((p_ref, m_ref)):
        for r in range(3):
            up_ref[3 * a + r] = ref[:, cy - 3 + r, :]
            down_ref[3 * a + r] = ref[:, r, :]
    lane = places((planes, cx), 1)
    up = jnp.zeros((planes, cx), F32)
    down = up
    for a in range(2):
        for j, s in enumerate(received(left_ref, right_ref, a, planes // 2, cy)):
            at = 3 * (4 * a + j)
            here = (lane >= at) & (lane < at + 3)
            up = jnp.where(here, turn(s, at - (OFF + cy - 3), 1), up)
            down = jnp.where(here, turn(s, at - OFF, 1), down)
    up_ref[6] = up
    down_ref[6] = down
    rows_ref[:cx] = x_ref[...]
    row_ref[...] = jnp.zeros(row_ref.shape, F32)
    base = left_ref.shape[0] - 16
    for s in range(16):
        row_ref[0:1, s * cx : (s + 1) * cx] = left_ref[base + s : base + s + 1, :]
        row_ref[3:4, s * cx : (s + 1) * cx] = right_ref[base + s : base + s + 1, :]
    row_ref[1:2, :] = x_ref[0:16, :][0:1].astype(F32)
    row_ref[2:3, :] = x_ref[cx - 16 : cx, :][15:16].astype(F32)
    rows_ref[cx:] = row_ref[...].astype(BF16)


def explicit_kernel(
    p_ref, m_ref, own_l_ref, own_r_ref, left_ref, right_ref, up_ref, down_ref,
    send_ref, fz_ref, fy_ref, fx_ref, edge_ref,
    v_ref, c_ref, f_ref, side_ref, rim_ref, turned_ref, gy_ref,
):
    planes, cy, cx = p_ref.shape
    pairs = planes // 2
    tall = cy + 2 * OFF
    lane = places((planes, cx), 1)
    plane = places((planes, cx), 0)

    def strips(a):
        out = []
        for j, s in enumerate(received(left_ref, right_ref, a, pairs, cy)):
            at = 3 * (4 * a + j)
            s = jnp.where((lane >= OFF - 3) & (lane < OFF), turn(up_ref[6], OFF - 3 - at, 1), s)
            s = jnp.where((lane >= OFF + cy) & (lane < OFF + cy + 3), turn(down_ref[6], OFF + cy - at, 1), s)
            out.append(s)
        own = []
        for ref, j, at in ((own_l_ref, 0, 0), (own_l_ref, 1, 1), (own_r_ref, 0, cx - 2), (own_r_ref, 1, cx - 1)):
            k = 2 * a + j
            s = strip(ref[k * pairs : (k + 1) * pairs, :], cy)
            for r in (1, 2):
                s = jnp.where(lane == OFF - 3 + r, turn(up_ref[3 * a + r], OFF - 3 + r - at, 1), s)
            for r in (0, 1):
                s = jnp.where(lane == OFF + cy + r, turn(down_ref[3 * a + r], OFF + cy + r - at, 1), s)
            own.append(s)
        return out[:2] + own[:2], own[2:] + out[2:]

    def strip_first(v, m, vl, ml, vr, mr):
        above = jnp.where(plane == planes - 1, 0.0, turn(m, -1, 0))
        fz = face_mob(m, above)
        gz = fz * (turn(v, -1, 0) - v)
        fy = face_mob(m, turn(m, -1, 1))
        gy = fy * (turn(v, -1, 1) - v)
        lap = gz - jnp.where(plane == 0, 0.0, turn(gz, 1, 0)) + gy - turn(gy, 1, 1)
        lap = lap + face_mob(m, mr) * (vr - v) + face_mob(m, ml) * (vl - v)
        return v + step_size * lap

    turned_ref[...] = jnp.zeros(turned_ref.shape, F32)
    for side, (v, m) in enumerate(zip(strips(0), strips(1), strict=True)):
        f = face_mob(m[1], m[2])
        a = strip_first(v[1], m[1], v[0], m[0], v[2], m[2])
        b = strip_first(v[2], m[2], v[1], m[1], v[3], m[3])
        turned_ref[pl.ds(2 - side, planes, stride=2), :] = f * (v[2] - v[1])
        turned_ref[pl.ds(66 - side, planes, stride=2), :] = f * (b - a)
        side_ref[...] = f
        even = turn(side_ref[pl.ds(0, pairs, stride=2), :], -OFF, 1)
        odd = turn(side_ref[pl.ds(1, pairs, stride=2), :], cy - OFF, 1)
        edge_ref[side * pairs : (side + 1) * pairs, :] = jnp.where(lane[:pairs] < cy, even, odd)
    across = turned_ref[...].T
    part = tall // 2

    def ends(k, z, h):
        return turn(across[h * part : (h + 1) * part], -(64 * k + 2 * z + 2), 1)

    blank = jnp.zeros((OFF, cx), F32)
    for ref in (v_ref, c_ref, f_ref):
        for z in (0, planes + 1):
            ref[z * tall : (z + 1) * tall, :] = jnp.zeros((tall, cx), F32)
    for ref, a, field in ((v_ref, 0, p_ref), (c_ref, 1, m_ref)):
        for z in range(planes):
            base = (z + 1) * tall
            ref[base : base + OFF, :] = blank
            ref[base + OFF : base + OFF + cy, :] = field[z]
            ref[base + OFF + cy : base + tall, :] = blank
        for r in range(3):
            ref[pl.ds(tall + OFF - 3 + r, planes, stride=tall), :] = up_ref[3 * a + r]
            ref[pl.ds(tall + OFF + cy + r, planes, stride=tall), :] = down_ref[3 * a + r]

    wide = places((part, cx), 1)

    def step(ref, z, h, fz, fy, fx, gz_before, end):
        at = (z + 1) * tall + h * part
        v = ref[at : at + part, :]
        gz = fz * (ref[at + tall : at + tall + part, :] - v)
        gy = fy * (ref[at + 1 : at + 1 + part, :] - v)
        flat = OFF + z * tall + h * part
        gy_ref[flat : flat + part, :] = gy
        gu = gy_ref[flat - 1 : flat - 1 + part, :]
        gx = jnp.where(wide == 0, end, fx * (v - turn(v, 1, 1)))
        lap = gz - gz_before + gy - gu + jnp.where(wide == cx - 1, end, turn(gx, -1, 1)) - gx
        return v + step_size * lap, gz

    fz_ref[:tall, :] = jnp.zeros((tall, cx), F32)
    fy_ref[:OFF, :] = jnp.zeros((OFF, cx), F32)
    gy_ref[:OFF, :] = jnp.zeros((OFF, cx), F32)
    for h in range(2):
        before = jnp.zeros((part, cx), F32)
        for z in range(planes):
            at = (z + 1) * tall + h * part
            flat = z * tall + h * part
            m = c_ref[at : at + part, :]
            fz = face_mob(m, c_ref[at + tall : at + tall + part, :])
            fy = face_mob(m, c_ref[at + 1 : at + 1 + part, :])
            fx = face_mob(m, turn(m, 1, 1))
            fz_ref[at : at + part, :] = fz
            fy_ref[OFF + flat : OFF + flat + part, :] = fy
            fx_ref[flat : flat + part, :] = fx
            out, before = step(v_ref, z, h, fz, fy, fx, before, ends(0, z, h))
            f_ref[at : at + part, :] = out

    rim_ref[...] = jnp.zeros(rim_ref.shape, F32)
    quarter = planes // 4
    for h in range(2):
        before = jnp.zeros((part, cx), F32)
        for z in range(planes):
            at = (z + 1) * tall + h * part
            flat = z * tall + h * part
            out, before = step(
                f_ref, z, h, fz_ref[at : at + part, :], fy_ref[OFF + flat : OFF + flat + part, :],
                fx_ref[flat : flat + part, :], before, ends(1, z, h),
            )
            v_ref[at : at + part, :] = out
    for z in range(planes):
        out = v_ref[(z + 1) * tall : (z + 2) * tall, :]
        q, at = z // quarter, z % quarter
        body = out[OFF : OFF + cy].astype(BF16)
        for x in range(4):
            send_ref[(q // 2) * 8 + x * 2 + q % 2, at * cy : (at + 1) * cy, :] = body
        rim_ref[q, 2 * at : 2 * at + 1, :] = out[OFF - 1 : OFF]
        rim_ref[q, 2 * at + 1 : 2 * at + 2, :] = out[OFF + cy : OFF + cy + 1]
    for q in range(4):
        rims = rim_ref[q].astype(BF16)
        for x in range(4):
            send_ref[(q // 2) * 8 + x * 2 + q % 2, quarter * cy :, :] = rims


def solve_x_kernel(block_ref, got_ref, x0_hbm, x1_hbm, x2_hbm, x3_hbm, out_ref, x0_ref, x1_ref, x2_ref, x3_ref, sems):
    own = block_ref[0]
    parts, lines, cx = got_ref.shape
    main = lines - 16
    moves = ((x0_hbm, x0_ref), (x1_hbm, x1_ref), (x2_hbm, x2_ref), (x3_hbm, x3_ref))
    copies = [pltpu.make_async_copy(src, dst, sems.at[i]) for i, (src, dst) in enumerate(moves)]
    for copy in copies:
        copy.start()
    a = jnp.concatenate([got_ref[s] for s in range(parts)], axis=1)
    for other, x_ref in enumerate((x0_ref, x1_ref, x2_ref, x3_ref)):
        copies[other].wait()
        block = own ^ other
        m = lax.dot_general(a, x_ref[:cx], NT, preferred_element_type=F32)
        out_ref[block, : main + 8] = m[: main + 8]
        e = lax.dot_general(x_ref[cx:], a[:main], NT, preferred_element_type=F32)
        out_ref[block, main + 8 : main + 12] = e[:4, :cx]
        out_ref[block, main + 12 :] = e[:4, cx:]


def implicit_kernel(back_ref, fz_ref, fy_ref, fx_ref, edge_ref, out_ref, c_ref, e_ref):
    planes, cy, cx = out_ref.shape
    tall = cy + 2 * OFF
    quarter, pairs = planes // 4, planes // 2
    main = quarter * cy

    def chemical(s):
        return s * s * s - s

    for z in (0, planes + 1):
        c_ref[z * tall : (z + 1) * tall, :] = jnp.zeros((tall, cx), F32)
    for q in range(4):
        e_ref[q * 8 : (q + 1) * 8, :] = chemical(back_ref[q, main + 8 : main + 16])
        rims = chemical(back_ref[q, main : main + 8])
        for at in range(quarter):
            base = (q * quarter + at + 1) * tall
            c_ref[base + OFF : base + OFF + cy, :] = chemical(back_ref[q, at * cy : (at + 1) * cy])
            c_ref[base + OFF - 1 : base + OFF, :] = rims[2 * at : 2 * at + 1]
            c_ref[base + OFF + cy : base + OFF + cy + 1, :] = rims[2 * at + 1 : 2 * at + 2]
    ends = [e_ref[pl.ds(j, pairs, stride=4), :] for j in range(4)]
    left = edge_ref[:pairs, :] * (ends[1] - ends[0])
    right = edge_ref[pairs:, :] * (ends[3] - ends[2])
    across = jnp.concatenate([left, right, jnp.zeros((cx - planes, cx), F32)], axis=0).T
    lane = places((cy, cx), 1)
    before = jnp.zeros((cy, cx), F32)
    for z in range(planes):
        base = (z + 1) * tall + OFF
        flat = z * tall + OFF
        c = c_ref[base : base + cy, :]
        gz = fz_ref[base : base + cy, :] * (c_ref[base + tall : base + tall + cy, :] - c)
        gy = fy_ref[flat + OFF : flat + OFF + cy, :] * (c_ref[base + 1 : base + 1 + cy, :] - c)
        gu = fy_ref[flat + OFF - 1 : flat + OFF - 1 + cy, :] * (c - c_ref[base - 1 : base - 1 + cy, :])
        rows = slice((z % 2) * cy, (z % 2 + 1) * cy)
        gl = jnp.broadcast_to(across[rows, z // 2 : z // 2 + 1], (cy, cx))
        gr = jnp.broadcast_to(across[rows, pairs + z // 2 : pairs + z // 2 + 1], (cy, cx))
        gx = jnp.where(lane == 0, gl, fx_ref[flat : flat + cy, :] * (c - turn(c, 1, 1)))
        lap = gz - before + gy - gu + jnp.where(lane == cx - 1, gr, turn(gx, -1, 1)) - gx
        s = back_ref[z // quarter, (z % quarter) * cy : (z % quarter + 1) * cy]
        out_ref[z] = (s + step_size * lap).astype(BF16)
        before = gz


def solve_y_near_kernel(side_ref, y_hbm, u_ref, sum_ref, y_ref, near_ref, sems):
    high = side_ref[0]
    half, _ = u_ref.shape
    halves = (high, 1 - high)
    columns = [y_hbm.at[:, pl.ds(pl.multiple_of(h * half, half), half)] for h in halves]
    copies = [pltpu.make_async_copy(c, ref, sems.at[i]) for i, (c, ref) in enumerate(zip(columns, (near_ref, y_ref), strict=True))]
    for copy in copies:
        copy.start()
    copies[0].wait()
    sum_ref[...] = jnp.dot(near_ref[...], u_ref[...], preferred_element_type=F32)
    copies[1].wait()


def solve_y_far_kernel(sum_ref, y_ref, u_ref, out_ref):
    total = sum_ref[...] + jnp.dot(y_ref[...], u_ref[...], preferred_element_type=F32)
    out_ref[...] = total.astype(BF16)


def pack_x(core, p, m, x_inverse, y_inverse):
    cx = p.shape[2]
    shape = (2 * p.shape[0] + 16, cx)
    cy, order = y_inverse.shape
    out = (kept(shape, F32),) * 2 + (kept(p.shape, F32),) * 2 + (kept(x_inverse.shape, BF16),)
    out += (away_kept((cy // 2, order), BF16),)
    scratch = (pltpu.VMEM((cy // 2, order), BF16), pltpu.SemaphoreType.DMA((4,)))
    return call(pack_x_kernel, out, (p, m, x_inverse, y_inverse), core, scratch, range(4), (5,))


def pack_y(p, m, x_inverse, left, right):
    cx, order = x_inverse.shape
    out = (kept((7, p.shape[0], cx), F32),) * 2 + (kept((cx + 16, order), BF16),)
    return call(pack_y_kernel, out, (p, m, x_inverse, left, right), scratch=(pltpu.VMEM((16, order), F32),))


def explicit(*args):
    planes, cy, cx = args[0].shape
    tall = cy + 2 * OFF
    lines = planes // 4 * cy + 16
    field = pltpu.VMEM(((planes + 2) * tall, cx), F32)
    out = (
        kept((16, lines, cx), BF16),
        kept(((planes + 1) * tall, cx), F32),
        kept((planes * tall + OFF, cx), F32),
        kept((planes * tall, cx), F32),
        kept((planes, cx), F32),
    )
    scratch = (field, field, field, pltpu.VMEM((planes, cx), F32))
    scratch += (pltpu.VMEM((4, 16, cx), F32), pltpu.VMEM((cx, cx), F32))
    scratch += (pltpu.VMEM((planes * tall + OFF, cx), F32),)
    return call(explicit_kernel, out, args, scratch=scratch)


def solve_x(block, got, x_blocks):
    _, lines, cx = got.shape
    blocks = pltpu.VMEM(x_blocks[0].shape, BF16)
    scratch = (blocks,) * 4 + (pltpu.SemaphoreType.DMA((4,)),)
    return call(solve_x_kernel, kept((4, lines, cx), F32), (got, *x_blocks), block, scratch, (1, 2, 3, 4))


def implicit(back, faces, planes, cy):
    cx = back.shape[2]
    tall = cy + 2 * OFF
    scratch = (pltpu.VMEM(((planes + 2) * tall, cx), F32), pltpu.VMEM((32, cx), F32))
    return call(implicit_kernel, kept((planes, cy, cx), BF16), (back, *faces), scratch=scratch)


def solve_y_near(side, y, u):
    half, cx = u.shape
    out = (kept((half, cx), F32), kept((half, half), BF16))
    scratch = (pltpu.VMEM((half, half), BF16), pltpu.SemaphoreType.DMA((2,)))
    return call(solve_y_near_kernel, out, (y, u), side, scratch, (0,))


def solve_y_far(*parts):
    return call(solve_y_far_kernel, kept(parts[-1].shape, BF16), parts)


def both_ways(to_before, to_after, axis):
    size = lax.axis_size(axis)
    up = [(i, i + 1) for i in range(size - 1)]
    return lax.ppermute(to_after, axis, up), lax.ppermute(to_before, axis, [(j, i) for i, j in up])


def local(phase_field, mobility, x_inverse, y_inverse):
    planes, cy, cx = phase_field.shape
    order = y_inverse.shape[1]
    half = order // 2
    core, low, high = lax.axis_index("c"), lax.axis_index("yl"), lax.axis_index("yh")
    swap = [(0, 1), (1, 0)]

    one = lambda v: v.reshape(1).astype(jnp.int32)

    own_l, own_r, phase_field, mobility, x_own, y_part = pack_x(one(core), phase_field, mobility, x_inverse, y_inverse)
    y_rows = lax.all_gather(y_part, ("z", "c"), axis=0, tiled=True)
    left, right = both_ways(own_l, own_r, GX)
    to_up, to_down, rows = pack_y(phase_field, mobility, x_own, left, right)
    up, down = both_ways(to_down, to_up, GY)
    rows_yl = lax.ppermute(rows, "yl", swap)
    x_blocks = (rows, lax.ppermute(rows, "c", swap), rows_yl, lax.ppermute(rows_yl, "c", swap))

    send, *faces = explicit(phase_field, mobility, own_l, own_r, left, right, up, down)
    got = lax.all_to_all(send, GX, 0, 0, tiled=True)
    back = solve_x(one(low * 2 + core), got, x_blocks)
    back = lax.all_to_all(back, ("yl", "c"), 0, 0, tiled=True)
    updated = implicit(back, faces, planes, cy)

    mine = lax.all_to_all(updated, "z", 0, 0, tiled=True).reshape(half, cx)
    y_rows, mine = lax.optimization_barrier((y_rows, mine))
    theirs = lax.ppermute(mine, "yh", swap)
    part, y_far = solve_y_near(one(high), y_rows, mine)
    out = solve_y_far(part, y_far, theirs).reshape(16, cy, cx)
    out = lax.all_to_all(out, "z", 0, 0, tiled=True)
    return out.astype(F32)


def solution(mesh):
    shape = (2, mesh.shape["gx"] // 4, 2, 2, mesh.shape["gy"] // 2)
    torus = Mesh(mesh.devices.reshape(shape), ("yl", "x", "c", "yh", "z"))
    in_specs = (P(None, GY, GX), P(None, GY, GX), P(GX, None), P(GY, None))
    return jax.shard_map(local, mesh=torus, in_specs=in_specs, out_specs=P(None, GY, GX), check_vma=False)
```

```python
import jax
import jax.numpy as jnp
from jax import lax
from jax.experimental import pallas as pl
from jax.experimental.pallas import tpu as pltpu
from jax.sharding import Mesh
from jax.sharding import PartitionSpec as P

GX = ("yl", "x", "c")
GY = ("yh", "z")

step_size = 0.15
F32 = jnp.float32
BF16 = jnp.bfloat16
NT = (((1,), (1,)), ((), ()))
VMEM = pl.BlockSpec(memory_space=pltpu.VMEM)
OFF = 8


def near(v):
    return pltpu.with_memory_space_constraint(v, pltpu.VMEM)


def away(v):
    return pltpu.with_memory_space_constraint(v, pltpu.HBM)


def kept(shape, dtype):
    return pltpu.VMEM(shape, dtype)


FAR = pl.BlockSpec(memory_space=pltpu.HBM)


def away_kept(shape, dtype):
    return pltpu.HBM(shape, dtype)


def call(kernel, out_shape, args, scalar=None, scratch=(), far=(), far_out=(), aliases=None):
    scalars = [] if scalar is None else [scalar]
    many = isinstance(out_shape, tuple)
    return pl.pallas_call(
        kernel,
        out_shape=out_shape,
        in_specs=[pl.BlockSpec(memory_space=pltpu.SMEM)] * len(scalars) + [FAR if i in far else VMEM for i in range(len(args))],
        out_specs=tuple(FAR if i in far_out else VMEM for i in range(len(out_shape))) if many else VMEM,
        scratch_shapes=list(scratch),
        input_output_aliases=aliases or {},
        compiler_params=pltpu.CompilerParams(vmem_limit_bytes=16 << 20),
    )(*scalars, *[away(v) if i in far else near(v) for i, v in enumerate(args)])


def face_mob(p, q):
    return 2.0 * p * q / jnp.maximum(p + q, 0.25)


def turn(x, shift, axis):
    return pltpu.roll(x, shift % x.shape[axis], axis)


def places(shape, axis):
    return lax.broadcasted_iota(jnp.int32, shape, axis)


def pack_x_kernel(core_ref, p_hbm, m_hbm, x_hbm, y_hbm, left_ref, right_ref, p_ref, m_ref, rows_hbm, part_hbm, x_ref, part_ref, sems):
    planes, _, cx = p_ref.shape
    pairs = planes // 2
    rows = part_hbm.shape[0]
    copies = (
        (y_hbm.at[pl.ds(pl.multiple_of(core_ref[0] * rows, rows), rows)], part_ref),
        (p_hbm, p_ref),
        (m_hbm, m_ref),
        (x_hbm, x_ref),
    )
    copies = [pltpu.make_async_copy(src, dst, sems.at[i]) for i, (src, dst) in enumerate(copies)]
    for copy in copies:
        copy.start()
    copies[0].wait()
    out = pltpu.make_async_copy(part_ref, part_hbm, sems.at[0])
    out.start()
    for a, ref in enumerate((p_ref, m_ref)):
        copies[1 + a].wait()
        for i in range(pairs):
            t = jnp.concatenate([ref[i], ref[i + pairs]], axis=0).T
            for j in range(2):
                k = (2 * a + j) * pairs + i
                left_ref[k : k + 1, :] = t[j : j + 1]
                right_ref[k : k + 1, :] = t[cx - 2 + j : cx - 1 + j]
    base = 4 * pairs
    copies[3].wait()
    own = pltpu.make_async_copy(x_ref, rows_hbm.at[pl.ds(0, cx)], sems.at[3])
    own.start()
    first = x_ref[0:16, :][0:1].astype(F32)
    last = x_ref[cx - 16 : cx, :][15:16].astype(F32)
    for s in range(16):
        left_ref[base + s : base + s + 1, :] = first[:, s * cx : (s + 1) * cx]
        right_ref[base + s : base + s + 1, :] = last[:, s * cx : (s + 1) * cx]
    out.wait()
    own.wait()


def strip(x, cy):
    both = jnp.concatenate([turn(x, OFF, 1), turn(x, OFF - cy, 1)], axis=0)
    lane = places(both.shape, 1)
    return jnp.where((lane >= OFF) & (lane < OFF + cy), both, 0.0)


def received(left_ref, right_ref, a, pairs, cy):
    refs = ((left_ref, 2 * a), (left_ref, 2 * a + 1), (right_ref, 2 * a), (right_ref, 2 * a + 1))
    return [strip(ref[k * pairs : (k + 1) * pairs, :], cy) for ref, k in refs]


def pack_y_kernel(
    p_ref, m_ref, own_l_ref, own_r_ref, left_ref, right_ref, _, up_ref, down_ref, rows_hbm, row_ref, cast_ref, sem
):
    planes, cy, cx = p_ref.shape
    base = left_ref.shape[0] - 16
    row_ref[...] = jnp.zeros(row_ref.shape, F32)
    for j, ref in enumerate((left_ref, own_l_ref, own_r_ref, right_ref)):
        for s in range(16):
            row_ref[j : j + 1, s * cx : (s + 1) * cx] = ref[base + s : base + s + 1, :]
    cast_ref[...] = row_ref[...].astype(BF16)
    copy = pltpu.make_async_copy(cast_ref, rows_hbm.at[pl.ds(cx, 16)], sem)
    copy.start()
    for a, ref in enumerate((p_ref, m_ref)):
        for r in range(3):
            up_ref[3 * a + r] = ref[:, cy - 3 + r, :]
            down_ref[3 * a + r] = ref[:, r, :]
    lane = places((planes, cx), 1)
    up = jnp.zeros((planes, cx), F32)
    down = up
    for a in range(2):
        for j, s in enumerate(received(left_ref, right_ref, a, planes // 2, cy)):
            at = 3 * (4 * a + j)
            here = (lane >= at) & (lane < at + 3)
            up = jnp.where(here, turn(s, at - (OFF + cy - 3), 1), up)
            down = jnp.where(here, turn(s, at - OFF, 1), down)
    up_ref[6] = up
    down_ref[6] = down
    copy.wait()


def explicit_kernel(
    p_ref, m_ref, own_l_ref, own_r_ref, left_ref, right_ref, up_ref, down_ref,
    send_hbm, fz_ref, fy_ref, fx_ref, edge_ref,
    v_ref, c_ref, f_ref, side_ref, rim_ref, turned_ref, gy_ref, quarter_ref, sems,
):
    planes, cy, cx = p_ref.shape
    pairs = planes // 2
    tall = cy + 2 * OFF
    lane = places((planes, cx), 1)
    plane = places((planes, cx), 0)

    def strips(a):
        out = []
        for j, s in enumerate(received(left_ref, right_ref, a, pairs, cy)):
            at = 3 * (4 * a + j)
            s = jnp.where((lane >= OFF - 3) & (lane < OFF), turn(up_ref[6], OFF - 3 - at, 1), s)
            s = jnp.where((lane >= OFF + cy) & (lane < OFF + cy + 3), turn(down_ref[6], OFF + cy - at, 1), s)
            out.append(s)
        own = []
        for ref, j, at in ((own_l_ref, 0, 0), (own_l_ref, 1, 1), (own_r_ref, 0, cx - 2), (own_r_ref, 1, cx - 1)):
            k = 2 * a + j
            s = strip(ref[k * pairs : (k + 1) * pairs, :], cy)
            for r in (1, 2):
                s = jnp.where(lane == OFF - 3 + r, turn(up_ref[3 * a + r], OFF - 3 + r - at, 1), s)
            for r in (0, 1):
                s = jnp.where(lane == OFF + cy + r, turn(down_ref[3 * a + r], OFF + cy + r - at, 1), s)
            own.append(s)
        return out[:2] + own[:2], own[2:] + out[2:]

    def strip_first(v, m, vl, ml, vr, mr):
        above = jnp.where(plane == planes - 1, 0.0, turn(m, -1, 0))
        fz = face_mob(m, above)
        gz = fz * (turn(v, -1, 0) - v)
        fy = face_mob(m, turn(m, -1, 1))
        gy = fy * (turn(v, -1, 1) - v)
        lap = gz - jnp.where(plane == 0, 0.0, turn(gz, 1, 0)) + gy - turn(gy, 1, 1)
        lap = lap + face_mob(m, mr) * (vr - v) + face_mob(m, ml) * (vl - v)
        return v + step_size * lap

    turned_ref[...] = jnp.zeros(turned_ref.shape, F32)
    for side, (v, m) in enumerate(zip(strips(0), strips(1), strict=True)):
        f = face_mob(m[1], m[2])
        a = strip_first(v[1], m[1], v[0], m[0], v[2], m[2])
        b = strip_first(v[2], m[2], v[1], m[1], v[3], m[3])
        turned_ref[pl.ds(2 - side, planes, stride=2), :] = f * (v[2] - v[1])
        turned_ref[pl.ds(66 - side, planes, stride=2), :] = f * (b - a)
        side_ref[...] = f
        even = turn(side_ref[pl.ds(0, pairs, stride=2), :], -OFF, 1)
        odd = turn(side_ref[pl.ds(1, pairs, stride=2), :], cy - OFF, 1)
        edge_ref[side * pairs : (side + 1) * pairs, :] = jnp.where(lane[:pairs] < cy, even, odd)
    across = turned_ref[...].T
    part = tall // 2

    def ends(k, z, h):
        return turn(across[h * part : (h + 1) * part], -(64 * k + 2 * z + 2), 1)

    blank = jnp.zeros((OFF, cx), F32)
    for ref in (v_ref, c_ref, f_ref):
        for z in (0, planes + 1):
            ref[z * tall : (z + 1) * tall, :] = jnp.zeros((tall, cx), F32)
    for ref, a, field in ((v_ref, 0, p_ref), (c_ref, 1, m_ref)):
        for z in range(planes):
            base = (z + 1) * tall
            ref[base : base + OFF, :] = blank
            ref[base + OFF : base + OFF + cy, :] = field[z]
            ref[base + OFF + cy : base + tall, :] = blank
        for r in range(3):
            ref[pl.ds(tall + OFF - 3 + r, planes, stride=tall), :] = up_ref[3 * a + r]
            ref[pl.ds(tall + OFF + cy + r, planes, stride=tall), :] = down_ref[3 * a + r]

    wide = places((part, cx), 1)

    def step(ref, z, h, fz, fy, fx, gz_before, end):
        at = (z + 1) * tall + h * part
        v = ref[at : at + part, :]
        gz = fz * (ref[at + tall : at + tall + part, :] - v)
        gy = fy * (ref[at + 1 : at + 1 + part, :] - v)
        flat = OFF + z * tall + h * part
        gy_ref[flat : flat + part, :] = gy
        gu = gy_ref[flat - 1 : flat - 1 + part, :]
        gx = jnp.where(wide == 0, end, fx * (v - turn(v, 1, 1)))
        lap = gz - gz_before + gy - gu + jnp.where(wide == cx - 1, end, turn(gx, -1, 1)) - gx
        return v + step_size * lap, gz

    fz_ref[:tall, :] = jnp.zeros((tall, cx), F32)
    fy_ref[:OFF, :] = jnp.zeros((OFF, cx), F32)
    gy_ref[:OFF, :] = jnp.zeros((OFF, cx), F32)
    for h in range(2):
        before = jnp.zeros((part, cx), F32)
        for z in range(planes):
            at = (z + 1) * tall + h * part
            flat = z * tall + h * part
            m = c_ref[at : at + part, :]
            fz = face_mob(m, c_ref[at + tall : at + tall + part, :])
            fy = face_mob(m, c_ref[at + 1 : at + 1 + part, :])
            fx = face_mob(m, turn(m, 1, 1))
            fz_ref[at : at + part, :] = fz
            fy_ref[OFF + flat : OFF + flat + part, :] = fy
            fx_ref[flat : flat + part, :] = fx
            out, before = step(v_ref, z, h, fz, fy, fx, before, ends(0, z, h))
            f_ref[at : at + part, :] = out

    rim_ref[...] = jnp.zeros(rim_ref.shape, F32)
    quarter = planes // 4
    before = [jnp.zeros((part, cx), F32)] * 2
    copies = []
    for z in range(planes):
        q, row = z // quarter, z % quarter
        outs = []
        for h in range(2):
            at = (z + 1) * tall + h * part
            flat = z * tall + h * part
            out, before[h] = step(
                f_ref, z, h, fz_ref[at : at + part, :], fy_ref[OFF + flat : OFF + flat + part, :],
                fx_ref[flat : flat + part, :], before[h], ends(1, z, h),
            )
            outs.append(out)
        out = jnp.concatenate(outs, axis=0)
        quarter_ref[q, row * cy : (row + 1) * cy, :] = out[OFF : OFF + cy].astype(BF16)
        rim_ref[q, 2 * row : 2 * row + 1, :] = out[OFF - 1 : OFF]
        rim_ref[q, 2 * row + 1 : 2 * row + 2, :] = out[OFF + cy : OFF + cy + 1]
        if row == quarter - 1:
            quarter_ref[q, quarter * cy :, :] = rim_ref[q].astype(BF16)
            for x in range(4):
                to = send_hbm.at[(q // 2) * 8 + x * 2 + q % 2]
                copies.append(pltpu.make_async_copy(quarter_ref.at[q], to, sems.at[q, x]))
                copies[-1].start()
    for copy in copies:
        copy.wait()


def solve_x_kernel(block_ref, got_ref, x0_hbm, x1_hbm, x2_hbm, x3_hbm, out_ref, x0_ref, x1_ref, x2_ref, x3_ref, sems):
    own = block_ref[0]
    parts, lines, cx = got_ref.shape
    main = lines - 16
    moves = ((x0_hbm, x0_ref), (x1_hbm, x1_ref), (x2_hbm, x2_ref), (x3_hbm, x3_ref))
    copies = [pltpu.make_async_copy(src, dst, sems.at[i]) for i, (src, dst) in enumerate(moves)]
    for copy in copies:
        copy.start()
    a = jnp.concatenate([got_ref[s] for s in range(parts)], axis=1)
    for other, x_ref in enumerate((x0_ref, x1_ref, x2_ref, x3_ref)):
        copies[other].wait()
        block = own ^ other
        m = lax.dot_general(a, x_ref[:cx], NT, preferred_element_type=F32)
        out_ref[block, : main + 8] = m[: main + 8]
        e = lax.dot_general(x_ref[cx:], a[:main], NT, preferred_element_type=F32)
        out_ref[block, main + 8 : main + 12] = e[:4, :cx]
        out_ref[block, main + 12 :] = e[:4, cx:]


def implicit_kernel(back_ref, fz_ref, fy_ref, fx_ref, edge_ref, out_ref, c_ref, e_ref):
    planes, cy, cx = out_ref.shape
    tall = cy + 2 * OFF
    quarter, pairs = planes // 4, planes // 2
    main = quarter * cy

    def chemical(s):
        return s * s * s - s

    for z in (0, planes + 1):
        c_ref[z * tall : (z + 1) * tall, :] = jnp.zeros((tall, cx), F32)
    for q in range(4):
        e_ref[q * 8 : (q + 1) * 8, :] = chemical(back_ref[q, main + 8 : main + 16])
        rims = chemical(back_ref[q, main : main + 8])
        for at in range(quarter):
            base = (q * quarter + at + 1) * tall
            c_ref[base + OFF : base + OFF + cy, :] = chemical(back_ref[q, at * cy : (at + 1) * cy])
            c_ref[base + OFF - 1 : base + OFF, :] = rims[2 * at : 2 * at + 1]
            c_ref[base + OFF + cy : base + OFF + cy + 1, :] = rims[2 * at + 1 : 2 * at + 2]
    ends = [e_ref[pl.ds(j, pairs, stride=4), :] for j in range(4)]
    left = edge_ref[:pairs, :] * (ends[1] - ends[0])
    right = edge_ref[pairs:, :] * (ends[3] - ends[2])
    across = jnp.concatenate([left, right, jnp.zeros((cx - planes, cx), F32)], axis=0).T
    lane = places((cy, cx), 1)
    before = jnp.zeros((cy, cx), F32)
    for z in range(planes):
        base = (z + 1) * tall + OFF
        flat = z * tall + OFF
        c = c_ref[base : base + cy, :]
        gz = fz_ref[base : base + cy, :] * (c_ref[base + tall : base + tall + cy, :] - c)
        gy = fy_ref[flat + OFF : flat + OFF + cy, :] * (c_ref[base + 1 : base + 1 + cy, :] - c)
        gu = fy_ref[flat + OFF - 1 : flat + OFF - 1 + cy, :] * (c - c_ref[base - 1 : base - 1 + cy, :])
        rows = slice((z % 2) * cy, (z % 2 + 1) * cy)
        gl = jnp.broadcast_to(across[rows, z // 2 : z // 2 + 1], (cy, cx))
        gr = jnp.broadcast_to(across[rows, pairs + z // 2 : pairs + z // 2 + 1], (cy, cx))
        gx = jnp.where(lane == 0, gl, fx_ref[flat : flat + cy, :] * (c - turn(c, 1, 1)))
        lap = gz - before + gy - gu + jnp.where(lane == cx - 1, gr, turn(gx, -1, 1)) - gx
        s = back_ref[z // quarter, (z % quarter) * cy : (z % quarter + 1) * cy]
        out_ref[z] = (s + step_size * lap).astype(BF16)
        before = gz


def solve_y_near_kernel(side_ref, y_hbm, u_ref, sum_ref, y_ref, near_ref, sems):
    high = side_ref[0]
    half, _ = u_ref.shape
    halves = (high, 1 - high)
    columns = [y_hbm.at[:, pl.ds(pl.multiple_of(h * half, half), half)] for h in halves]
    copies = [pltpu.make_async_copy(c, ref, sems.at[i]) for i, (c, ref) in enumerate(zip(columns, (near_ref, y_ref), strict=True))]
    for copy in copies:
        copy.start()
    copies[0].wait()
    sum_ref[...] = jnp.dot(near_ref[...], u_ref[...], preferred_element_type=F32)
    copies[1].wait()


def solve_y_far_kernel(sum_ref, y_ref, u_ref, out_ref):
    total = sum_ref[...] + jnp.dot(y_ref[...], u_ref[...], preferred_element_type=F32)
    out_ref[...] = total.astype(BF16)


def pack_x(core, p, m, x_inverse, y_inverse):
    cx = p.shape[2]
    shape = (2 * p.shape[0] + 16, cx)
    cy, order = y_inverse.shape
    out = (kept(shape, F32),) * 2 + (kept(p.shape, F32),) * 2 + (away_kept((cx + 16, order), BF16),)
    out += (away_kept((cy // 2, order), BF16),)
    scratch = (pltpu.VMEM((cx, order), BF16), pltpu.VMEM((cy // 2, order), BF16), pltpu.SemaphoreType.DMA((4,)))
    return call(pack_x_kernel, out, (p, m, x_inverse, y_inverse), core, scratch, range(4), (4, 5))


def pack_y(p, m, own_l, own_r, left, right, rows):
    order = rows.shape[1]
    out = (kept((7, p.shape[0], p.shape[2]), F32),) * 2 + (away_kept(rows.shape, BF16),)
    scratch = (pltpu.VMEM((16, order), F32), pltpu.VMEM((16, order), BF16), pltpu.SemaphoreType.DMA(()))
    args = (p, m, own_l, own_r, left, right, rows)
    return call(pack_y_kernel, out, args, scratch=scratch, far=(6,), far_out=(2,), aliases={6: 2})


def explicit(*args):
    planes, cy, cx = args[0].shape
    tall = cy + 2 * OFF
    lines = planes // 4 * cy + 16
    field = pltpu.VMEM(((planes + 2) * tall, cx), F32)
    out = (
        away_kept((16, lines, cx), BF16),
        kept(((planes + 1) * tall, cx), F32),
        kept((planes * tall + OFF, cx), F32),
        kept((planes * tall, cx), F32),
        kept((planes, cx), F32),
    )
    scratch = (field, field, field, pltpu.VMEM((planes, cx), F32))
    scratch += (pltpu.VMEM((4, 16, cx), F32), pltpu.VMEM((cx, cx), F32))
    scratch += (pltpu.VMEM((planes * tall + OFF, cx), F32), pltpu.VMEM((4, lines, cx), BF16), pltpu.SemaphoreType.DMA((4, 4)))
    return call(explicit_kernel, out, args, scratch=scratch, far_out=(0,))


def solve_x(block, got, x_blocks):
    _, lines, cx = got.shape
    blocks = pltpu.VMEM(x_blocks[0].shape, BF16)
    scratch = (blocks,) * 4 + (pltpu.SemaphoreType.DMA((4,)),)
    return call(solve_x_kernel, kept((4, lines, cx), F32), (got, *x_blocks), block, scratch, (1, 2, 3, 4))


def implicit(back, faces, planes, cy):
    cx = back.shape[2]
    tall = cy + 2 * OFF
    scratch = (pltpu.VMEM(((planes + 2) * tall, cx), F32), pltpu.VMEM((32, cx), F32))
    return call(implicit_kernel, kept((planes, cy, cx), BF16), (back, *faces), scratch=scratch)


def solve_y_near(side, y, u):
    half, cx = u.shape
    out = (kept((half, cx), F32), kept((half, half), BF16))
    scratch = (pltpu.VMEM((half, half), BF16), pltpu.SemaphoreType.DMA((2,)))
    return call(solve_y_near_kernel, out, (y, u), side, scratch, (0,))


def solve_y_far(*parts):
    return call(solve_y_far_kernel, kept(parts[-1].shape, BF16), parts)


def both_ways(to_before, to_after, axis):
    size = lax.axis_size(axis)
    up = [(i, i + 1) for i in range(size - 1)]
    return lax.ppermute(to_after, axis, up), lax.ppermute(to_before, axis, [(j, i) for i, j in up])


def local(phase_field, mobility, x_inverse, y_inverse):
    planes, cy, cx = phase_field.shape
    order = y_inverse.shape[1]
    half = order // 2
    core, low, high = lax.axis_index("c"), lax.axis_index("yl"), lax.axis_index("yh")
    swap = [(0, 1), (1, 0)]

    one = lambda v: v.reshape(1).astype(jnp.int32)

    own_l, own_r, phase_field, mobility, rows, y_part = pack_x(one(core), phase_field, mobility, x_inverse, y_inverse)
    y_rows = lax.all_gather(y_part, ("z", "c"), axis=0, tiled=True)
    left, right = both_ways(own_l, own_r, GX)
    to_up, to_down, rows = pack_y(phase_field, mobility, own_l, own_r, left, right, rows)
    up, down = both_ways(to_down, to_up, GY)
    rows_yl = lax.ppermute(rows, "yl", swap)
    x_blocks = (rows, lax.ppermute(rows, "c", swap), rows_yl, lax.ppermute(rows_yl, "c", swap))

    send, *faces = explicit(phase_field, mobility, own_l, own_r, left, right, up, down)
    got = lax.all_to_all(send, GX, 0, 0, tiled=True)
    back = solve_x(one(low * 2 + core), got, x_blocks)
    back = lax.all_to_all(back, ("yl", "c"), 0, 0, tiled=True)
    updated = implicit(back, faces, planes, cy)

    mine = lax.all_to_all(updated, "z", 0, 0, tiled=True).reshape(half, cx)
    y_rows, mine = lax.optimization_barrier((y_rows, mine))
    theirs = lax.ppermute(mine, "yh", swap)
    part, y_far = solve_y_near(one(high), y_rows, mine)
    out = solve_y_far(part, y_far, theirs).reshape(16, cy, cx)
    out = lax.all_to_all(out, "z", 0, 0, tiled=True)
    return out.astype(F32)


def solution(mesh):
    shape = (2, mesh.shape["gx"] // 4, 2, 2, mesh.shape["gy"] // 2)
    torus = Mesh(mesh.devices.reshape(shape), ("yl", "x", "c", "yh", "z"))
    in_specs = (P(None, GY, GX), P(None, GY, GX), P(GX, None), P(GY, None))
    return jax.shard_map(local, mesh=torus, in_specs=in_specs, out_specs=P(None, GY, GX), check_vma=False)
```

```python
import jax
import jax.numpy as jnp
from jax import lax
from jax.experimental import pallas as pl
from jax.experimental.pallas import tpu as pltpu
from jax.sharding import Mesh
from jax.sharding import PartitionSpec as P

GX = ("yl", "x", "c")
GY = ("yh", "z")

step_size = 0.15
F32 = jnp.float32
BF16 = jnp.bfloat16
NT = (((1,), (1,)), ((), ()))
VMEM = pl.BlockSpec(memory_space=pltpu.VMEM)
OFF = 8


def near(v):
    return pltpu.with_memory_space_constraint(v, pltpu.VMEM)


def away(v):
    return pltpu.with_memory_space_constraint(v, pltpu.HBM)


def kept(shape, dtype):
    return pltpu.VMEM(shape, dtype)


FAR = pl.BlockSpec(memory_space=pltpu.HBM)


def away_kept(shape, dtype):
    return pltpu.HBM(shape, dtype)


def call(kernel, out_shape, args, scalar=None, scratch=(), far=(), far_out=(), aliases=None):
    scalars = [] if scalar is None else [scalar]
    many = isinstance(out_shape, tuple)
    return pl.pallas_call(
        kernel,
        out_shape=out_shape,
        in_specs=[pl.BlockSpec(memory_space=pltpu.SMEM)] * len(scalars) + [FAR if i in far else VMEM for i in range(len(args))],
        out_specs=tuple(FAR if i in far_out else VMEM for i in range(len(out_shape))) if many else VMEM,
        scratch_shapes=list(scratch),
        input_output_aliases=aliases or {},
        compiler_params=pltpu.CompilerParams(vmem_limit_bytes=16 << 20),
    )(*scalars, *[away(v) if i in far else near(v) for i, v in enumerate(args)])


def face_mob(p, q):
    return 2.0 * p * q / jnp.maximum(p + q, 0.25)


def turn(x, shift, axis):
    return pltpu.roll(x, shift % x.shape[axis], axis)


def places(shape, axis):
    return lax.broadcasted_iota(jnp.int32, shape, axis)


def pack_x_kernel(core_ref, p_hbm, m_hbm, x_hbm, y_hbm, left_ref, right_ref, p_ref, m_ref, rows_hbm, part_hbm, x_ref, part_ref, sems):
    planes, _, cx = p_ref.shape
    pairs = planes // 2
    rows = part_hbm.shape[0]
    copies = (
        (y_hbm.at[pl.ds(pl.multiple_of(core_ref[0] * rows, rows), rows)], part_ref),
        (p_hbm, p_ref),
        (m_hbm, m_ref),
        (x_hbm, x_ref),
    )
    copies = [pltpu.make_async_copy(src, dst, sems.at[i]) for i, (src, dst) in enumerate(copies)]
    for copy in copies:
        copy.start()
    copies[0].wait()
    out = pltpu.make_async_copy(part_ref, part_hbm, sems.at[0])
    out.start()
    copies[3].wait()
    own = pltpu.make_async_copy(x_ref, rows_hbm.at[pl.ds(0, cx)], sems.at[3])
    own.start()
    for a, ref in enumerate((p_ref, m_ref)):
        copies[1 + a].wait()
        for i in range(pairs):
            t = jnp.concatenate([ref[i], ref[i + pairs]], axis=0).T
            for j in range(2):
                k = (2 * a + j) * pairs + i
                left_ref[k : k + 1, :] = t[j : j + 1]
                right_ref[k : k + 1, :] = t[cx - 2 + j : cx - 1 + j]
    base = 4 * pairs
    first = x_ref[0:16, :][0:1].astype(F32)
    last = x_ref[cx - 16 : cx, :][15:16].astype(F32)
    for s in range(16):
        left_ref[base + s : base + s + 1, :] = first[:, s * cx : (s + 1) * cx]
        right_ref[base + s : base + s + 1, :] = last[:, s * cx : (s + 1) * cx]
    out.wait()
    own.wait()


def strip(x, cy):
    both = jnp.concatenate([turn(x, OFF, 1), turn(x, OFF - cy, 1)], axis=0)
    lane = places(both.shape, 1)
    return jnp.where((lane >= OFF) & (lane < OFF + cy), both, 0.0)


def received(left_ref, right_ref, a, pairs, cy):
    refs = ((left_ref, 2 * a), (left_ref, 2 * a + 1), (right_ref, 2 * a), (right_ref, 2 * a + 1))
    return [strip(ref[k * pairs : (k + 1) * pairs, :], cy) for ref, k in refs]


def pack_y_kernel(
    p_ref, m_ref, own_l_ref, own_r_ref, left_ref, right_ref, _, up_ref, down_ref, rows_hbm, row_ref, cast_ref, sem
):
    planes, cy, cx = p_ref.shape
    base = left_ref.shape[0] - 16
    row_ref[...] = jnp.zeros(row_ref.shape, F32)
    for j, ref in enumerate((left_ref, own_l_ref, own_r_ref, right_ref)):
        for s in range(16):
            row_ref[j : j + 1, s * cx : (s + 1) * cx] = ref[base + s : base + s + 1, :]
    cast_ref[...] = row_ref[...].astype(BF16)
    copy = pltpu.make_async_copy(cast_ref, rows_hbm.at[pl.ds(cx, 16)], sem)
    copy.start()
    for a, ref in enumerate((p_ref, m_ref)):
        for r in range(3):
            up_ref[3 * a + r] = ref[:, cy - 3 + r, :]
            down_ref[3 * a + r] = ref[:, r, :]
    lane = places((planes, cx), 1)
    up = jnp.zeros((planes, cx), F32)
    down = up
    for a in range(2):
        for j, s in enumerate(received(left_ref, right_ref, a, planes // 2, cy)):
            at = 3 * (4 * a + j)
            here = (lane >= at) & (lane < at + 3)
            up = jnp.where(here, turn(s, at - (OFF + cy - 3), 1), up)
            down = jnp.where(here, turn(s, at - OFF, 1), down)
    up_ref[6] = up
    down_ref[6] = down
    copy.wait()


def explicit_kernel(
    p_ref, m_ref, own_l_ref, own_r_ref, left_ref, right_ref, up_ref, down_ref,
    send_hbm, fz_ref, fy_ref, fx_ref, edge_ref,
    v_ref, c_ref, f_ref, side_ref, rim_ref, turned_ref, quarter_ref, sems,
):
    planes, cy, cx = p_ref.shape
    pairs = planes // 2
    tall = cy + 2 * OFF
    lane = places((planes, cx), 1)
    plane = places((planes, cx), 0)

    def strips(a):
        out = []
        for j, s in enumerate(received(left_ref, right_ref, a, pairs, cy)):
            at = 3 * (4 * a + j)
            s = jnp.where((lane >= OFF - 3) & (lane < OFF), turn(up_ref[6], OFF - 3 - at, 1), s)
            s = jnp.where((lane >= OFF + cy) & (lane < OFF + cy + 3), turn(down_ref[6], OFF + cy - at, 1), s)
            out.append(s)
        own = []
        for ref, j, at in ((own_l_ref, 0, 0), (own_l_ref, 1, 1), (own_r_ref, 0, cx - 2), (own_r_ref, 1, cx - 1)):
            k = 2 * a + j
            s = strip(ref[k * pairs : (k + 1) * pairs, :], cy)
            for r in (1, 2):
                s = jnp.where(lane == OFF - 3 + r, turn(up_ref[3 * a + r], OFF - 3 + r - at, 1), s)
            for r in (0, 1):
                s = jnp.where(lane == OFF + cy + r, turn(down_ref[3 * a + r], OFF + cy + r - at, 1), s)
            own.append(s)
        return out[:2] + own[:2], own[2:] + out[2:]

    def strip_first(v, m, vl, ml, vr, mr):
        above = jnp.where(plane == planes - 1, 0.0, turn(m, -1, 0))
        fz = face_mob(m, above)
        gz = fz * (turn(v, -1, 0) - v)
        fy = face_mob(m, turn(m, -1, 1))
        gy = fy * (turn(v, -1, 1) - v)
        lap = gz - jnp.where(plane == 0, 0.0, turn(gz, 1, 0)) + gy - turn(gy, 1, 1)
        lap = lap + face_mob(m, mr) * (vr - v) + face_mob(m, ml) * (vl - v)
        return v + step_size * lap

    turned_ref[...] = jnp.zeros(turned_ref.shape, F32)
    for side, (v, m) in enumerate(zip(strips(0), strips(1), strict=True)):
        f = face_mob(m[1], m[2])
        a = strip_first(v[1], m[1], v[0], m[0], v[2], m[2])
        b = strip_first(v[2], m[2], v[1], m[1], v[3], m[3])
        turned_ref[pl.ds(2 - side, planes, stride=2), :] = f * (v[2] - v[1])
        turned_ref[pl.ds(66 - side, planes, stride=2), :] = f * (b - a)
        side_ref[...] = f
        even = turn(side_ref[pl.ds(0, pairs, stride=2), :], -OFF, 1)
        odd = turn(side_ref[pl.ds(1, pairs, stride=2), :], cy - OFF, 1)
        edge_ref[side * pairs : (side + 1) * pairs, :] = jnp.where(lane[:pairs] < cy, even, odd)
    across = turned_ref[...].T

    def ends(k, z):
        return turn(across[:tall], -(64 * k + 2 * z + 2), 1)

    blank = jnp.zeros((OFF, cx), F32)
    for ref in (v_ref, c_ref, f_ref):
        for z in (0, planes + 1):
            ref[z * tall : (z + 1) * tall, :] = jnp.zeros((tall, cx), F32)
    for ref, a, field in ((v_ref, 0, p_ref), (c_ref, 1, m_ref)):
        for z in range(planes):
            base = (z + 1) * tall
            ref[base : base + OFF, :] = blank
            ref[base + OFF : base + OFF + cy, :] = field[z]
            ref[base + OFF + cy : base + tall, :] = blank
        for r in range(3):
            ref[pl.ds(tall + OFF - 3 + r, planes, stride=tall), :] = up_ref[3 * a + r]
            ref[pl.ds(tall + OFF + cy + r, planes, stride=tall), :] = down_ref[3 * a + r]

    wide = places((tall, cx), 1)

    def step(v, above, fz, fy, fx, gz_before, end):
        gz = fz * (above - v)
        gy = fy * (turn(v, -1, 0) - v)
        gx = jnp.where(wide == 0, end, fx * (v - turn(v, 1, 1)))
        lap = gz - gz_before + gy - turn(gy, 1, 0)
        lap = lap + jnp.where(wide == cx - 1, end, turn(gx, -1, 1)) - gx
        return v + step_size * lap, gz

    fz_ref[:tall, :] = jnp.zeros((tall, cx), F32)
    fy_ref[:OFF, :] = jnp.zeros((OFF, cx), F32)
    before = jnp.zeros((tall, cx), F32)
    for z in range(planes):
        here, above = pl.ds((z + 1) * tall, tall), pl.ds((z + 2) * tall, tall)
        m = c_ref[here, :]
        fz = face_mob(m, c_ref[above, :])
        fy = face_mob(m, turn(m, -1, 0))
        fx = face_mob(m, turn(m, 1, 1))
        fz_ref[here, :] = fz
        fy_ref[pl.ds(OFF + z * tall, tall), :] = fy
        fx_ref[pl.ds(z * tall, tall), :] = fx
        out, before = step(v_ref[here, :], v_ref[above, :], fz, fy, fx, before, ends(0, z))
        f_ref[here, :] = out

    rim_ref[...] = jnp.zeros(rim_ref.shape, F32)
    quarter = planes // 4
    before = jnp.zeros((tall, cx), F32)
    copies = []
    for z in range(planes):
        here, above = pl.ds((z + 1) * tall, tall), pl.ds((z + 2) * tall, tall)
        fy, fx = fy_ref[pl.ds(OFF + z * tall, tall), :], fx_ref[pl.ds(z * tall, tall), :]
        out, before = step(f_ref[here, :], f_ref[above, :], fz_ref[here, :], fy, fx, before, ends(1, z))
        q, row = z // quarter, z % quarter
        quarter_ref[q, row * cy : (row + 1) * cy, :] = out[OFF : OFF + cy].astype(BF16)
        rim_ref[q, 2 * row : 2 * row + 1, :] = out[OFF - 1 : OFF]
        rim_ref[q, 2 * row + 1 : 2 * row + 2, :] = out[OFF + cy : OFF + cy + 1]
        if row == quarter - 1:
            quarter_ref[q, quarter * cy :, :] = rim_ref[q].astype(BF16)
            for x in range(4):
                to = send_hbm.at[(q // 2) * 8 + x * 2 + q % 2]
                copies.append(pltpu.make_async_copy(quarter_ref.at[q], to, sems.at[q, x]))
                copies[-1].start()
    for copy in copies:
        copy.wait()


def solve_x_kernel(block_ref, got_ref, x0_hbm, x1_hbm, x2_hbm, x3_hbm, out_ref, x0_ref, x1_ref, x2_ref, x3_ref, sems):
    own = block_ref[0]
    parts, lines, cx = got_ref.shape
    main = lines - 16
    moves = ((x0_hbm, x0_ref), (x1_hbm, x1_ref), (x2_hbm, x2_ref), (x3_hbm, x3_ref))
    copies = [pltpu.make_async_copy(src, dst, sems.at[i]) for i, (src, dst) in enumerate(moves)]
    for copy in copies:
        copy.start()
    a = jnp.concatenate([got_ref[s] for s in range(parts)], axis=1)
    for copy in copies:
        copy.wait()
    for other, x_ref in enumerate((x0_ref, x1_ref, x2_ref, x3_ref)):
        block = own ^ other
        m = lax.dot_general(a, x_ref[:cx], NT, preferred_element_type=F32)
        out_ref[block, : main + 8] = m[: main + 8]
        e = lax.dot_general(x_ref[cx:], a[:main], NT, preferred_element_type=F32)
        out_ref[block, main + 8 : main + 12] = e[:4, :cx]
        out_ref[block, main + 12 :] = e[:4, cx:]


def implicit_kernel(back_ref, fz_ref, fy_ref, fx_ref, edge_ref, out_ref, c_ref, e_ref):
    planes, cy, cx = out_ref.shape
    tall = cy + 2 * OFF
    quarter, pairs = planes // 4, planes // 2
    main = quarter * cy

    def chemical(s):
        return s * s * s - s

    for z in (0, planes + 1):
        c_ref[z * tall : (z + 1) * tall, :] = jnp.zeros((tall, cx), F32)
    for q in range(4):
        e_ref[q * 8 : (q + 1) * 8, :] = chemical(back_ref[q, main + 8 : main + 16])
        rims = chemical(back_ref[q, main : main + 8])
        for at in range(quarter):
            base = (q * quarter + at + 1) * tall
            c_ref[base + OFF : base + OFF + cy, :] = chemical(back_ref[q, at * cy : (at + 1) * cy])
            c_ref[base + OFF - 1 : base + OFF, :] = rims[2 * at : 2 * at + 1]
            c_ref[base + OFF + cy : base + OFF + cy + 1, :] = rims[2 * at + 1 : 2 * at + 2]
    ends = [e_ref[pl.ds(j, pairs, stride=4), :] for j in range(4)]
    left = edge_ref[:pairs, :] * (ends[1] - ends[0])
    right = edge_ref[pairs:, :] * (ends[3] - ends[2])
    across = jnp.concatenate([left, right, jnp.zeros((cx - planes, cx), F32)], axis=0).T
    lane = places((cy, cx), 1)
    before = jnp.zeros((cy, cx), F32)
    for z in range(planes):
        base = (z + 1) * tall + OFF
        flat = z * tall + OFF
        c = c_ref[base : base + cy, :]
        gz = fz_ref[base : base + cy, :] * (c_ref[base + tall : base + tall + cy, :] - c)
        gy = fy_ref[flat + OFF : flat + OFF + cy, :] * (c_ref[base + 1 : base + 1 + cy, :] - c)
        gu = fy_ref[flat + OFF - 1 : flat + OFF - 1 + cy, :] * (c - c_ref[base - 1 : base - 1 + cy, :])
        rows = slice((z % 2) * cy, (z % 2 + 1) * cy)
        gl = jnp.broadcast_to(across[rows, z // 2 : z // 2 + 1], (cy, cx))
        gr = jnp.broadcast_to(across[rows, pairs + z // 2 : pairs + z // 2 + 1], (cy, cx))
        gx = jnp.where(lane == 0, gl, fx_ref[flat : flat + cy, :] * (c - turn(c, 1, 1)))
        lap = gz - before + gy - gu + jnp.where(lane == cx - 1, gr, turn(gx, -1, 1)) - gx
        s = back_ref[z // quarter, (z % quarter) * cy : (z % quarter + 1) * cy]
        out_ref[z] = (s + step_size * lap).astype(BF16)
        before = gz


def solve_y_near_kernel(side_ref, y_hbm, u_ref, sum_ref, y_ref, near_ref, sems):
    high = side_ref[0]
    half, _ = u_ref.shape
    halves = (high, 1 - high)
    columns = [y_hbm.at[:, pl.ds(pl.multiple_of(h * half, half), half)] for h in halves]
    copies = [pltpu.make_async_copy(c, ref, sems.at[i]) for i, (c, ref) in enumerate(zip(columns, (near_ref, y_ref), strict=True))]
    for copy in copies:
        copy.start()
    copies[0].wait()
    sum_ref[...] = jnp.dot(near_ref[...], u_ref[...], preferred_element_type=F32)
    copies[1].wait()


def solve_y_far_kernel(sum_ref, y_ref, u_ref, out_ref):
    total = sum_ref[...] + jnp.dot(y_ref[...], u_ref[...], preferred_element_type=F32)
    out_ref[...] = total.astype(BF16)


def pack_x(core, p, m, x_inverse, y_inverse):
    cx = p.shape[2]
    shape = (2 * p.shape[0] + 16, cx)
    cy, order = y_inverse.shape
    out = (kept(shape, F32),) * 2 + (kept(p.shape, F32),) * 2 + (away_kept((cx + 16, order), BF16),)
    out += (away_kept((cy // 2, order), BF16),)
    scratch = (pltpu.VMEM((cx, order), BF16), pltpu.VMEM((cy // 2, order), BF16), pltpu.SemaphoreType.DMA((4,)))
    return call(pack_x_kernel, out, (p, m, x_inverse, y_inverse), core, scratch, range(4), (4, 5))


def pack_y(p, m, own_l, own_r, left, right, rows):
    order = rows.shape[1]
    out = (kept((7, p.shape[0], p.shape[2]), F32),) * 2 + (away_kept(rows.shape, BF16),)
    scratch = (pltpu.VMEM((16, order), F32), pltpu.VMEM((16, order), BF16), pltpu.SemaphoreType.DMA(()))
    args = (p, m, own_l, own_r, left, right, rows)
    return call(pack_y_kernel, out, args, scratch=scratch, far=(6,), far_out=(2,), aliases={6: 2})


def explicit(*args):
    planes, cy, cx = args[0].shape
    tall = cy + 2 * OFF
    lines = planes // 4 * cy + 16
    field = pltpu.VMEM(((planes + 2) * tall, cx), F32)
    out = (
        away_kept((16, lines, cx), BF16),
        kept(((planes + 1) * tall, cx), F32),
        kept((planes * tall + OFF, cx), F32),
        kept((planes * tall, cx), F32),
        kept((planes, cx), F32),
    )
    scratch = (field, field, field, pltpu.VMEM((planes, cx), F32))
    scratch += (pltpu.VMEM((4, 16, cx), F32), pltpu.VMEM((cx, cx), F32))
    scratch += (pltpu.VMEM((4, lines, cx), BF16), pltpu.SemaphoreType.DMA((4, 4)))
    return call(explicit_kernel, out, args, scratch=scratch, far_out=(0,))


def solve_x(block, got, x_blocks):
    _, lines, cx = got.shape
    blocks = pltpu.VMEM(x_blocks[0].shape, BF16)
    scratch = (blocks,) * 4 + (pltpu.SemaphoreType.DMA((4,)),)
    return call(solve_x_kernel, kept((4, lines, cx), F32), (got, *x_blocks), block, scratch, (1, 2, 3, 4))


def implicit(back, faces, planes, cy):
    cx = back.shape[2]
    tall = cy + 2 * OFF
    scratch = (pltpu.VMEM(((planes + 2) * tall, cx), F32), pltpu.VMEM((32, cx), F32))
    return call(implicit_kernel, kept((planes, cy, cx), BF16), (back, *faces), scratch=scratch)


def solve_y_near(side, y, u):
    half, cx = u.shape
    out = (kept((half, cx), F32), kept((half, half), BF16))
    scratch = (pltpu.VMEM((half, half), BF16), pltpu.SemaphoreType.DMA((2,)))
    return call(solve_y_near_kernel, out, (y, u), side, scratch, (0,))


def solve_y_far(*parts):
    return call(solve_y_far_kernel, kept(parts[-1].shape, BF16), parts)


def both_ways(to_before, to_after, axis):
    size = lax.axis_size(axis)
    up = [(i, i + 1) for i in range(size - 1)]
    return lax.ppermute(to_after, axis, up), lax.ppermute(to_before, axis, [(j, i) for i, j in up])


def local(phase_field, mobility, x_inverse, y_inverse):
    planes, cy, cx = phase_field.shape
    order = y_inverse.shape[1]
    half = order // 2
    core, low, high = lax.axis_index("c"), lax.axis_index("yl"), lax.axis_index("yh")
    swap = [(0, 1), (1, 0)]

    one = lambda v: v.reshape(1).astype(jnp.int32)

    own_l, own_r, phase_field, mobility, rows, y_part = pack_x(one(core), phase_field, mobility, x_inverse, y_inverse)
    y_rows = lax.all_gather(y_part, ("z", "c"), axis=0, tiled=True)
    left, right = both_ways(own_l, own_r, GX)
    to_up, to_down, rows = pack_y(phase_field, mobility, own_l, own_r, left, right, rows)
    up, down = both_ways(to_down, to_up, GY)
    rows_yl = lax.ppermute(rows, "yl", swap)
    x_blocks = (rows, lax.ppermute(rows, "c", swap), rows_yl, lax.ppermute(rows_yl, "c", swap))

    send, *faces = explicit(phase_field, mobility, own_l, own_r, left, right, up, down)
    got = lax.all_to_all(send, GX, 0, 0, tiled=True)
    back = solve_x(one(low * 2 + core), got, x_blocks)
    back = lax.all_to_all(back, ("yl", "c"), 0, 0, tiled=True)
    updated = implicit(back, faces, planes, cy)

    mine = lax.all_to_all(updated, "z", 0, 0, tiled=True).reshape(half, cx)
    y_rows, mine = lax.optimization_barrier((y_rows, mine))
    theirs = lax.ppermute(mine, "yh", swap)
    part, y_far = solve_y_near(one(high), y_rows, mine)
    out = solve_y_far(part, y_far, theirs).reshape(16, cy, cx)
    out = lax.all_to_all(out, "z", 0, 0, tiled=True)
    return out.astype(F32)


def solution(mesh):
    shape = (2, mesh.shape["gx"] // 4, 2, 2, mesh.shape["gy"] // 2)
    torus = Mesh(mesh.devices.reshape(shape), ("yl", "x", "c", "yh", "z"))
    in_specs = (P(None, GY, GX), P(None, GY, GX), P(GX, None), P(GY, None))
    return jax.shard_map(local, mesh=torus, in_specs=in_specs, out_specs=P(None, GY, GX), check_vma=False)
```

```python
import jax
import jax.numpy as jnp
from jax import lax
from jax.experimental import pallas as pl
from jax.experimental.pallas import tpu as pltpu
from jax.sharding import Mesh
from jax.sharding import PartitionSpec as P

GX = ("yl", "x", "c")
GY = ("yh", "z")

step_size = 0.15
F32 = jnp.float32
BF16 = jnp.bfloat16
NT = (((1,), (1,)), ((), ()))
VMEM = pl.BlockSpec(memory_space=pltpu.VMEM)
OFF = 8


def near(v):
    return pltpu.with_memory_space_constraint(v, pltpu.VMEM)


def away(v):
    return pltpu.with_memory_space_constraint(v, pltpu.HBM)


def kept(shape, dtype):
    return pltpu.VMEM(shape, dtype)


FAR = pl.BlockSpec(memory_space=pltpu.HBM)


def away_kept(shape, dtype):
    return pltpu.HBM(shape, dtype)


def call(kernel, out_shape, args, scalar=None, scratch=(), far=(), far_out=(), aliases=None):
    scalars = [] if scalar is None else [scalar]
    many = isinstance(out_shape, tuple)
    return pl.pallas_call(
        kernel,
        out_shape=out_shape,
        in_specs=[pl.BlockSpec(memory_space=pltpu.SMEM)] * len(scalars) + [FAR if i in far else VMEM for i in range(len(args))],
        out_specs=tuple(FAR if i in far_out else VMEM for i in range(len(out_shape))) if many else VMEM,
        scratch_shapes=list(scratch),
        input_output_aliases=aliases or {},
        compiler_params=pltpu.CompilerParams(vmem_limit_bytes=16 << 20),
    )(*scalars, *[away(v) if i in far else near(v) for i, v in enumerate(args)])


def face_mob(p, q):
    return 2.0 * p * q / jnp.maximum(p + q, 0.25)


def turn(x, shift, axis):
    return pltpu.roll(x, shift % x.shape[axis], axis)


def places(shape, axis):
    return lax.broadcasted_iota(jnp.int32, shape, axis)


def pack_x_kernel(core_ref, p_hbm, m_hbm, x_hbm, y_hbm, left_ref, right_ref, p_ref, m_ref, part_hbm, first_ref, last_ref, part_ref, sems):
    planes, _, cx = p_ref.shape
    pairs = planes // 2
    rows = part_hbm.shape[0]
    copies = (
        (y_hbm.at[pl.ds(pl.multiple_of(core_ref[0] * rows, rows), rows)], part_ref),
        (p_hbm, p_ref),
        (m_hbm, m_ref),
        (x_hbm.at[pl.ds(0, 16)], first_ref),
        (x_hbm.at[pl.ds(cx - 16, 16)], last_ref),
    )
    copies = [pltpu.make_async_copy(src, dst, sems.at[i]) for i, (src, dst) in enumerate(copies)]
    for copy in copies:
        copy.start()
    copies[0].wait()
    out = pltpu.make_async_copy(part_ref, part_hbm, sems.at[0])
    out.start()
    for a, ref in enumerate((p_ref, m_ref)):
        copies[1 + a].wait()
        for i in range(pairs):
            t = jnp.concatenate([ref[i], ref[i + pairs]], axis=0).T
            for j in range(2):
                k = (2 * a + j) * pairs + i
                left_ref[k : k + 1, :] = t[j : j + 1]
                right_ref[k : k + 1, :] = t[cx - 2 + j : cx - 1 + j]
    base = 4 * pairs
    copies[3].wait()
    copies[4].wait()
    first = first_ref[0:1, :].astype(F32)
    last = last_ref[15:16, :].astype(F32)
    for s in range(16):
        left_ref[base + s : base + s + 1, :] = first[:, s * cx : (s + 1) * cx]
        right_ref[base + s : base + s + 1, :] = last[:, s * cx : (s + 1) * cx]
    out.wait()


def strip(x, cy):
    both = jnp.concatenate([turn(x, OFF, 1), turn(x, OFF - cy, 1)], axis=0)
    lane = places(both.shape, 1)
    return jnp.where((lane >= OFF) & (lane < OFF + cy), both, 0.0)


def received(left_ref, right_ref, a, pairs, cy):
    refs = ((left_ref, 2 * a), (left_ref, 2 * a + 1), (right_ref, 2 * a), (right_ref, 2 * a + 1))
    return [strip(ref[k * pairs : (k + 1) * pairs, :], cy) for ref, k in refs]


def pack_rows_kernel(x_hbm, own_l_ref, own_r_ref, left_ref, right_ref, rows_hbm, row_ref, rows_ref, sem):
    cx = x_hbm.shape[0]
    come = pltpu.make_async_copy(x_hbm, rows_ref.at[pl.ds(0, cx)], sem)
    come.start()
    base = left_ref.shape[0] - 16
    row_ref[...] = jnp.zeros(row_ref.shape, F32)
    for j, ref in enumerate((left_ref, own_l_ref, own_r_ref, right_ref)):
        for s in range(16):
            row_ref[j : j + 1, s * 128 : (s + 1) * 128] = ref[base + s : base + s + 1, :]
    rows_ref[cx:] = row_ref[...].astype(BF16)
    come.wait()
    leave = pltpu.make_async_copy(rows_ref, rows_hbm, sem)
    leave.start()
    leave.wait()


def pack_y_kernel(p_ref, m_ref, left_ref, right_ref, up_ref, down_ref):
    planes, cy, cx = p_ref.shape
    for a, ref in enumerate((p_ref, m_ref)):
        for r in range(3):
            up_ref[3 * a + r] = ref[:, cy - 3 + r, :]
            down_ref[3 * a + r] = ref[:, r, :]
    lane = places((planes, cx), 1)
    up = jnp.zeros((planes, cx), F32)
    down = up
    for a in range(2):
        for j, s in enumerate(received(left_ref, right_ref, a, planes // 2, cy)):
            at = 3 * (4 * a + j)
            here = (lane >= at) & (lane < at + 3)
            up = jnp.where(here, turn(s, at - (OFF + cy - 3), 1), up)
            down = jnp.where(here, turn(s, at - OFF, 1), down)
    up_ref[6] = up
    down_ref[6] = down


def explicit_kernel(
    p_ref, m_ref, own_l_ref, own_r_ref, left_ref, right_ref, up_ref, down_ref,
    send_hbm, fz_ref, fy_ref, fx_ref, edge_ref,
    v_ref, c_ref, f_ref, side_ref, rim_ref, turned_ref, quarter_ref, sems,
):
    planes, cy, cx = p_ref.shape
    pairs = planes // 2
    tall = cy + 2 * OFF
    lane = places((planes, cx), 1)
    plane = places((planes, cx), 0)

    def strips(a):
        out = []
        for j, s in enumerate(received(left_ref, right_ref, a, pairs, cy)):
            at = 3 * (4 * a + j)
            s = jnp.where((lane >= OFF - 3) & (lane < OFF), turn(up_ref[6], OFF - 3 - at, 1), s)
            s = jnp.where((lane >= OFF + cy) & (lane < OFF + cy + 3), turn(down_ref[6], OFF + cy - at, 1), s)
            out.append(s)
        own = []
        for ref, j, at in ((own_l_ref, 0, 0), (own_l_ref, 1, 1), (own_r_ref, 0, cx - 2), (own_r_ref, 1, cx - 1)):
            k = 2 * a + j
            s = strip(ref[k * pairs : (k + 1) * pairs, :], cy)
            for r in (1, 2):
                s = jnp.where(lane == OFF - 3 + r, turn(up_ref[3 * a + r], OFF - 3 + r - at, 1), s)
            for r in (0, 1):
                s = jnp.where(lane == OFF + cy + r, turn(down_ref[3 * a + r], OFF + cy + r - at, 1), s)
            own.append(s)
        return out[:2] + own[:2], own[2:] + out[2:]

    def strip_first(v, m, vl, ml, vr, mr):
        above = jnp.where(plane == planes - 1, 0.0, turn(m, -1, 0))
        fz = face_mob(m, above)
        gz = fz * (turn(v, -1, 0) - v)
        fy = face_mob(m, turn(m, -1, 1))
        gy = fy * (turn(v, -1, 1) - v)
        lap = gz - jnp.where(plane == 0, 0.0, turn(gz, 1, 0)) + gy - turn(gy, 1, 1)
        lap = lap + face_mob(m, mr) * (vr - v) + face_mob(m, ml) * (vl - v)
        return v + step_size * lap

    turned_ref[...] = jnp.zeros(turned_ref.shape, F32)
    for side, (v, m) in enumerate(zip(strips(0), strips(1), strict=True)):
        f = face_mob(m[1], m[2])
        a = strip_first(v[1], m[1], v[0], m[0], v[2], m[2])
        b = strip_first(v[2], m[2], v[1], m[1], v[3], m[3])
        turned_ref[pl.ds(2 - side, planes, stride=2), :] = f * (v[2] - v[1])
        turned_ref[pl.ds(66 - side, planes, stride=2), :] = f * (b - a)
        side_ref[...] = f
        even = turn(side_ref[pl.ds(0, pairs, stride=2), :], -OFF, 1)
        odd = turn(side_ref[pl.ds(1, pairs, stride=2), :], cy - OFF, 1)
        edge_ref[side * pairs : (side + 1) * pairs, :] = jnp.where(lane[:pairs] < cy, even, odd)
    across = turned_ref[...].T

    def ends(k, z):
        return turn(across[:tall], -(64 * k + 2 * z + 2), 1)

    blank = jnp.zeros((OFF, cx), F32)
    for ref in (v_ref, c_ref, f_ref):
        for z in (0, planes + 1):
            ref[z * tall : (z + 1) * tall, :] = jnp.zeros((tall, cx), F32)
    for ref, a, field in ((v_ref, 0, p_ref), (c_ref, 1, m_ref)):
        for z in range(planes):
            base = (z + 1) * tall
            ref[base : base + OFF, :] = blank
            ref[base + OFF : base + OFF + cy, :] = field[z]
            ref[base + OFF + cy : base + tall, :] = blank
        for r in range(3):
            ref[pl.ds(tall + OFF - 3 + r, planes, stride=tall), :] = up_ref[3 * a + r]
            ref[pl.ds(tall + OFF + cy + r, planes, stride=tall), :] = down_ref[3 * a + r]

    wide = places((tall, cx), 1)

    def step(v, above, fz, fy, fx, gz_before, end):
        gz = fz * (above - v)
        gy = fy * (turn(v, -1, 0) - v)
        gx = jnp.where(wide == 0, end, fx * (v - turn(v, 1, 1)))
        lap = gz - gz_before + gy - turn(gy, 1, 0)
        lap = lap + jnp.where(wide == cx - 1, end, turn(gx, -1, 1)) - gx
        return v + step_size * lap, gz

    fz_ref[:tall, :] = jnp.zeros((tall, cx), F32)
    fy_ref[:OFF, :] = jnp.zeros((OFF, cx), F32)
    before = jnp.zeros((tall, cx), F32)
    for z in range(planes):
        here, above = pl.ds((z + 1) * tall, tall), pl.ds((z + 2) * tall, tall)
        m = c_ref[here, :]
        fz = face_mob(m, c_ref[above, :])
        fy = face_mob(m, turn(m, -1, 0))
        fx = face_mob(m, turn(m, 1, 1))
        fz_ref[here, :] = fz
        fy_ref[pl.ds(OFF + z * tall, tall), :] = fy
        fx_ref[pl.ds(z * tall, tall), :] = fx
        out, before = step(v_ref[here, :], v_ref[above, :], fz, fy, fx, before, ends(0, z))
        f_ref[here, :] = out

    rim_ref[...] = jnp.zeros(rim_ref.shape, F32)
    quarter = planes // 4
    before = jnp.zeros((tall, cx), F32)
    copies = []
    for z in range(planes):
        here, above = pl.ds((z + 1) * tall, tall), pl.ds((z + 2) * tall, tall)
        fy, fx = fy_ref[pl.ds(OFF + z * tall, tall), :], fx_ref[pl.ds(z * tall, tall), :]
        out, before = step(f_ref[here, :], f_ref[above, :], fz_ref[here, :], fy, fx, before, ends(1, z))
        q, row = z // quarter, z % quarter
        quarter_ref[q, row * cy : (row + 1) * cy, :] = out[OFF : OFF + cy].astype(BF16)
        rim_ref[q, 2 * row : 2 * row + 1, :] = out[OFF - 1 : OFF]
        rim_ref[q, 2 * row + 1 : 2 * row + 2, :] = out[OFF + cy : OFF + cy + 1]
        if row == quarter - 1:
            quarter_ref[q, quarter * cy :, :] = rim_ref[q].astype(BF16)
            for x in range(4):
                to = send_hbm.at[(q // 2) * 8 + x * 2 + q % 2]
                copies.append(pltpu.make_async_copy(quarter_ref.at[q], to, sems.at[q, x]))
                copies[-1].start()
    for copy in copies:
        copy.wait()


def solve_x_kernel(block_ref, got_ref, x0_hbm, x1_hbm, x2_hbm, x3_hbm, out_ref, x0_ref, x1_ref, x2_ref, x3_ref, sems):
    own = block_ref[0]
    parts, lines, cx = got_ref.shape
    main = lines - 16
    moves = ((x0_hbm, x0_ref), (x1_hbm, x1_ref), (x2_hbm, x2_ref), (x3_hbm, x3_ref))
    copies = [pltpu.make_async_copy(src, dst, sems.at[i]) for i, (src, dst) in enumerate(moves)]
    for copy in copies:
        copy.start()
    a = jnp.concatenate([got_ref[s] for s in range(parts)], axis=1)
    for other, x_ref in enumerate((x0_ref, x1_ref, x2_ref, x3_ref)):
        copies[other].wait()
        block = own ^ other
        m = lax.dot_general(a, x_ref[:cx], NT, preferred_element_type=F32)
        out_ref[block, : main + 8] = m[: main + 8]
        e = lax.dot_general(x_ref[cx:], a[:main], NT, preferred_element_type=F32)
        out_ref[block, main + 8 : main + 12] = e[:4, :cx]
        out_ref[block, main + 12 :] = e[:4, cx:]


def implicit_kernel(back_ref, fz_ref, fy_ref, fx_ref, edge_ref, out_ref, c_ref, e_ref):
    planes, cy, cx = out_ref.shape
    tall = cy + 2 * OFF
    quarter, pairs = planes // 4, planes // 2
    main = quarter * cy

    def chemical(s):
        return s * s * s - s

    for z in (0, planes + 1):
        c_ref[z * tall : (z + 1) * tall, :] = jnp.zeros((tall, cx), F32)
    for q in range(4):
        e_ref[q * 8 : (q + 1) * 8, :] = chemical(back_ref[q, main + 8 : main + 16])
        rims = chemical(back_ref[q, main : main + 8])
        for at in range(quarter):
            base = (q * quarter + at + 1) * tall
            c_ref[base + OFF : base + OFF + cy, :] = chemical(back_ref[q, at * cy : (at + 1) * cy])
            c_ref[base + OFF - 1 : base + OFF, :] = rims[2 * at : 2 * at + 1]
            c_ref[base + OFF + cy : base + OFF + cy + 1, :] = rims[2 * at + 1 : 2 * at + 2]
    ends = [e_ref[pl.ds(j, pairs, stride=4), :] for j in range(4)]
    left = edge_ref[:pairs, :] * (ends[1] - ends[0])
    right = edge_ref[pairs:, :] * (ends[3] - ends[2])
    across = jnp.concatenate([left, right, jnp.zeros((cx - planes, cx), F32)], axis=0).T
    lane = places((cy, cx), 1)
    before = jnp.zeros((cy, cx), F32)
    for z in range(planes):
        base = (z + 1) * tall + OFF
        flat = z * tall + OFF
        c = c_ref[base : base + cy, :]
        gz = fz_ref[base : base + cy, :] * (c_ref[base + tall : base + tall + cy, :] - c)
        gy = fy_ref[flat + OFF : flat + OFF + cy, :] * (c_ref[base + 1 : base + 1 + cy, :] - c)
        gu = fy_ref[flat + OFF - 1 : flat + OFF - 1 + cy, :] * (c - c_ref[base - 1 : base - 1 + cy, :])
        rows = slice((z % 2) * cy, (z % 2 + 1) * cy)
        gl = jnp.broadcast_to(across[rows, z // 2 : z // 2 + 1], (cy, cx))
        gr = jnp.broadcast_to(across[rows, pairs + z // 2 : pairs + z // 2 + 1], (cy, cx))
        gx = jnp.where(lane == 0, gl, fx_ref[flat : flat + cy, :] * (c - turn(c, 1, 1)))
        lap = gz - before + gy - gu + jnp.where(lane == cx - 1, gr, turn(gx, -1, 1)) - gx
        s = back_ref[z // quarter, (z % quarter) * cy : (z % quarter + 1) * cy]
        out_ref[z] = (s + step_size * lap).astype(BF16)
        before = gz


def solve_y_near_kernel(side_ref, y_hbm, u_ref, sum_ref, y_ref, near_ref, sems):
    high = side_ref[0]
    half, _ = u_ref.shape
    halves = (high, 1 - high)
    columns = [y_hbm.at[:, pl.ds(pl.multiple_of(h * half, half), half)] for h in halves]
    copies = [pltpu.make_async_copy(c, ref, sems.at[i]) for i, (c, ref) in enumerate(zip(columns, (near_ref, y_ref), strict=True))]
    for copy in copies:
        copy.start()
    copies[0].wait()
    sum_ref[...] = jnp.dot(near_ref[...], u_ref[...], preferred_element_type=F32)
    copies[1].wait()


def solve_y_far_kernel(sum_ref, y_ref, u_ref, out_ref):
    total = sum_ref[...] + jnp.dot(y_ref[...], u_ref[...], preferred_element_type=F32)
    out_ref[...] = total.astype(BF16)


def pack_x(core, p, m, x_inverse, y_inverse):
    cx = p.shape[2]
    shape = (2 * p.shape[0] + 16, cx)
    cy, order = y_inverse.shape
    out = (kept(shape, F32),) * 2 + (kept(p.shape, F32),) * 2 + (away_kept((cy // 2, order), BF16),)
    few = pltpu.VMEM((16, order), BF16)
    scratch = (few, few, pltpu.VMEM((cy // 2, order), BF16), pltpu.SemaphoreType.DMA((5,)))
    return call(pack_x_kernel, out, (p, m, x_inverse, y_inverse), core, scratch, range(4), (4,))


def pack_rows(x_inverse, own_l, own_r, left, right):
    cx, order = x_inverse.shape
    shape = (cx + 16, order)
    scratch = (pltpu.VMEM((16, order), F32), pltpu.VMEM(shape, BF16), pltpu.SemaphoreType.DMA(()))
    args = (x_inverse, own_l, own_r, left, right)
    return call(pack_rows_kernel, (away_kept(shape, BF16),), args, scratch=scratch, far=(0,), far_out=(0,))[0]


def pack_y(p, m, left, right):
    out = (kept((7, p.shape[0], p.shape[2]), F32),) * 2
    return call(pack_y_kernel, out, (p, m, left, right))


def explicit(*args):
    planes, cy, cx = args[0].shape
    tall = cy + 2 * OFF
    lines = planes // 4 * cy + 16
    field = pltpu.VMEM(((planes + 2) * tall, cx), F32)
    out = (
        away_kept((16, lines, cx), BF16),
        kept(((planes + 1) * tall, cx), F32),
        kept((planes * tall + OFF, cx), F32),
        kept((planes * tall, cx), F32),
        kept((planes, cx), F32),
    )
    scratch = (field, field, field, pltpu.VMEM((planes, cx), F32))
    scratch += (pltpu.VMEM((4, 16, cx), F32), pltpu.VMEM((cx, cx), F32))
    scratch += (pltpu.VMEM((4, lines, cx), BF16), pltpu.SemaphoreType.DMA((4, 4)))
    return call(explicit_kernel, out, args, scratch=scratch, far_out=(0,))


def solve_x(block, got, x_blocks):
    _, lines, cx = got.shape
    blocks = pltpu.VMEM(x_blocks[0].shape, BF16)
    scratch = (blocks,) * 4 + (pltpu.SemaphoreType.DMA((4,)),)
    return call(solve_x_kernel, kept((4, lines, cx), F32), (got, *x_blocks), block, scratch, (1, 2, 3, 4))


def implicit(back, faces, planes, cy):
    cx = back.shape[2]
    tall = cy + 2 * OFF
    scratch = (pltpu.VMEM(((planes + 2) * tall, cx), F32), pltpu.VMEM((32, cx), F32))
    return call(implicit_kernel, kept((planes, cy, cx), BF16), (back, *faces), scratch=scratch)


def solve_y_near(side, y, u):
    half, cx = u.shape
    out = (kept((half, cx), F32), kept((half, half), BF16))
    scratch = (pltpu.VMEM((half, half), BF16), pltpu.SemaphoreType.DMA((2,)))
    return call(solve_y_near_kernel, out, (y, u), side, scratch, (0,))


def solve_y_far(*parts):
    return call(solve_y_far_kernel, kept(parts[-1].shape, BF16), parts)


def both_ways(to_before, to_after, axis):
    size = lax.axis_size(axis)
    up = [(i, i + 1) for i in range(size - 1)]
    return lax.ppermute(to_after, axis, up), lax.ppermute(to_before, axis, [(j, i) for i, j in up])


def local(phase_field, mobility, x_inverse, y_inverse):
    planes, cy, cx = phase_field.shape
    order = y_inverse.shape[1]
    half = order // 2
    core, low, high = lax.axis_index("c"), lax.axis_index("yl"), lax.axis_index("yh")
    swap = [(0, 1), (1, 0)]

    one = lambda v: v.reshape(1).astype(jnp.int32)

    own_l, own_r, phase_field, mobility, y_part = pack_x(one(core), phase_field, mobility, x_inverse, y_inverse)
    y_rows = lax.all_gather(y_part, ("z", "c"), axis=0, tiled=True)
    left, right = both_ways(own_l, own_r, GX)
    to_up, to_down = pack_y(phase_field, mobility, left, right)
    up, down = both_ways(to_down, to_up, GY)
    rows = pack_rows(x_inverse, own_l, own_r, left, right)
    rows_yl = lax.ppermute(rows, "yl", swap)
    x_blocks = (rows, lax.ppermute(rows, "c", swap), rows_yl, lax.ppermute(rows_yl, "c", swap))

    send, *faces = explicit(phase_field, mobility, own_l, own_r, left, right, up, down)
    got = lax.all_to_all(send, GX, 0, 0, tiled=True)
    back = solve_x(one(low * 2 + core), got, x_blocks)
    back = lax.all_to_all(back, ("yl", "c"), 0, 0, tiled=True)
    updated = implicit(back, faces, planes, cy)

    mine = lax.all_to_all(updated, "z", 0, 0, tiled=True).reshape(half, cx)
    y_rows, mine = lax.optimization_barrier((y_rows, mine))
    theirs = lax.ppermute(mine, "yh", swap)
    part, y_far = solve_y_near(one(high), y_rows, mine)
    out = solve_y_far(part, y_far, theirs).reshape(16, cy, cx)
    out = lax.all_to_all(out, "z", 0, 0, tiled=True)
    return out.astype(F32)


def solution(mesh):
    shape = (2, mesh.shape["gx"] // 4, 2, 2, mesh.shape["gy"] // 2)
    torus = Mesh(mesh.devices.reshape(shape), ("yl", "x", "c", "yh", "z"))
    in_specs = (P(None, GY, GX), P(None, GY, GX), P(GX, None), P(GY, None))
    return jax.shard_map(local, mesh=torus, in_specs=in_specs, out_specs=P(None, GY, GX), check_vma=False)
```
